32 devices in a mesh: seq: 16 (over z, x, core), heads: 2 (over y).
Axes of the slice: x: 2, y: 2, z: 4, core: 2. Of those that a mesh axis runs over, the one named last changes fastest.
Arguments:
- frames: float32 [16384, 768], P('seq'), may hold values from -6 to 6
- cotangent: float32 [16384, 768], P('seq'), may hold values from -6 to 6
- lengths: int32 [64], replicated, may hold values from 1 to 1536, 16384 in all
- kernel: float32 [768, 48, 128], P('heads', None, 'seq'), may hold values from -0.078125 to 0.078125
- kernel_moment: float32 [768, 48, 128], P('heads', None, 'seq'), may hold values from -224 to 224
- kernel_average: float32 [768, 48, 128], P('heads', None, 'seq'), may hold values from -0.078125 to 0.078125
- project: float32 [768, 3, 768], P('seq', None, 'heads'), may hold values from -0.21875 to 0.21875
- project_moment: float32 [768, 3, 768], P('seq', None, 'heads'), may hold values from -224 to 224
- project_average: float32 [768, 3, 768], P('seq', None, 'heads'), may hold values from -0.21875 to 0.21875
- combine: float32 [768, 768], P('heads', 'seq'), may hold values from -0.875 to 0.875
- combine_moment: float32 [768, 768], P('heads', 'seq'), may hold values from -224 to 224
- combine_average: float32 [768, 768], P('heads', 'seq'), may hold values from -0.875 to 0.875
- expand: float32 [768, 3072], P('seq', 'heads'), may hold values from -0.21875 to 0.21875
- expand_moment: float32 [768, 3072], P('seq', 'heads'), may hold values from -224 to 224
- expand_average: float32 [768, 3072], P('seq', 'heads'), may hold values from -0.21875 to 0.21875
- shrink: float32 [3072, 768], P('heads', 'seq'), may hold values from -0.109375 to 0.109375
- shrink_moment: float32 [3072, 768], P('heads', 'seq'), may hold values from -224 to 224
- shrink_average: float32 [3072, 768], P('heads', 'seq'), may hold values from -0.109375 to 0.109375
- unitbias: float32 [3072], P(('heads', 'seq')), may hold values from -3 to 3
- unitbias_moment: float32 [3072], P(('heads', 'seq')), may hold values from -224 to 224
- unitbias_average: float32 [3072], P(('heads', 'seq')), may hold values from -3 to 3
- chanbias: float32 [3, 768], P(None, ('heads', 'seq')), may hold values from -3 to 3
- chanbias_moment: float32 [3, 768], P(None, ('heads', 'seq')), may hold values from -224 to 224
- chanbias_average: float32 [3, 768], P(None, ('heads', 'seq')), may hold values from -3 to 3
- outbias: float32 [2, 768], P(None, 'seq'), may hold values from -3 to 3
- outbias_moment: float32 [2, 768], P(None, 'seq'), may hold values from -224 to 224
- outbias_average: float32 [2, 768], P(None, 'seq'), may hold values from -3 to 3
- normparams: float32 [3, 2, 768], P(None, None, 'seq'), may hold values from -1.2 to 1.3, as said below
- normparams_moment: float32 [3, 2, 768], P(None, None, 'seq'), may hold values from -224 to 224
- normparams_average: float32 [3, 2, 768], P(None, None, 'seq'), may hold values from -1.2 to 1.3, as said below
Outputs:
- layer_out: float32 [16384, 768], P('seq')
- frames_grad: float32 [16384, 768], P('seq')
- kernel_grad: float32 [768, 48, 128], P('heads', None, 'seq')
- kernel_next: float32 [768, 48, 128], P('heads', None, 'seq')
- kernel_newmoment: float32 [768, 48, 128], P('heads', None, 'seq')
- kernel_newaverage: float32 [768, 48, 128], P('heads', None, 'seq')
- kernel_bfloat: bfloat16 [768, 48, 128], P('heads', None, 'seq')
- project_grad: float32 [768, 3, 768], P('seq', None, 'heads')
- project_next: float32 [768, 3, 768], P('seq', None, 'heads')
- project_newmoment: float32 [768, 3, 768], P('seq', None, 'heads')
- project_newaverage: float32 [768, 3, 768], P('seq', None, 'heads')
- project_bfloat: bfloat16 [768, 3, 768], P('seq', None, 'heads')
- combine_grad: float32 [768, 768], P('heads', 'seq')
- combine_next: float32 [768, 768], P('heads', 'seq')
- combine_newmoment: float32 [768, 768], P('heads', 'seq')
- combine_newaverage: float32 [768, 768], P('heads', 'seq')
- combine_bfloat: bfloat16 [768, 768], P('heads', 'seq')
- expand_grad: float32 [768, 3072], P('seq', 'heads')
- expand_next: float32 [768, 3072], P('seq', 'heads')
- expand_newmoment: float32 [768, 3072], P('seq', 'heads')
- expand_newaverage: float32 [768, 3072], P('seq', 'heads')
- expand_bfloat: bfloat16 [768, 3072], P('seq', 'heads')
- shrink_grad: float32 [3072, 768], P('heads', 'seq')
- shrink_next: float32 [3072, 768], P('heads', 'seq')
- shrink_newmoment: float32 [3072, 768], P('heads', 'seq')
- shrink_newaverage: float32 [3072, 768], P('heads', 'seq')
- shrink_bfloat: bfloat16 [3072, 768], P('heads', 'seq')
- unitbias_grad: float32 [3072], P(('heads', 'seq'))
- unitbias_next: float32 [3072], P(('heads', 'seq'))
- unitbias_newmoment: float32 [3072], P(('heads', 'seq'))
- unitbias_newaverage: float32 [3072], P(('heads', 'seq'))
- unitbias_bfloat: bfloat16 [3072], P(('heads', 'seq'))
- chanbias_grad: float32 [3, 768], P(None, ('heads', 'seq'))
- chanbias_next: float32 [3, 768], P(None, ('heads', 'seq'))
- chanbias_newmoment: float32 [3, 768], P(None, ('heads', 'seq'))
- chanbias_newaverage: float32 [3, 768], P(None, ('heads', 'seq'))
- chanbias_bfloat: bfloat16 [3, 768], P(None, ('heads', 'seq'))
- outbias_grad: float32 [2, 768], P(None, 'seq')
- outbias_next: float32 [2, 768], P(None, 'seq')
- outbias_newmoment: float32 [2, 768], P(None, 'seq')
- outbias_newaverage: float32 [2, 768], P(None, 'seq')
- outbias_bfloat: bfloat16 [2, 768], P(None, 'seq')
- normparams_grad: float32 [3, 2, 768], P(None, None, 'seq')
- normparams_next: float32 [3, 2, 768], P(None, None, 'seq')
- normparams_newmoment: float32 [3, 2, 768], P(None, None, 'seq')
- normparams_newaverage: float32 [3, 2, 768], P(None, None, 'seq')
- normparams_bfloat: bfloat16 [3, 2, 768], P(None, None, 'seq')
The draws below stay inside these ranges and needn't reach their ends.
Inputs may be any that keep to these rules, and one draw needn't show every extreme that they name: lengths sum to 16384; the longest is exactly 1536. `normparams`: entry [n, 0] holds norm n's gains, entry [n, 1] its shifts. `normparams_average`: entry [n, 0] holds gains, entry [n, 1] shifts.
All inputs are finite; a program needn't handle non-finite values.
Results may differ from the reference program's by a relative error of at most 0.015.
Values may be sent and summed in bfloat16 or wider, within the bound.
No kernel may reach another device: no remote copies, remote signals or barrier semaphores. Data moves between devices by JAX's collectives and lax.ppermute only.
A program may use at most 512 MiB of HBM per device.

```python
import math
import jax
import jax.numpy as jnp
import numpy as np
from jax import lax

D = 768
HEADS = 12
HEAD = 64
FF = 3072
K = 128
GROUPS = 16
TOK_DEV = 1024
CG = 48
MAXLEN = 1536
TOKENS = 16384
UTTS = 64


def norm_table(key):
    gain_key, shift_key = jax.random.split(key)
    gains = jax.random.uniform(gain_key, (3, 1, D), jnp.float32, 0.7, 1.3)
    shifts = 0.3 * jax.random.truncated_normal(shift_key, -4.0, 4.0, (3, 1, D), jnp.float32)
    return jnp.concatenate([gains, shifts], axis=1)


def draw_normparams(key, part):
    return norm_table(jax.random.fold_in(key, 11))


def draw_normparams_average(key, part):
    return norm_table(jax.random.fold_in(key, 29))


def levels(stream_key, dims, cuts, smallest, high):
    loudness, own = 1.0, jax.random.fold_in(stream_key, 6)
    for position, shards_of in cuts:
        heights = jnp.exp(jax.random.uniform(jax.random.fold_in(own, position), (shards_of,), jnp.float32, smallest / len(cuts), high / len(cuts)))
        loudness = loudness * jnp.repeat(heights, dims[position] // shards_of).reshape([-1 if axis == position else 1 for axis in range(len(dims))])
    return loudness


def length_profile(amount, total, bound, skew):
    loads = [(1 << 20) // math.isqrt(grade ** skew) + 1 for grade in range(2, amount + 1)]
    spare, given = total - bound - (amount - 1), [1] * (amount - 1)
    while spare > 0:
        free = [i for i in range(amount - 1) if given[i] < bound]
        mass, budget = sum([loads[i] for i in free]), spare
        for i in free:
            more = min(bound - given[i], max(1, budget * loads[i] // mass), spare)
            given[i] = given[i] + more
            spare = spare - more
    return np.array([bound] + given)


def uneven(key, number_of, total, limit, lean):
    if number_of == 2:
        one = jax.random.randint(key, (), max(1, total - limit), min(limit, total - 1) + 1)
        return jnp.stack([one, total - one])
    tallies = jnp.asarray(length_profile(number_of, total, limit, lean), jnp.int32)
    pairs = (number_of - 1) // 2
    giver, receiver = tallies[1:1 + 2 * pairs:2], tallies[2:2 + 2 * pairs:2]
    room = jnp.minimum(giver - 1, limit - receiver)
    moved = jax.random.randint(jax.random.fold_in(key, 1), (pairs,), 0, 1 << 20) % (room + 1)
    tallies = tallies.at[1:1 + 2 * pairs:2].set(giver - moved).at[2:2 + 2 * pairs:2].set(receiver + moved)
    return tallies[jax.random.permutation(jax.random.fold_in(key, 2), number_of)]


def centred(stream_key, shape, width, bound, shards=(), held_as=jnp.bfloat16):
    result = width * jax.random.normal(stream_key, shape, jnp.float32)
    if shards:
        result = result * levels(stream_key, shape, shards, -0.22, 0.18)
    return jnp.clip(result, -bound, bound).astype(held_as)


def setup_inputs(seed: int = 0) -> dict:
    key_list = jax.random.split(jax.random.key(seed), 31)
    frames = centred(key_list[0], (TOKENS, D), 1.0, 6.0, ((0, 16),), jnp.float32)
    cotangent = centred(key_list[1], (TOKENS, D), 1.0, 6.0, ((0, 16),), jnp.float32)
    lengths = uneven(key_list[2], UTTS, TOKENS, MAXLEN, 2).astype(jnp.int32)
    kernel = centred(key_list[3], (D, CG, K), (CG * K) ** -0.5, 0.078125, ((0, 2), (2, 16)), jnp.float32)
    kernel_moment = centred(key_list[4], (D, CG, K), (0.3 * TOKENS ** 0.5), 224.0, ((0, 2), (2, 16)), jnp.float32)
    kernel_average = centred(key_list[5], (D, CG, K), (CG * K) ** -0.5, 0.078125, ((0, 2), (2, 16)), jnp.float32)
    project = centred(key_list[6], (D, 3, D), D ** -0.5, 0.21875, ((0, 16), (2, 2)), jnp.float32)
    project_moment = centred(key_list[7], (D, 3, D), (0.3 * TOKENS ** 0.5), 224.0, ((0, 16), (2, 2)), jnp.float32)
    project_average = centred(key_list[8], (D, 3, D), D ** -0.5, 0.21875, ((0, 16), (2, 2)), jnp.float32)
    combine = centred(key_list[9], (D, D), (D // 16) ** -0.5, 0.875, ((0, 2), (1, 16)), jnp.float32)
    combine_moment = centred(key_list[10], (D, D), (0.3 * TOKENS ** 0.5), 224.0, ((0, 2), (1, 16)), jnp.float32)
    combine_average = centred(key_list[11], (D, D), (D // 16) ** -0.5, 0.875, ((0, 2), (1, 16)), jnp.float32)
    expand = centred(key_list[12], (D, FF), D ** -0.5, 0.21875, ((0, 16), (1, 2)), jnp.float32)
    expand_moment = centred(key_list[13], (D, FF), (0.3 * TOKENS ** 0.5), 224.0, ((0, 16), (1, 2)), jnp.float32)
    expand_average = centred(key_list[14], (D, FF), D ** -0.5, 0.21875, ((0, 16), (1, 2)), jnp.float32)
    shrink = centred(key_list[15], (FF, D), FF ** -0.5, 0.109375, ((0, 2), (1, 16)), jnp.float32)
    shrink_moment = centred(key_list[16], (FF, D), (0.3 * TOKENS ** 0.5), 224.0, ((0, 2), (1, 16)), jnp.float32)
    shrink_average = centred(key_list[17], (FF, D), FF ** -0.5, 0.109375, ((0, 2), (1, 16)), jnp.float32)
    unitbias = centred(key_list[18], (FF,), 0.5, 3.0, ((0, 32),), jnp.float32)
    unitbias_moment = centred(key_list[19], (FF,), (0.3 * TOKENS ** 0.5), 224.0, ((0, 32),), jnp.float32)
    unitbias_average = centred(key_list[20], (FF,), 0.5, 3.0, ((0, 32),), jnp.float32)
    chanbias = centred(key_list[21], (3, D), 0.5, 3.0, ((1, 32),), jnp.float32)
    chanbias_moment = centred(key_list[22], (3, D), (0.3 * TOKENS ** 0.5), 224.0, ((1, 32),), jnp.float32)
    chanbias_average = centred(key_list[23], (3, D), 0.5, 3.0, ((1, 32),), jnp.float32)
    outbias = centred(key_list[24], (2, D), 0.5, 3.0, ((1, 16),), jnp.float32)
    outbias_moment = centred(key_list[25], (2, D), (0.3 * TOKENS ** 0.5), 224.0, ((1, 16),), jnp.float32)
    outbias_average = centred(key_list[26], (2, D), 0.5, 3.0, ((1, 16),), jnp.float32)
    normparams = draw_normparams(jax.random.fold_in(key_list[30], 71), 0)
    normparams_moment = centred(key_list[28], (3, 2, D), (0.3 * TOKENS ** 0.5), 224.0, ((2, 16),), jnp.float32)
    normparams_average = draw_normparams_average(jax.random.fold_in(key_list[30], 71), 0)
    return dict(frames=frames, cotangent=cotangent, lengths=lengths, kernel=kernel, kernel_moment=kernel_moment, kernel_average=kernel_average, project=project, project_moment=project_moment, project_average=project_average, combine=combine, combine_moment=combine_moment, combine_average=combine_average, expand=expand, expand_moment=expand_moment, expand_average=expand_average, shrink=shrink, shrink_moment=shrink_moment, shrink_average=shrink_average, unitbias=unitbias, unitbias_moment=unitbias_moment, unitbias_average=unitbias_average, chanbias=chanbias, chanbias_moment=chanbias_moment, chanbias_average=chanbias_average, outbias=outbias, outbias_moment=outbias_moment, outbias_average=outbias_average, normparams=normparams, normparams_moment=normparams_moment, normparams_average=normparams_average)


@jax.custom_vjp
def low(v):
    return lax.optimization_barrier(v.astype(jnp.bfloat16)).astype(jnp.float32)

@jax.custom_vjp
def low_back(v):
    return v

def low_keep(v):
    return (low(v), None)

def low_pass(kept, grad):
    return (grad,)

def back_keep(v):
    return (v, None)

def back_low(kept, grad):
    return (low(grad),)
low.defvjp(low_keep, low_pass)
low_back.defvjp(back_keep, back_low)
EPSILON = 1e-05
NEGATIVE = -1e+30
tap_group = 16

def layer_norm(values, gain, shift):
    centered = values - lax.optimization_barrier(jnp.mean(values, axis=-1, keepdims=True))
    scale = lax.rsqrt(lax.optimization_barrier(jnp.mean(centered * centered, axis=-1, keepdims=True)) + EPSILON)
    return centered * scale * gain + shift

def gelu_exact(values):
    return jax.nn.gelu(values, approximate=False)

def segment_of(positions, ends, total):
    counted = lax.optimization_barrier(jnp.sum((ends[None, :] <= positions[:, None]).astype(jnp.int32), axis=1))
    before = (positions < 0).astype(jnp.int32)
    inside = (positions >= 0) & (positions < total)
    return jnp.where(inside, counted, -1 - before)

def tap_window(padded, pad_seg, row_seg, start, count, rows, groups, ingroup):
    pieces = jnp.stack([padded[start + j:start + j + rows] for j in range(count)])
    valid = jnp.stack([pad_seg[start + j:start + j + rows] == row_seg for j in range(count)])
    window = jnp.where(valid[:, :, None], pieces, jnp.zeros((), padded.dtype))
    return window.reshape(count, rows, groups, ingroup)

def nesterov(weight, grad, moment, average, rate):
    moment_new = 0.5 * moment + grad
    weight_new = weight - rate * (grad + 0.5 * moment_new)
    average_new = 0.5 * average + 0.5 * weight_new
    return (grad, weight_new, moment_new, average_new, weight_new.astype(jnp.bfloat16))

def reference(frames, cotangent, lengths, kernel, kernel_moment, kernel_average, project, project_moment, project_average, combine, combine_moment, combine_average, expand, expand_moment, expand_average, shrink, shrink_moment, shrink_average, unitbias, unitbias_moment, unitbias_average, chanbias, chanbias_moment, chanbias_average, outbias, outbias_moment, outbias_average, normparams, normparams_moment, normparams_average):
    ends = jnp.cumsum(lengths).astype(jnp.int32)
    blocks = TOKENS // TOK_DEV
    half_taps = K // 2
    seg_rows = segment_of(jnp.arange(TOKENS, dtype=jnp.int32), ends, TOKENS)
    seg_conv = segment_of(jnp.arange(-half_taps, TOKENS + half_taps, dtype=jnp.int32), ends, TOKENS)
    seg_keys = segment_of(jnp.arange(-2 * TOK_DEV, TOKENS + 2 * TOK_DEV, dtype=jnp.int32), ends, TOKENS)
    indices = jnp.arange(blocks, dtype=jnp.int32)
    highest = lax.Precision.HIGHEST

    def forward(x, w_kernel, w_project, w_combine, w_expand, w_shrink, b_unit, b_chan, b_out, w_norm):
        xr = low(x)
        padded = jnp.pad(xr, ((half_taps, half_taps), (0, 0)))
        kernel4 = w_kernel.reshape(GROUPS, CG, CG, K)

        def conv_rows(index):
            start = (index * TOK_DEV).astype(jnp.int32)
            window = lax.dynamic_slice_in_dim(padded, start, TOK_DEV + K, 0)
            seg_win = lax.dynamic_slice_in_dim(seg_conv, start, TOK_DEV + K, 0)
            seg_row = lax.dynamic_slice_in_dim(seg_rows, start, TOK_DEV, 0)
            summed = jnp.zeros((TOK_DEV, GROUPS, CG), jnp.float32)
            for first_tap in range(0, K, tap_group):
                taps = tap_window(window, seg_win, seg_row, first_tap, tap_group, TOK_DEV, GROUPS, CG)
                summed = summed + jnp.einsum('jtgi,goij->tgo', taps, kernel4[..., first_tap:first_tap + tap_group], precision=highest)
            return summed.reshape(TOK_DEV, D)
        conv = lax.map(jax.checkpoint(conv_rows), indices).reshape(TOKENS, D)
        pre = low_back(conv) + b_chan[0]
        spread = low(gelu_exact(pre))
        h1 = layer_norm(x + spread, w_norm[0, 0], w_norm[0, 1])
        h1r = low(h1)
        proj = jnp.dot(h1r, w_project.reshape(D, 3 * D), precision=highest).reshape(TOKENS, 3, D)
        queries = low_back(low((proj[:, 0] + b_chan[1]) * HEAD ** (-0.5))).reshape(TOKENS, HEADS, HEAD)
        keys = low_back(low(proj[:, 1])).reshape(TOKENS, HEADS, HEAD)
        values = low_back(low(proj[:, 2] + b_chan[2])).reshape(TOKENS, HEADS, HEAD)
        pad_keys = jnp.pad(keys, ((2 * TOK_DEV, 2 * TOK_DEV), (0, 0), (0, 0)))
        pad_values = jnp.pad(values, ((2 * TOK_DEV, 2 * TOK_DEV), (0, 0), (0, 0)))

        def attend_rows(index):
            start = (index * TOK_DEV).astype(jnp.int32)
            q_rows = lax.dynamic_slice_in_dim(queries, start, TOK_DEV, 0)
            k_rows = lax.dynamic_slice_in_dim(pad_keys, start, 5 * TOK_DEV, 0)
            v_rows = lax.dynamic_slice_in_dim(pad_values, start, 5 * TOK_DEV, 0)
            seg_q = lax.dynamic_slice_in_dim(seg_rows, start, TOK_DEV, 0)
            seg_k = lax.dynamic_slice_in_dim(seg_keys, start, 5 * TOK_DEV, 0)
            raw = low_back(jnp.einsum('thd,khd->htk', q_rows, k_rows, precision=highest))
            raw = jnp.where((seg_q[:, None] == seg_k[None, :])[None], raw, NEGATIVE)
            weights = low(jax.nn.softmax(raw, axis=-1))
            return jnp.einsum('htk,khd->thd', weights, v_rows, precision=highest).reshape(TOK_DEV, D)
        mixed = lax.map(jax.checkpoint(attend_rows), indices).reshape(TOKENS, D)
        attended = low_back(low(mixed))
        branch = low_back(jnp.dot(attended, w_combine, precision=highest)) + b_out[0]
        h2 = layer_norm(h1 + branch, w_norm[1, 0], w_norm[1, 1])
        h2r = low(h2)
        inner = low_back(jnp.dot(h2r, w_expand, precision=highest)) + b_unit
        hidden = low(gelu_exact(inner))
        outer = low_back(jnp.dot(hidden, w_shrink, precision=highest)) + b_out[1]
        return layer_norm(h2 + outer, w_norm[2, 0], w_norm[2, 1])

    def rounded(weight):
        return weight.astype(jnp.bfloat16).astype(jnp.float32)
    layer_out, pullback = jax.vjp(forward, frames, rounded(kernel), rounded(project), rounded(combine), rounded(expand), rounded(shrink), rounded(unitbias), rounded(chanbias), rounded(outbias), rounded(normparams))
    grads = pullback(cotangent)
    root = TOKENS ** 0.5
    small_rate = 0.1 / root
    unit_rate = 0.5 / root
    kernel_out = nesterov(kernel, grads[1], kernel_moment, kernel_average, (CG * K) ** (-0.5) / root)
    project_out = nesterov(project, grads[2], project_moment, project_average, D ** (-0.5) / root)
    combine_out = nesterov(combine, grads[3], combine_moment, combine_average, (D // 16) ** (-0.5) / root)
    expand_out = nesterov(expand, grads[4], expand_moment, expand_average, D ** (-0.5) / root)
    shrink_out = nesterov(shrink, grads[5], shrink_moment, shrink_average, FF ** (-0.5) / root)
    unit_out = nesterov(unitbias, grads[6], unitbias_moment, unitbias_average, unit_rate)
    chan_out = nesterov(chanbias, grads[7], chanbias_moment, chanbias_average, small_rate)
    outb_out = nesterov(outbias, grads[8], outbias_moment, outbias_average, small_rate)
    norm_out = nesterov(normparams, grads[9], normparams_moment, normparams_average, small_rate)
    return (layer_out, grads[0], kernel_out[0], kernel_out[1], kernel_out[2], kernel_out[3], kernel_out[4], project_out[0], project_out[1], project_out[2], project_out[3], project_out[4], combine_out[0], combine_out[1], combine_out[2], combine_out[3], combine_out[4], expand_out[0], expand_out[1], expand_out[2], expand_out[3], expand_out[4], shrink_out[0], shrink_out[1], shrink_out[2], shrink_out[3], shrink_out[4], unit_out[0], unit_out[1], unit_out[2], unit_out[3], unit_out[4], chan_out[0], chan_out[1], chan_out[2], chan_out[3], chan_out[4], outb_out[0], outb_out[1], outb_out[2], outb_out[3], outb_out[4], norm_out[0], norm_out[1], norm_out[2], norm_out[3], norm_out[4])
```

```python
import functools

import jax
import jax.numpy as jnp
from jax import lax
from jax.experimental import pallas as pl
from jax.experimental.pallas import tpu as pltpu
from jax.sharding import PartitionSpec as P

HEAD = 64
EPSILON = 1e-05

bf16, f32, i32 = jnp.bfloat16, jnp.float32, jnp.int32
CG, TAPS, GROUPS, HALO = 48, 128, 8, 64
ROWS, WIN, HALF = 1024, 1152, 384
CM, XM = 272, 304
NQ = 33
LCAP = 1408
PJ = 134
VLIM = 58 << 20


def iota(shape, dim):
    return lax.broadcasted_iota(i32, shape, dim)


def block_plan(starts, ends, first):
    w0 = first - HALO
    b = jnp.clip(starts - w0, 0, WIN)
    e = jnp.clip(ends - w0, 0, WIN)
    nblk = (e - b + 3) // 4
    n = starts.shape[0]
    before = jnp.arange(n)[None, :] < jnp.arange(n)[:, None]
    bs = jnp.sum(jnp.where(before, nblk[None, :], 0), axis=1).astype(i32)
    bs = bs + (jnp.clip(-w0, 0, WIN) + 3) // 4
    w = jnp.arange(WIN, dtype=i32)
    inside = (b[None, :] <= w[:, None]) & (w[:, None] < e[None, :])
    p = jnp.sum(jnp.where(inside, 4 * bs - b + w[:, None] + 1, 0), axis=1).astype(i32) - 1
    m = jnp.arange(LCAP, dtype=i32)
    hit = (bs[None, :] <= m[:, None]) & (m[:, None] < (bs + nblk)[None, :])
    bseg = jnp.sum(jnp.where(hit, jnp.arange(1, n + 1, dtype=i32)[None, :], 0), axis=1).astype(i32) - 1
    chunks = jnp.maximum((p[HALO + ROWS - 1] // 4 - 16) // CM + 1, 1)
    return (
        jnp.reshape(chunks, (1,)).astype(i32),
        jnp.broadcast_to(p[None, :], (8, WIN)),
        jnp.broadcast_to(p[:, None], (WIN, 128)),
        jnp.broadcast_to(bseg[:, None], (LCAP, 128)),
    )


def select_pair(h, rows, base):
    lane = iota((rows, 256), 1)
    src = CG * (2 * h + (lane >> 7)) + (lane & 63) - base
    ok = ((lane & 63) < CG) & (iota((rows, 256), 0) == src)
    return jnp.where(ok, 1.0, 0.0).astype(bf16)


def build_selector(s_ref, prow, c, first, rows):
    for t in range(4):
        pos = 4 * (iota((rows, prow.shape[1]), 0) + (CM * c + first)) + t
        s_ref[t] = jnp.where(pos == prow, 1.0, 0.0).astype(bf16)


def build_blocks(s_ref, dup, rows):
    y = [
        jnp.dot(s_ref[t], dup, preferred_element_type=f32).astype(bf16) for t in range(4)
    ]
    low = iota((rows, 128), 1) < 64
    out = []
    for g in range(2):
        tiles = [v[:, 128 * g : 128 * g + 128] for v in y]
        out.append(
            jnp.concatenate(
                [jnp.where(low, tiles[0], tiles[1]), jnp.where(low, tiles[2], tiles[3])], axis=1
            )
        )
    return out


def build_taps(k_ref, sel, p_ref, base_tile):
    p_ref[...] = jnp.zeros_like(p_ref)
    step = 16
    for j0 in range(0, TAPS, step):
        part = k_ref[pl.ds(j0, step), :, pl.ds(pl.multiple_of(base_tile * 128, 128), 256)]
        d = jnp.dot(part.reshape(step * CG, 256), sel, preferred_element_type=f32)
        d = d.astype(bf16).reshape(step, CG, 256)
        for g in range(2):
            p_ref[g, pl.ds(j0 + 2, step), 0:CG, 0:64] = d[:, :, 128 * g : 128 * g + 64]
            p_ref[g, pl.ds(j0 + 3, step), 0:CG, 64:128] = d[:, :, 128 * g + 64 : 128 * g + 128]


def conv_kernel(
    back, chunks_ref, prow_ref, pcol_ref, bseg_ref, x_ref, k_ref, out_ref, s_ref, mask_ref, p_ref, xb_ref
):
    h = pl.program_id(0)
    base_tile = h // 2
    chunks = chunks_ref[0]

    @pl.when(h == 0)
    def _():
        out_ref[...] = jnp.zeros_like(out_ref)

    sel = select_pair(h, 256, 128 * base_tile)
    build_taps(k_ref, sel, p_ref, base_tile)
    lanes = pl.ds(pl.multiple_of(base_tile * 128, 128), 256)
    dup = jnp.dot(x_ref[:, lanes], sel, preferred_element_type=f32).astype(bf16)

    def chunk(c, carry):
        @pl.when((h == 0) | (chunks > 1))
        def _():
            build_selector(s_ref, prow_ref[0:1, :], c, 0, XM)
            seg = bseg_ref[pl.ds(pl.multiple_of(CM * c, 16), XM), :]
            for q in range(NQ):
                same = seg[q : q + CM] == seg[16 : 16 + CM]
                mask_ref[q] = jnp.where(same, 1.0, 0.0).astype(bf16)

        xb = build_blocks(s_ref, dup, XM)
        for g in range(2):
            xb_ref[g] = xb[g]
        pcol = pcol_ref[pl.ds(HALO, ROWS), :]
        local = (pcol >> 2) - (16 + CM * c)
        place = jnp.where(
            jnp.concatenate([local] * 3, axis=1)[:, :CM] == iota((ROWS, CM), 1), 1.0, 0.0
        ).astype(bf16)
        phase = pcol & 3
        hi = iota((ROWS, 128), 1) >> 6
        pick = jnp.concatenate([phase == hi, phase == hi + 2], axis=1)
        total = jnp.zeros((ROWS, 256), f32)
        for g in range(2):
            acc = jnp.zeros((CM, 256), f32)
            for q in range(NQ):
                m = mask_ref[q]
                xs = xb_ref[g, q : q + CM, :] * jnp.concatenate([m, m], axis=1)
                if back:
                    a, b = 130 - 4 * q, 128 - 4 * q
                else:
                    a, b = 4 * q + 2, 4 * q
                w = jnp.concatenate(
                    [
                        p_ref[g, a : a + 4].reshape(256, 128),
                        p_ref[g, b : b + 4].reshape(256, 128),
                    ],
                    axis=1,
                )
                dims = (((1,), (1 if back else 0,)), ((), ()))
                acc = acc + lax.dot_general(xs, w, dims, preferred_element_type=f32)
            y = jnp.dot(place, acc.astype(bf16), preferred_element_type=f32)
            y = jnp.where(pick, y, 0.0).astype(bf16)
            lane = iota((256, 256), 1)
            row = iota((256, 256), 0) & 63
            fold = (row < CG) & (lane == CG * (2 * h + g) - 128 * base_tile + row)
            total = total + jnp.dot(
                y, jnp.where(fold, 1.0, 0.0).astype(bf16), preferred_element_type=f32
            )
        out_ref[:, lanes] += total
        return carry

    lax.fori_loop(0, chunks, chunk, 0)


def smem():
    return pl.BlockSpec(memory_space=pltpu.SMEM)


def whole(shape):
    return pl.BlockSpec(shape, lambda h: (0,) * len(shape))


def conv(plan, window, taps, back):
    chunks, prow, pcol, bseg = plan
    return pl.pallas_call(
        functools.partial(conv_kernel, back),
        grid=(4,),
        out_shape=jax.ShapeDtypeStruct((ROWS, HALF), f32),
        in_specs=[
            smem(),
            whole((8, WIN)),
            whole((WIN, 128)),
            whole((LCAP, 128)),
            whole((WIN, HALF)),
            whole((TAPS, CG, HALF)),
        ],
        out_specs=whole((ROWS, HALF)),
        scratch_shapes=[
            pltpu.VMEM((4, XM, WIN), bf16),
            pltpu.VMEM((NQ, CM, 128), bf16),
            pltpu.VMEM((2, PJ, 64, 128), bf16),
            pltpu.VMEM((2, XM, 256), bf16),
        ],
        compiler_params=pltpu.CompilerParams(vmem_limit_bytes=VLIM),
        cost_estimate=pl.CostEstimate(flops=30_000_000_000, bytes_accessed=9_000_000, transcendentals=0),
        name="conv_back" if back else "conv_forward",
    )(chunks, prow, pcol, bseg, window, taps)


def tap_grad_kernel(
    chunks_ref, prow_ref, bseg_ref, x_ref, d_ref, out_ref, s_ref, sd_ref, mask_ref, xt_ref, dp_ref, acc_ref
):
    h = pl.program_id(0)
    base_tile = h // 2
    chunks = chunks_ref[0]

    @pl.when(h == 0)
    def _():
        out_ref[...] = jnp.zeros_like(out_ref)
        dp_ref[...] = jnp.zeros_like(dp_ref)

    acc_ref[...] = jnp.zeros_like(acc_ref)
    sel = select_pair(h, 256, 128 * base_tile)
    lanes = pl.ds(pl.multiple_of(base_tile * 128, 128), 256)
    xdup = jnp.dot(x_ref[:, lanes], sel, preferred_element_type=f32).astype(bf16)
    ddup = jnp.dot(d_ref[:, lanes], sel, preferred_element_type=f32).astype(bf16)

    def chunk(c, carry):
        @pl.when((h == 0) | (chunks > 1))
        def _():
            build_selector(s_ref, prow_ref[0:1, :], c, 0, XM)
            build_selector(sd_ref, prow_ref[0:1, HALO : HALO + ROWS], c, 16, CM)
            seg = bseg_ref[pl.ds(pl.multiple_of(CM * c, 16), XM), :]
            none = jnp.full((32, 128), -7, i32)
            own = jnp.concatenate([none, seg[16 : 16 + CM], none], axis=0)
            for q in range(NQ):
                same = seg == own[32 - q : 32 - q + XM]
                mask_ref[q] = jnp.where(same, 1.0, 0.0).astype(bf16)

        xb = build_blocks(s_ref, xdup, XM)
        db = build_blocks(sd_ref, ddup, CM)
        for g in range(2):
            xt_ref[g] = xb[g].T
            dp_ref[g, 32 : 32 + CM, :] = db[g]
        for g in range(2):
            for q in range(NQ):
                m = mask_ref[q]
                ds = dp_ref[g, 32 - q : 32 - q + XM, :] * jnp.concatenate([m, m], axis=1)
                part = jnp.dot(xt_ref[g], ds, preferred_element_type=f32)
                acc_ref[g, 4 * q + 2 : 4 * q + 6] += part[:, 0:128].reshape(4, 64, 128)
                acc_ref[g, 4 * q : 4 * q + 4] += part[:, 128:256].reshape(4, 64, 128)
        return carry

    lax.fori_loop(0, chunks, chunk, 0)
    low = iota((1, 1, 128), 2) < 64
    row = iota((128, 256), 0)
    lane = iota((128, 256), 1)
    src = CG * (2 * h + (row >> 6)) + (row & 63) - 128 * base_tile
    back = jnp.where(((row & 63) < CG) & (lane == src), 1.0, 0.0).astype(bf16)
    step = 16
    for j0 in range(0, TAPS, step):
        now = [acc_ref[g, j0 + 2 : j0 + 2 + step, 0:CG, :] for g in range(2)]
        nxt = [acc_ref[g, j0 + 3 : j0 + 3 + step, 0:CG, :] for g in range(2)]
        here = jnp.where(low, now[0], nxt[1]).reshape(step * CG, 128)
        far = jnp.where(low, now[1], nxt[0]).reshape(step * CG, 128)
        both = (here + pltpu.roll(far, 64, 1)).astype(bf16)
        o = jnp.dot(both, back, preferred_element_type=f32).astype(bf16).reshape(step, CG, 256)
        out_ref[j0 : j0 + step, :, lanes] += o


def tap_grad(plan, window, d_conv):
    chunks, prow, pcol, bseg = plan
    return pl.pallas_call(
        tap_grad_kernel,
        grid=(4,),
        out_shape=jax.ShapeDtypeStruct((TAPS, CG, HALF), bf16),
        in_specs=[
            smem(),
            whole((8, WIN)),
            whole((LCAP, 128)),
            whole((WIN, HALF)),
            whole((ROWS, HALF)),
        ],
        out_specs=whole((TAPS, CG, HALF)),
        scratch_shapes=[
            pltpu.VMEM((4, XM, WIN), bf16),
            pltpu.VMEM((4, CM, ROWS), bf16),
            pltpu.VMEM((NQ, XM, 128), bf16),
            pltpu.VMEM((2, 256, XM), bf16),
            pltpu.VMEM((2, 32 + CM + 32, 256), bf16),
            pltpu.VMEM((2, PJ, 64, 128), f32),
        ],
        compiler_params=pltpu.CompilerParams(vmem_limit_bytes=VLIM),
        cost_estimate=pl.CostEstimate(flops=40_000_000_000, bytes_accessed=9_000_000, transcendentals=0),
        name="tap_gradient",
    )(chunks, prow, bseg, window, d_conv)
REACH = 1536
SPAN = ROWS + 2 * REACH
QT, KT = 256, 256
NEG = -1e30


def segment_count(ends, positions):
    return jnp.sum((ends[None, :] <= positions[:, None]).astype(i32), axis=1).astype(i32)

def attention_plan(starts, ends, first):
    w = first - REACH + jnp.arange(SPAN, dtype=i32)
    kseg = segment_count(ends, w)
    kseg = jnp.where(w < 0, -1, kseg)
    qseg = kseg[REACH : REACH + ROWS]
    edge = qseg.reshape(ROWS // QT, QT)
    n = jnp.arange(starts.shape[0], dtype=i32)
    head = jnp.sum(jnp.where(n[None] == edge[:, :1], starts[None], 0), axis=1) - (first - REACH)
    tail = jnp.sum(jnp.where(n[None] == edge[:, -1:], ends[None], 0), axis=1) - (first - REACH)
    lo = jnp.clip(head // KT, 0, SPAN // KT - 1)
    hi = jnp.clip((tail + KT - 1) // KT, 1, SPAN // KT)
    return (
        jnp.stack([lo, hi]).astype(i32),
        jnp.broadcast_to(qseg[None], (8, ROWS)),
        jnp.broadcast_to(kseg[:, None], (SPAN, 128)),
    )

def split_heads(a):
    low = iota(a.shape, 1) < 64
    zero = jnp.zeros((), a.dtype)
    return jnp.where(low, a, zero), jnp.where(low, zero, a)

def forward_kernel(range_ref, qseg_ref, kseg_ref, q_ref, k_ref, v_ref, o_ref, lse_ref, vt_ref, m_ref, l_ref, acc_ref):
    qi = pl.program_id(1)

    @pl.when(qi == 0)
    def _():
        def flip(t, carry):
            at = pl.ds(pl.multiple_of(t * KT, KT), KT)
            vt_ref[:, at] = v_ref[at, :].T
            return carry
        lax.fori_loop(range_ref[0, 0], range_ref[1, ROWS // QT - 1], flip, 0)

    qs = split_heads(q_ref[...])
    m_ref[...] = jnp.full_like(m_ref, NEG)
    l_ref[...] = jnp.zeros_like(l_ref)
    acc_ref[...] = jnp.zeros_like(acc_ref)

    def tile(t, carry):
        at = pl.ds(pl.multiple_of(t * KT, KT), KT)
        ks = kseg_ref[at, :]
        same = jnp.concatenate([ks] * (QT // 128), axis=1) == qseg_ref[0:1, :]
        k = k_ref[at, :]
        for e in range(2):
            s = lax.dot_general(k, qs[e], (((1,), (1,)), ((), ())), preferred_element_type=f32)
            s = jnp.where(same, s, NEG)
            m = m_ref[e : e + 1, :]
            new = jnp.maximum(m, jnp.max(s, axis=0, keepdims=True))
            p = jnp.exp(s - new)
            alpha = jnp.exp(m - new)
            l_ref[e : e + 1, :] = l_ref[e : e + 1, :] * alpha + jnp.sum(p, axis=0, keepdims=True)
            vt = vt_ref[64 * e : 64 * e + 64, at]
            acc_ref[e] = acc_ref[e] * alpha + jnp.dot(vt, p.astype(bf16), preferred_element_type=f32)
            m_ref[e : e + 1, :] = new
        return carry

    lax.fori_loop(range_ref[0, qi], range_ref[1, qi], tile, 0)
    o = jnp.concatenate([acc_ref[e] / l_ref[e : e + 1, :] for e in range(2)], axis=0)
    o_ref[...] = o.T
    lse_ref[0] = m_ref[...] + jnp.log(l_ref[...])


def attend(plan, q, kv):
    ranges, qseg, kseg = plan
    return pl.pallas_call(
        forward_kernel,
        grid=(HALF // 128, ROWS // QT),
        out_shape=(
            jax.ShapeDtypeStruct((ROWS, HALF), f32),
            jax.ShapeDtypeStruct((HALF // 128, 8, ROWS), f32),
        ),
        in_specs=[
            pl.BlockSpec(memory_space=pltpu.SMEM),
            pl.BlockSpec((8, QT), lambda h, i: (0, i)),
            pl.BlockSpec((SPAN, 128), lambda h, i: (0, 0)),
            pl.BlockSpec((QT, 128), lambda h, i: (i, h)),
            pl.BlockSpec((SPAN, 128), lambda h, i: (0, h)),
            pl.BlockSpec((SPAN, 128), lambda h, i: (0, h + HALF // 128)),
        ],
        out_specs=(
            pl.BlockSpec((QT, 128), lambda h, i: (i, h)),
            pl.BlockSpec((1, 8, QT), lambda h, i: (h, 0, i)),
        ),
        scratch_shapes=[
            pltpu.VMEM((128, SPAN), bf16),
            pltpu.VMEM((8, QT), f32),
            pltpu.VMEM((8, QT), f32),
            pltpu.VMEM((2, 64, QT), f32),
        ],
        compiler_params=pltpu.CompilerParams(vmem_limit_bytes=VLIM),
        cost_estimate=pl.CostEstimate(flops=20_000_000_000, bytes_accessed=12_000_000, transcendentals=0),
        name="attention_forward",
    )(ranges, qseg, kseg, q, kv, kv)


def backward_kernel(range_ref, qseg_ref, kseg_ref, q_ref, k_ref, v_ref, do_ref, o_ref, lse_ref,
                    dq_ref, dk_far_ref, dv_far_ref, dk_own_ref, dv_own_ref, kt_ref, dk_ref, dv_ref, dqt_ref):
    qi = pl.program_id(1)
    last = ROWS // QT - 1

    @pl.when(qi == 0)
    def _():
        dk_ref[...] = jnp.zeros_like(dk_ref)
        dv_ref[...] = jnp.zeros_like(dv_ref)
        def flip(t, carry):
            at = pl.ds(pl.multiple_of(t * KT, KT), KT)
            kt_ref[:, at] = k_ref[at, :].T
            return carry
        lax.fori_loop(range_ref[0, 0], range_ref[1, last], flip, 0)

    qs = split_heads(q_ref[...])
    dos = split_heads(do_ref[...])
    qcat = jnp.concatenate(qs, axis=0)
    docat = jnp.concatenate(dos, axis=0)
    dm = (do_ref[...].astype(f32) * o_ref[...]).T
    delta = [jnp.sum(dm[64 * e : 64 * e + 64], axis=0, keepdims=True) for e in range(2)]
    dqt_ref[...] = jnp.zeros_like(dqt_ref)

    def tile(t, carry):
        at = pl.ds(pl.multiple_of(t * KT, KT), KT)
        ks = kseg_ref[at, :]
        same = jnp.concatenate([ks] * (QT // 128), axis=1) == qseg_ref[0:1, :]
        k = k_ref[at, :]
        v = v_ref[at, :]
        ps, dss = [], []
        for e in range(2):
            dims = (((1,), (1,)), ((), ()))
            s = lax.dot_general(k, qs[e], dims, preferred_element_type=f32)
            p = jnp.exp(jnp.where(same, s - lse_ref[0, e : e + 1, :], NEG))
            dp = lax.dot_general(v, dos[e], dims, preferred_element_type=f32)
            ds = (p * (dp - delta[e])).astype(bf16)
            dqt_ref[e] += jnp.dot(kt_ref[64 * e : 64 * e + 64, at], ds, preferred_element_type=f32)
            ps.append(p.astype(bf16))
            dss.append(ds)
        dk_ref[at, :] += jnp.dot(jnp.concatenate(dss, axis=1), qcat, preferred_element_type=f32)
        dv_ref[at, :] += jnp.dot(jnp.concatenate(ps, axis=1), docat, preferred_element_type=f32)
        return carry

    lax.fori_loop(range_ref[0, qi], range_ref[1, qi], tile, 0)
    dq = jnp.concatenate([dqt_ref[0], dqt_ref[1]], axis=0).T
    dq_ref[...] = dq.astype(bf16) * jnp.asarray(0.125, bf16)

    @pl.when(qi == last)
    def _():
        for far, own, acc in ((dk_far_ref, dk_own_ref, dk_ref), (dv_far_ref, dv_own_ref, dv_ref)):
            far[0:REACH, :] = acc[0:REACH, :].astype(bf16)
            far[REACH : 2 * REACH, :] = acc[REACH + ROWS : SPAN, :].astype(bf16)
            own[...] = acc[REACH : REACH + ROWS, :]


def attend_back(plan, q, kv, d_att, mixed, lse):
    ranges, qseg, kseg = plan
    rowspec = pl.BlockSpec((QT, 128), lambda h, i: (i, h))
    span = pl.BlockSpec((SPAN, 128), lambda h, i: (0, h))
    span_v = pl.BlockSpec((SPAN, 128), lambda h, i: (0, h + HALF // 128))
    far = pl.BlockSpec((2 * REACH, 128), lambda h, i: (0, h))
    own = pl.BlockSpec((ROWS, 128), lambda h, i: (0, h))
    dq, dk_far, dv_far, dk_own, dv_own = pl.pallas_call(
        backward_kernel,
        grid=(HALF // 128, ROWS // QT),
        out_shape=(
            jax.ShapeDtypeStruct((ROWS, HALF), bf16),
            jax.ShapeDtypeStruct((2 * REACH, HALF), bf16),
            jax.ShapeDtypeStruct((2 * REACH, HALF), bf16),
            jax.ShapeDtypeStruct((ROWS, HALF), f32),
            jax.ShapeDtypeStruct((ROWS, HALF), f32),
        ),
        in_specs=[
            pl.BlockSpec(memory_space=pltpu.SMEM),
            pl.BlockSpec((8, QT), lambda h, i: (0, i)),
            pl.BlockSpec((SPAN, 128), lambda h, i: (0, 0)),
            rowspec, span, span_v, rowspec, rowspec,
            pl.BlockSpec((1, 8, QT), lambda h, i: (h, 0, i)),
        ],
        out_specs=(rowspec, far, far, own, own),
        scratch_shapes=[
            pltpu.VMEM((128, SPAN), bf16),
            pltpu.VMEM((SPAN, 128), f32),
            pltpu.VMEM((SPAN, 128), f32),
            pltpu.VMEM((2, 64, QT), f32),
        ],
        compiler_params=pltpu.CompilerParams(vmem_limit_bytes=VLIM),
        cost_estimate=pl.CostEstimate(flops=50_000_000_000, bytes_accessed=25_000_000, transcendentals=0),
        name="attention_backward",
    )(ranges, qseg, kseg, q, kv, kv, d_att, mixed, lse)
    return dq, jnp.concatenate([dk_far, dv_far], axis=1), jnp.concatenate([dk_own, dv_own], axis=1)


def exchange(part):
    return lax.ppermute(part, "heads", [(0, 1), (1, 0)])


def pair_sum(part):
    half = part.astype(bf16)
    return half.astype(f32) + exchange(half).astype(f32)


def side_by_side(own, other, index):
    return jnp.where(
        index == 0,
        jnp.concatenate([own, other], axis=1),
        jnp.concatenate([other, own], axis=1),
    )


def passed(block, distance):
    count = lax.axis_size("seq")
    route = [(i - distance, i) for i in range(count) if 0 <= i - distance < count]
    return lax.ppermute(block, "seq", route)


def layer_norm(values, gain, shift):
    centered = values - jnp.mean(values, axis=-1, keepdims=True)
    scale = lax.rsqrt(jnp.mean(centered * centered, axis=-1, keepdims=True) + EPSILON)
    return centered * scale * gain + shift


def gelu_exact(values):
    return jax.nn.gelu(values, approximate=False)


def nesterov(weight, grad, moment, average, rate):
    moment_new = 0.5 * moment + grad
    weight_new = weight - rate * (grad + 0.5 * moment_new)
    average_new = 0.5 * average + 0.5 * weight_new
    return (grad, weight_new, moment_new, average_new, weight_new.astype(bf16))


def dot(a, b, ca, cb):
    return lax.dot_general(a, b, (((ca,), (cb,)), ((), ())), preferred_element_type=f32)


def gathered(shard):
    return lax.all_gather(shard, "seq", axis=0, tiled=True)


def scattered(whole_sum):
    return lax.psum_scatter(whole_sum, "seq", scatter_dimension=0, tiled=True)


def body(
    frames,
    cotangent,
    lengths,
    kernel,
    kernel_moment,
    kernel_average,
    project,
    project_moment,
    project_average,
    combine,
    combine_moment,
    combine_average,
    expand,
    expand_moment,
    expand_average,
    shrink,
    shrink_moment,
    shrink_average,
    unitbias,
    unitbias_moment,
    unitbias_average,
    chanbias,
    chanbias_moment,
    chanbias_average,
    outbias,
    outbias_moment,
    outbias_average,
    normparams,
    normparams_moment,
    normparams_average,
):
    devices = lax.axis_size("seq")
    rows, width = frames.shape
    total = devices * rows
    first = lax.axis_index("seq") * rows
    index = lax.axis_index("heads")
    local = project.shape[0]
    hidden_units = expand.shape[1]

    w_kernel = gathered(jnp.transpose(kernel, (2, 1, 0)).astype(bf16))
    small = jnp.concatenate(
        [unitbias, chanbias.reshape(-1), outbias.reshape(-1), normparams.reshape(-1)]
    ).astype(bf16)
    w_small = gathered(small[None])
    w_first = gathered(
        jnp.concatenate(
            [project[:, 0], project[:, 1], project[:, 2], combine.T], axis=1
        ).astype(bf16)
    )
    w_second = gathered(jnp.concatenate([expand, shrink.T], axis=1).astype(bf16))
    cuts = [unitbias.size, chanbias.size, outbias.size, normparams.size]
    parts, at = [], 0
    for size in cuts:
        parts.append(w_small[:, at : at + size].astype(f32))
        at += size
    b_unit = parts[0].reshape(-1)
    b_chan = jnp.transpose(parts[1].reshape(devices, 3, -1), (1, 0, 2)).reshape(3, -1)
    b_out = jnp.transpose(parts[2].reshape(devices, 2, -1), (1, 0, 2)).reshape(2, -1)
    norms = jnp.transpose(parts[3].reshape(devices, 3, 2, -1), (1, 2, 0, 3)).reshape(3, 2, -1)

    count = lengths.shape[0]
    order = jnp.arange(count, dtype=i32)
    ends = jnp.sum(jnp.where(order[None, :] <= order[:, None], lengths[None, :], 0), axis=1).astype(i32)
    starts = ends - lengths
    plan = block_plan(starts, ends, first)
    reach = attention_plan(starts, ends, first)

    x_half = lax.dynamic_slice_in_dim(frames, index * HALF, HALF, 1).astype(bf16)
    window = jnp.concatenate(
        [passed(x_half[rows - HALO :], 1), x_half, passed(x_half[:HALO], -1)], axis=0
    )
    pre = conv(plan, window, w_kernel, False) + b_chan[0]
    spread_part = gelu_exact(pre).astype(bf16)
    spread = side_by_side(spread_part, exchange(spread_part), index)
    h1, norm0_back = jax.vjp(layer_norm, frames + spread.astype(f32), norms[0, 0], norms[0, 1])
    h1_half = h1.astype(bf16)
    proj = dot(h1_half, w_first[:, : 3 * HALF], 1, 0)
    scale = HEAD ** (-0.5)
    queries = ((proj[:, :HALF] + b_chan[1]) * scale).astype(bf16)
    keys = proj[:, HALF : 2 * HALF].astype(bf16)
    values = (proj[:, 2 * HALF :] + b_chan[2]).astype(bf16)
    both = jnp.concatenate([keys, values], axis=1)
    near = REACH - rows
    span = jnp.concatenate(
        [
            passed(both[rows - near :], 2),
            passed(both, 1),
            both,
            passed(both, -1),
            passed(both[:near], -2),
        ],
        axis=0,
    )
    mixed, lse = attend(reach, queries, span)
    attended = mixed.astype(bf16)
    w_combine = w_first[:, 3 * HALF :]
    branch = pair_sum(dot(attended, w_combine, 1, 1))
    h2, norm1_back = jax.vjp(layer_norm, h1 + branch + b_out[0], norms[1, 0], norms[1, 1])
    h2_half = h2.astype(bf16)
    w_expand = w_second[:, :hidden_units]
    w_shrink = w_second[:, hidden_units:]
    inner = dot(h2_half, w_expand, 1, 0) + b_unit
    hidden, gelu_inner_back = jax.vjp(gelu_exact, inner)
    hidden_half = hidden.astype(bf16)
    outer = pair_sum(dot(hidden_half, w_shrink, 1, 1))
    layer_out, norm2_back = jax.vjp(layer_norm, h2 + outer + b_out[1], norms[2, 0], norms[2, 1])
    dx3, gain2_grad, shift2_grad = norm2_back(cotangent)
    outer_bias_grad = jnp.sum(dx3, axis=0)
    d_out = dx3.astype(bf16)
    d_hidden = dot(d_out, w_shrink, 1, 0)
    d_inner = gelu_inner_back(d_hidden)[0]
    unit_grad = jnp.sum(d_inner, axis=0)
    d_inner_half = d_inner.astype(bf16)
    dh2 = dx3 + pair_sum(dot(d_inner_half, w_expand, 1, 1))
    second_sum = scattered(
        jnp.concatenate(
            [dot(h2_half, d_inner_half, 0, 0).astype(bf16), dot(d_out, hidden_half, 0, 0).astype(bf16)],
            axis=1,
        )
    ).astype(f32)
    dx2, gain1_grad, shift1_grad = norm1_back(dh2)
    branch_bias_grad = jnp.sum(dx2, axis=0)
    d_branch = dx2.astype(bf16)
    d_att = dot(d_branch, w_combine, 1, 0).astype(bf16)
    dq_half, far, own = attend_back(reach, queries, span, d_att, mixed, lse)
    d_both = own
    for distance, lo, hi, to in (
        (2, 0, near, rows - near),
        (1, near, REACH, 0),
        (-1, REACH, REACH + rows, 0),
        (-2, REACH + rows, 2 * REACH, 0),
    ):
        back = passed(far[lo:hi], -distance).astype(f32)
        pad = (to, rows - to - back.shape[0])
        d_both = d_both + jnp.pad(back, (pad, (0, 0)))
    d_both_half = d_both.astype(bf16)
    stacked = jnp.concatenate([dq_half, d_both_half], axis=1)
    query_bias_grad = jnp.sum(dq_half.astype(f32), axis=0)
    value_bias_grad = jnp.sum(d_both_half[:, HALF:].astype(f32), axis=0)
    dh1 = dx2 + pair_sum(dot(stacked, w_first[:, : 3 * HALF], 1, 1))
    first_sum = scattered(
        jnp.concatenate(
            [dot(h1_half, stacked, 0, 0).astype(bf16), dot(d_branch, attended, 0, 0).astype(bf16)],
            axis=1,
        )
    ).astype(f32)
    dx1, gain0_grad, shift0_grad = norm0_back(dh1)
    d_spread = lax.dynamic_slice_in_dim(dx1, index * HALF, HALF, 1)
    d_conv = jax.vjp(gelu_exact, pre)[1](d_spread)[0]
    conv_bias_grad = jnp.sum(d_conv, axis=0)
    d_conv_half = d_conv.astype(bf16)
    kernel_sum = scattered(tap_grad(plan, window, d_conv_half)).astype(f32)
    d_window = jnp.concatenate(
        [passed(d_conv_half[rows - HALO :], 1), d_conv_half, passed(d_conv_half[:HALO], -1)], axis=0
    )
    d_input = conv(plan, d_window, w_kernel, True).astype(bf16)
    frames_grad = dx1 + side_by_side(d_input, exchange(d_input), index).astype(f32)

    spread_out = lambda grad, lead: jnp.transpose(
        grad.reshape(lead, devices, -1), (1, 0, 2)
    ).reshape(devices, -1)
    small_sum = scattered(
        jnp.concatenate(
            [
                unit_grad.reshape(devices, -1),
                spread_out(jnp.stack([conv_bias_grad, query_bias_grad, value_bias_grad]), 3),
                spread_out(jnp.stack([branch_bias_grad, outer_bias_grad]), 2),
                spread_out(
                    jnp.stack(
                        [gain0_grad, shift0_grad, gain1_grad, shift1_grad, gain2_grad, shift2_grad]
                    ),
                    6,
                ),
            ],
            axis=1,
        )
    )[0]
    pieces, at = [], 0
    for size in cuts:
        pieces.append(small_sum[at : at + size])
        at += size
    unit_sum = pieces[0]
    chan_sum = pieces[1].reshape(chanbias.shape)
    out_sum = pieces[2].reshape(outbias.shape)
    norm_sum = pieces[3].reshape(normparams.shape)
    project_sum = jnp.stack([first_sum[:, HALF * i : HALF * (i + 1)] for i in range(3)], axis=1)

    root = total**0.5
    small_rate = 0.1 / root
    out = [layer_out, frames_grad]
    for weight, grad, moment, average, rate in (
        (kernel, jnp.transpose(kernel_sum, (2, 1, 0)), kernel_moment, kernel_average, (CG * TAPS) ** (-0.5) / root),
        (project, project_sum, project_moment, project_average, width ** (-0.5) / root),
        (combine, first_sum[:, 3 * HALF :].T, combine_moment, combine_average, (width // 16) ** (-0.5) / root),
        (expand, second_sum[:, :hidden_units], expand_moment, expand_average, width ** (-0.5) / root),
        (shrink, second_sum[:, hidden_units:].T, shrink_moment, shrink_average, (2 * hidden_units) ** (-0.5) / root),
        (unitbias, unit_sum, unitbias_moment, unitbias_average, 0.5 / root),
        (chanbias, chan_sum, chanbias_moment, chanbias_average, small_rate),
        (outbias, out_sum, outbias_moment, outbias_average, small_rate),
        (normparams, norm_sum, normparams_moment, normparams_average, small_rate),
    ):
        out.extend(nesterov(weight, grad, moment, average, rate))
    return tuple(out)


def solution(mesh):
    kernel_spec = P("heads", None, "seq")
    project_spec = P("seq", None, "heads")
    tall = P("heads", "seq")
    wide = P("seq", "heads")
    unit = P(("heads", "seq"))
    chan = P(None, ("heads", "seq"))
    outb = P(None, "seq")
    norm = P(None, None, "seq")
    weights = (kernel_spec, project_spec, tall, wide, tall, unit, chan, outb, norm)
    rows = P("seq", None)
    return jax.shard_map(
        body,
        mesh=mesh,
        in_specs=(rows, rows, P()) + tuple(s for s in weights for _ in range(3)),
        out_specs=(rows, rows) + tuple(s for s in weights for _ in range(5)),
        check_vma=False,
    )
```

```python
import functools

import jax
import jax.numpy as jnp
from jax import lax
from jax.experimental import pallas as pl
from jax.experimental.pallas import tpu as pltpu
from jax.sharding import PartitionSpec as P

HEAD = 64
PAIRS = 3
EPSILON = 1e-05

bf16, f32, i32 = jnp.bfloat16, jnp.float32, jnp.int32
CG, TAPS, GROUPS, HALO = 48, 128, 8, 64
ROWS, WIN, HALF = 1024, 1152, 384
CM, XM = 272, 304
NQ = 33
LCAP = 1408
PJ = 134
EXTRA = 16
VLIM = 58 << 20


def iota(shape, dim):
    return lax.broadcasted_iota(i32, shape, dim)


def block_plan(starts, ends, first):
    w0 = first - HALO
    b = jnp.clip(starts - w0, 0, WIN)
    e = jnp.clip(ends - w0, 0, WIN)
    nblk = (e - b + 3) // 4
    n = starts.shape[0]
    before = jnp.arange(n)[None, :] < jnp.arange(n)[:, None]
    bs = jnp.sum(jnp.where(before, nblk[None, :], 0), axis=1).astype(i32)
    bs = bs + (jnp.clip(-w0, 0, WIN) + 3) // 4
    w = jnp.arange(WIN, dtype=i32)
    inside = (b[None, :] <= w[:, None]) & (w[:, None] < e[None, :])
    p = jnp.sum(jnp.where(inside, 4 * bs - b + w[:, None] + 1, 0), axis=1).astype(i32) - 1
    m = jnp.arange(LCAP, dtype=i32)
    hit = (bs[None, :] <= m[:, None]) & (m[:, None] < (bs + nblk)[None, :])
    bseg = jnp.sum(jnp.where(hit, jnp.arange(1, n + 1, dtype=i32)[None, :], 0), axis=1).astype(i32) - 1
    chunks = jnp.maximum((p[HALO + ROWS - 1] // 4 - 16) // CM + 1, 1)
    return (
        jnp.reshape(chunks, (1,)).astype(i32),
        jnp.broadcast_to(p[None, :], (8, WIN)),
        jnp.broadcast_to(p[:, None], (WIN, 128)),
        jnp.broadcast_to(bseg[:, None], (LCAP, 128)),
    )


def select_pair(h, rows, base):
    lane = iota((rows, 256), 1)
    src = CG * (2 * h + (lane >> 7)) + (lane & 63) - base
    ok = ((lane & 63) < CG) & (iota((rows, 256), 0) == src)
    return jnp.where(ok, 1.0, 0.0).astype(bf16)


def build_selector(s_ref, prow, c, first, rows):
    for t in range(4):
        pos = 4 * (iota((rows, prow.shape[1]), 0) + (CM * c + first)) + t
        s_ref[t] = jnp.where(pos == prow, 1.0, 0.0).astype(bf16)


def build_blocks(s_ref, dup, rows):
    y = [
        jnp.dot(s_ref[t], dup, preferred_element_type=f32).astype(bf16) for t in range(4)
    ]
    low = iota((rows, 128), 1) < 64
    out = []
    for g in range(2):
        tiles = [v[:, 128 * g : 128 * g + 128] for v in y]
        out.append(
            jnp.concatenate(
                [jnp.where(low, tiles[0], tiles[1]), jnp.where(low, tiles[2], tiles[3])], axis=1
            )
        )
    return out


def build_taps(k_ref, sel, p_ref, base_tile):
    p_ref[...] = jnp.zeros_like(p_ref)
    step = 16
    for j0 in range(0, TAPS, step):
        part = k_ref[pl.ds(j0, step), :, pl.ds(pl.multiple_of(base_tile * 128, 128), 256)]
        d = jnp.dot(part.reshape(step * CG, 256), sel, preferred_element_type=f32)
        d = d.astype(bf16).reshape(step, CG, 256)
        for g in range(2):
            p_ref[g, pl.ds(j0 + 2, step), 0:CG, 0:64] = d[:, :, 128 * g : 128 * g + 64]
            p_ref[g, pl.ds(j0 + 3, step), 0:CG, 64:128] = d[:, :, 128 * g + 64 : 128 * g + 128]


def conv_kernel(
    back, chunks_ref, prow_ref, pcol_ref, bseg_ref, x_ref, k_ref, out_ref, s_ref, mask_ref, p_ref, xb_ref
):
    h = pl.program_id(0)
    base_tile = h // 2
    chunks = chunks_ref[0]

    @pl.when(h == 0)
    def _():
        out_ref[...] = jnp.zeros_like(out_ref)

    sel = select_pair(h, 256, 128 * base_tile)
    build_taps(k_ref, sel, p_ref, base_tile)
    lanes = pl.ds(pl.multiple_of(base_tile * 128, 128), 256)
    dup = jnp.dot(x_ref[:, lanes], sel, preferred_element_type=f32).astype(bf16)

    def chunk(c, carry):
        @pl.when((h == 0) | (chunks > 1))
        def _():
            build_selector(s_ref, prow_ref[0:1, :], c, 0, XM)
            seg = bseg_ref[pl.ds(pl.multiple_of(CM * c, 16), XM), :]
            for q in range(NQ):
                same = seg[q : q + CM] == seg[16 : 16 + CM]
                mask_ref[q] = jnp.where(same, 1.0, 0.0).astype(bf16)

        xb = build_blocks(s_ref, dup, XM)
        for g in range(2):
            xb_ref[g] = xb[g]
        pcol = pcol_ref[pl.ds(HALO, ROWS), :]
        local = (pcol >> 2) - (16 + CM * c)
        place = jnp.where(
            jnp.concatenate([local] * 3, axis=1)[:, :CM] == iota((ROWS, CM), 1), 1.0, 0.0
        ).astype(bf16)
        phase = pcol & 3
        hi = iota((ROWS, 128), 1) >> 6
        pick = jnp.concatenate([phase == hi, phase == hi + 2], axis=1)
        total = jnp.zeros((ROWS, 256), f32)
        for g in range(2):
            acc = jnp.zeros((CM, 256), f32)
            for q in range(NQ):
                m = mask_ref[q]
                xs = xb_ref[g, q : q + CM, :] * jnp.concatenate([m, m], axis=1)
                if back:
                    a, b = 130 - 4 * q, 128 - 4 * q
                else:
                    a, b = 4 * q + 2, 4 * q
                w = jnp.concatenate(
                    [
                        p_ref[g, a : a + 4].reshape(256, 128),
                        p_ref[g, b : b + 4].reshape(256, 128),
                    ],
                    axis=1,
                )
                dims = (((1,), (1 if back else 0,)), ((), ()))
                acc = acc + lax.dot_general(xs, w, dims, preferred_element_type=f32)
            y = jnp.dot(place, acc.astype(bf16), preferred_element_type=f32)
            y = jnp.where(pick, y, 0.0).astype(bf16)
            lane = iota((256, 256), 1)
            row = iota((256, 256), 0) & 63
            fold = (row < CG) & (lane == CG * (2 * h + g) - 128 * base_tile + row)
            total = total + jnp.dot(
                y, jnp.where(fold, 1.0, 0.0).astype(bf16), preferred_element_type=f32
            )
        out_ref[:, lanes] += total
        return carry

    lax.fori_loop(0, chunks, chunk, 0)


def smem():
    return pl.BlockSpec(memory_space=pltpu.SMEM)


def whole(shape):
    return pl.BlockSpec(shape, lambda h: (0,) * len(shape))


def conv(plan, window, taps, back):
    chunks, prow, pcol, bseg = plan
    return pl.pallas_call(
        functools.partial(conv_kernel, back),
        grid=(4,),
        out_shape=jax.ShapeDtypeStruct((ROWS, HALF), f32),
        in_specs=[
            smem(),
            whole((8, WIN)),
            whole((WIN, 128)),
            whole((LCAP, 128)),
            whole((WIN, HALF)),
            whole((TAPS, CG, HALF)),
        ],
        out_specs=whole((ROWS, HALF)),
        scratch_shapes=[
            pltpu.VMEM((4, XM, WIN), bf16),
            pltpu.VMEM((NQ, CM, 128), bf16),
            pltpu.VMEM((2, PJ, 64, 128), bf16),
            pltpu.VMEM((2, XM, 256), bf16),
        ],
        compiler_params=pltpu.CompilerParams(vmem_limit_bytes=VLIM),
        cost_estimate=pl.CostEstimate(flops=30_000_000_000, bytes_accessed=9_000_000, transcendentals=0),
        name="conv_back" if back else "conv_forward",
    )(chunks, prow, pcol, bseg, window, taps)


def tap_grad_kernel(
    chunks_ref, prow_ref, bseg_ref, x_ref, d_ref, small_ref, out_ref, s_ref, sd_ref, mask_ref, xt_ref, dp_ref, acc_ref
):
    h = pl.program_id(0)
    base_tile = h // 2
    chunks = chunks_ref[0]

    @pl.when(h == 0)
    def _():
        out_ref[...] = jnp.zeros_like(out_ref)
        out_ref[:, out_ref.shape[1] - EXTRA :, :] = small_ref[...]
        dp_ref[...] = jnp.zeros_like(dp_ref)

    acc_ref[...] = jnp.zeros_like(acc_ref)
    sel = select_pair(h, 256, 128 * base_tile)
    lanes = pl.ds(pl.multiple_of(base_tile * 128, 128), 256)
    xdup = jnp.dot(x_ref[:, lanes], sel, preferred_element_type=f32).astype(bf16)
    ddup = jnp.dot(d_ref[:, lanes], sel, preferred_element_type=f32).astype(bf16)

    def chunk(c, carry):
        @pl.when((h == 0) | (chunks > 1))
        def _():
            build_selector(s_ref, prow_ref[0:1, :], c, 0, XM)
            build_selector(sd_ref, prow_ref[0:1, HALO : HALO + ROWS], c, 16, CM)
            seg = bseg_ref[pl.ds(pl.multiple_of(CM * c, 16), XM), :]
            none = jnp.full((32, 128), -7, i32)
            own = jnp.concatenate([none, seg[16 : 16 + CM], none], axis=0)
            for q in range(NQ):
                same = seg == own[32 - q : 32 - q + XM]
                mask_ref[q] = jnp.where(same, 1.0, 0.0).astype(bf16)

        xb = build_blocks(s_ref, xdup, XM)
        db = build_blocks(sd_ref, ddup, CM)
        for g in range(2):
            xt_ref[g] = xb[g].T
            dp_ref[g, 32 : 32 + CM, :] = db[g]
        for g in range(2):
            for q in range(NQ):
                m = mask_ref[q]
                ds = dp_ref[g, 32 - q : 32 - q + XM, :] * jnp.concatenate([m, m], axis=1)
                part = jnp.dot(xt_ref[g], ds, preferred_element_type=f32)
                acc_ref[g, 4 * q + 2 : 4 * q + 6] += part[:, 0:128].reshape(4, 64, 128)
                acc_ref[g, 4 * q : 4 * q + 4] += part[:, 128:256].reshape(4, 64, 128)
        return carry

    lax.fori_loop(0, chunks, chunk, 0)
    per = TAPS // out_ref.shape[0]
    low = iota((1, 1, 128), 2) < 64
    row = iota((128, 256), 0)
    lane = iota((128, 256), 1)
    src = CG * (2 * h + (row >> 6)) + (row & 63) - 128 * base_tile
    back = jnp.where(((row & 63) < CG) & (lane == src), 1.0, 0.0).astype(bf16)
    step = 16
    for j0 in range(0, TAPS, step):
        now = [acc_ref[g, j0 + 2 : j0 + 2 + step, 0:CG, :] for g in range(2)]
        nxt = [acc_ref[g, j0 + 3 : j0 + 3 + step, 0:CG, :] for g in range(2)]
        here = jnp.where(low, now[0], nxt[1]).reshape(step * CG, 128)
        far = jnp.where(low, now[1], nxt[0]).reshape(step * CG, 128)
        both = (here + pltpu.roll(far, 64, 1)).astype(bf16)
        o = jnp.dot(both, back, preferred_element_type=f32).astype(bf16)
        o = o.reshape(step // per, per * CG, 256)
        out_ref[j0 // per : (j0 + step) // per, 0 : per * CG, lanes] += o


def tap_grad(plan, window, d_conv, small):
    chunks, prow, pcol, bseg = plan
    devices = small.shape[0]
    shape = (devices, TAPS // devices * CG + EXTRA, HALF)
    return pl.pallas_call(
        tap_grad_kernel,
        grid=(4,),
        out_shape=jax.ShapeDtypeStruct(shape, bf16),
        in_specs=[
            smem(),
            whole((8, WIN)),
            whole((LCAP, 128)),
            whole((WIN, HALF)),
            whole((ROWS, HALF)),
            whole(small.shape),
        ],
        out_specs=whole(shape),
        scratch_shapes=[
            pltpu.VMEM((4, XM, WIN), bf16),
            pltpu.VMEM((4, CM, ROWS), bf16),
            pltpu.VMEM((NQ, XM, 128), bf16),
            pltpu.VMEM((2, 256, XM), bf16),
            pltpu.VMEM((2, 32 + CM + 32, 256), bf16),
            pltpu.VMEM((2, PJ, 64, 128), f32),
        ],
        compiler_params=pltpu.CompilerParams(vmem_limit_bytes=VLIM),
        cost_estimate=pl.CostEstimate(flops=40_000_000_000, bytes_accessed=9_000_000, transcendentals=0),
        name="tap_gradient",
    )(chunks, prow, bseg, window, d_conv, small)
REACH = 1536
SPAN = ROWS + 2 * REACH
QT, KT = 128, 1664
NEAR = REACH - ROWS
NEG = -1e30


def segment_count(ends, positions):
    return jnp.sum((ends[None, :] <= positions[:, None]).astype(i32), axis=1).astype(i32)

def attention_plan(starts, ends, first, odd):
    w = first - REACH + jnp.arange(SPAN, dtype=i32)
    kseg = segment_count(ends, w)
    kseg = jnp.where(w < 0, -1, kseg)
    qseg = kseg[REACH : REACH + ROWS]
    edge = qseg.reshape(ROWS // QT, QT)
    n = jnp.arange(starts.shape[0], dtype=i32)
    head = jnp.sum(jnp.where(n[None] == edge[:, :1], starts[None], 0), axis=1) - (first - REACH)
    tail = jnp.sum(jnp.where(n[None] == edge[:, -1:], ends[None], 0), axis=1) - (first - REACH)
    lo = jnp.clip(head // 128, 0, SPAN // 128)
    hi = jnp.clip((tail + 127) // 128, 1, SPAN // 128)
    tiles = jnp.maximum((hi - lo + KT // 128 - 1) // (KT // 128), 1)
    lo = jnp.minimum(lo, SPAN // 128 - tiles * (KT // 128))
    return (
        jnp.stack([lo, tiles, jnp.full_like(lo, odd)]).astype(i32),
        jnp.broadcast_to(qseg[None], (8, ROWS)),
        jnp.broadcast_to(kseg[:, None], (SPAN, 128)),
    )

def split_heads(a):
    low = iota(a.shape, 1) < 64
    zero = jnp.zeros((), a.dtype)
    return jnp.where(low, a, zero), jnp.where(low, zero, a)

def spots(range_ref):
    odd = range_ref[2, 0] == 1
    right, end = REACH + ROWS, SPAN - NEAR
    at = [
        jnp.where(odd, NEAR, right),
        jnp.where(odd, right, NEAR),
        jnp.where(odd, end, 0),
        jnp.where(odd, 0, end),
    ]
    return [pl.multiple_of(x, NEAR) for x in at]


def fill_span(range_ref, span_ref, own, others):
    span_ref[REACH : REACH + ROWS, :] = own[...]
    for at, piece in zip(spots(range_ref), others):
        span_ref[pl.ds(at, piece.shape[0]), :] = piece[...]


def flip_span(src_ref, dst_ref, lane):
    for at in range(0, SPAN, 512):
        dst_ref[:, at : at + 512] = src_ref[at : at + 512, lane : lane + 128].T


def same_segment(kseg_ref, qseg_ref, at):
    ks = kseg_ref[at, :]
    ks = jnp.concatenate([ks] * (QT // 128), axis=1) if QT > 128 else ks
    return ks == qseg_ref[0:1, :]


def forward_kernel(range_ref, qseg_ref, kseg_ref, q_ref, k0, k1, k2, k3, k4, o_ref, half_ref, lse_ref, span_ref, vt_ref):
    qi = pl.program_id(0)

    @pl.when(qi == 0)
    def _():
        fill_span(range_ref, span_ref, k0, (k1, k2, k3, k4))
        flip_span(span_ref, vt_ref, 128)

    qs = split_heads(q_ref[...])

    first, count = range_ref[0, qi], range_ref[1, qi]

    def tile(t, carry):
        at = pl.ds(pl.multiple_of((first + t * (KT // 128)) * 128, 128), KT)
        same = same_segment(kseg_ref, qseg_ref, at)
        k = span_ref[at, 0:128]
        out = []
        for e in range(2):
            m, l, acc = carry[e]
            s = lax.dot_general(k, qs[e], (((1,), (1,)), ((), ())), preferred_element_type=f32)
            s = jnp.where(same, s, NEG)
            new = jnp.maximum(m, jnp.max(s, axis=0, keepdims=True))
            p = jnp.exp(s - new)
            alpha = jnp.exp(m - new)
            l = l * alpha + jnp.sum(p, axis=0, keepdims=True)
            vt = vt_ref[64 * e : 64 * e + 64, at]
            acc = acc * alpha + jnp.dot(vt, p.astype(bf16), preferred_element_type=f32)
            out.append((new, l, acc))
        return tuple(out)

    start = (jnp.full((1, QT), NEG, f32), jnp.zeros((1, QT), f32), jnp.zeros((64, QT), f32))
    ends = lax.fori_loop(0, count, tile, (start, start))
    o = jnp.concatenate([acc / l for _, l, acc in ends], axis=0).T
    o_ref[...] = o
    half_ref[...] = o.astype(bf16)
    for e in range(2):
        lse_ref[e : e + 1, :] = ends[e][0] + jnp.log(ends[e][1])


def piece_specs(h):
    return [pl.BlockSpec((n, 256), lambda i: (0, h)) for n in (ROWS, ROWS, ROWS, NEAR, NEAR)]


def attend(plan, h, q, pieces):
    ranges, qseg, kseg = plan
    return pl.pallas_call(
        forward_kernel,
        grid=(ROWS // QT,),
        out_shape=(
            jax.ShapeDtypeStruct((ROWS, 128), f32),
            jax.ShapeDtypeStruct((ROWS, 128), bf16),
            jax.ShapeDtypeStruct((8, ROWS), f32),
        ),
        in_specs=[
            pl.BlockSpec(memory_space=pltpu.SMEM),
            pl.BlockSpec((8, QT), lambda i: (0, i)),
            pl.BlockSpec((SPAN, 128), lambda i: (0, 0)),
            pl.BlockSpec((QT, 128), lambda i: (i, h)),
        ]
        + piece_specs(h),
        out_specs=(
            pl.BlockSpec((QT, 128), lambda i: (i, 0)),
            pl.BlockSpec((QT, 128), lambda i: (i, 0)),
            pl.BlockSpec((8, QT), lambda i: (0, i)),
        ),
        scratch_shapes=[pltpu.VMEM((SPAN, 256), bf16), pltpu.VMEM((128, SPAN), bf16)],
        compiler_params=pltpu.CompilerParams(vmem_limit_bytes=VLIM),
        cost_estimate=pl.CostEstimate(flops=8_000_000_000, bytes_accessed=8_000_000, transcendentals=0),
        name="attention_forward",
    )(ranges, qseg, kseg, q, *pieces)


def backward_kernel(range_ref, qseg_ref, kseg_ref, q_ref, k0, k1, k2, k3, k4, do_ref, o_ref, lse_ref,
                    dq_ref, own_ref, f1, f2, f3, f4, span_ref, kt_ref, dkv_ref):
    qi = pl.program_id(0)
    last = ROWS // QT - 1

    @pl.when(qi == 0)
    def _():
        dkv_ref[...] = jnp.zeros_like(dkv_ref)
        fill_span(range_ref, span_ref, k0, (k1, k2, k3, k4))
        flip_span(span_ref, kt_ref, 0)

    qs = split_heads(q_ref[...])
    dos = split_heads(do_ref[...])
    qcat = jnp.concatenate(qs, axis=0)
    docat = jnp.concatenate(dos, axis=0)
    dm = (do_ref[...].astype(f32) * o_ref[...]).T
    delta = [jnp.sum(dm[64 * e : 64 * e + 64], axis=0, keepdims=True) for e in range(2)]

    first, count = range_ref[0, qi], range_ref[1, qi]

    def tile(t, carry):
        at = pl.ds(pl.multiple_of((first + t * (KT // 128)) * 128, 128), KT)
        same = same_segment(kseg_ref, qseg_ref, at)
        k = span_ref[at, 0:128]
        v = span_ref[at, 128:256]
        ps, dss, out = [], [], []
        for e in range(2):
            dims = (((1,), (1,)), ((), ()))
            s = lax.dot_general(k, qs[e], dims, preferred_element_type=f32)
            p = jnp.exp(jnp.where(same, s - lse_ref[e : e + 1, :], NEG))
            dp = lax.dot_general(v, dos[e], dims, preferred_element_type=f32)
            ds = (p * (dp - delta[e])).astype(bf16)
            kt = kt_ref[64 * e : 64 * e + 64, at]
            out.append(carry[e] + jnp.dot(kt, ds, preferred_element_type=f32))
            ps.append(p.astype(bf16))
            dss.append(ds)
        dkv_ref[at, 0:128] += jnp.dot(jnp.concatenate(dss, axis=1), qcat, preferred_element_type=f32)
        dkv_ref[at, 128:256] += jnp.dot(jnp.concatenate(ps, axis=1), docat, preferred_element_type=f32)
        return tuple(out)

    zero = jnp.zeros((64, QT), f32)
    dqt = lax.fori_loop(0, count, tile, (zero, zero))
    dq = jnp.concatenate(dqt, axis=0).T
    dq_ref[...] = dq.astype(bf16) * jnp.asarray(0.125, bf16)

    @pl.when(qi == last)
    def _():
        for at, far in zip(spots(range_ref), (f1, f2, f3, f4)):
            far[...] = dkv_ref[pl.ds(at, far.shape[0]), :].astype(bf16)
        own_ref[...] = dkv_ref[REACH : REACH + ROWS, :]


def attend_back(plan, h, q, pieces, d_att, mixed, lse):
    ranges, qseg, kseg = plan
    rowspec = pl.BlockSpec((QT, 128), lambda i: (i, 0))
    colspec = pl.BlockSpec((QT, 128), lambda i: (i, h))
    return pl.pallas_call(
        backward_kernel,
        grid=(ROWS // QT,),
        out_shape=(
            jax.ShapeDtypeStruct((ROWS, 128), bf16),
            jax.ShapeDtypeStruct((ROWS, 256), f32),
        )
        + tuple(jax.ShapeDtypeStruct((n, 256), bf16) for n in (ROWS, ROWS, NEAR, NEAR)),
        in_specs=[
            pl.BlockSpec(memory_space=pltpu.SMEM),
            pl.BlockSpec((8, QT), lambda i: (0, i)),
            pl.BlockSpec((SPAN, 128), lambda i: (0, 0)),
            colspec,
        ]
        + piece_specs(h)
        + [colspec, rowspec, pl.BlockSpec((8, QT), lambda i: (0, i))],
        out_specs=(
            rowspec,
            pl.BlockSpec((ROWS, 256), lambda i: (0, 0)),
        )
        + tuple(pl.BlockSpec((n, 256), lambda i: (0, 0)) for n in (ROWS, ROWS, NEAR, NEAR)),
        scratch_shapes=[
            pltpu.VMEM((SPAN, 256), bf16),
            pltpu.VMEM((128, SPAN), bf16),
            pltpu.VMEM((SPAN, 256), f32),
        ],
        compiler_params=pltpu.CompilerParams(vmem_limit_bytes=VLIM),
        cost_estimate=pl.CostEstimate(flops=8_000_000_000, bytes_accessed=12_000_000, transcendentals=0),
        name="attention_backward",
    )(ranges, qseg, kseg, q, *pieces, d_att, mixed, lse)


def exchange(part):
    return lax.ppermute(part, "heads", [(0, 1), (1, 0)])


def pair_sum(part):
    half = part.astype(bf16)
    return half.astype(f32) + exchange(half).astype(f32)


def side_by_side(own, other, index):
    return jnp.where(
        index == 0,
        jnp.concatenate([own, other], axis=1),
        jnp.concatenate([other, own], axis=1),
    )


def passed(block, distance):
    count = lax.axis_size("seq")
    route = [(i - distance, i) for i in range(count) if 0 <= i - distance < count]
    return lax.ppermute(block, "seq", route)


def across_cores(block):
    return lax.ppermute(block, "seq", [(i, i ^ 1) for i in range(lax.axis_size("seq"))])


def across_chips(block):
    count = lax.axis_size("seq")
    route = [(i, i + 1 if i % 2 else i - 1) for i in range(count)]
    return lax.ppermute(block, "seq", [(i, j) for i, j in route if 0 <= j < count])


def chip_along(block, step):
    count = lax.axis_size("seq")
    route = [(i, i - 2 * step if i % 2 else i + 2 * step) for i in range(count)]
    return lax.ppermute(block, "seq", [(i, j) for i, j in route if 0 <= j < count])


def layer_norm(values, gain, shift):
    centered = values - jnp.mean(values, axis=-1, keepdims=True)
    scale = lax.rsqrt(jnp.mean(centered * centered, axis=-1, keepdims=True) + EPSILON)
    return centered * scale * gain + shift


def gelu_exact(values):
    return jax.nn.gelu(values, approximate=False)


def nesterov(weight, grad, moment, average, rate):
    moment_new = 0.5 * moment + grad
    weight_new = weight - rate * (grad + 0.5 * moment_new)
    average_new = 0.5 * average + 0.5 * weight_new
    return (grad, weight_new, moment_new, average_new, weight_new.astype(bf16))


def dot(a, b, ca, cb):
    return lax.dot_general(a, b, (((ca,), (cb,)), ((), ())), preferred_element_type=f32)


def gathered(shard):
    return lax.all_gather(shard, "seq", axis=0, tiled=True)


def scattered(whole_sum):
    return lax.psum_scatter(whole_sum, "seq", scatter_dimension=0, tiled=True)


def body(
    frames,
    cotangent,
    lengths,
    kernel,
    kernel_moment,
    kernel_average,
    project,
    project_moment,
    project_average,
    combine,
    combine_moment,
    combine_average,
    expand,
    expand_moment,
    expand_average,
    shrink,
    shrink_moment,
    shrink_average,
    unitbias,
    unitbias_moment,
    unitbias_average,
    chanbias,
    chanbias_moment,
    chanbias_average,
    outbias,
    outbias_moment,
    outbias_average,
    normparams,
    normparams_moment,
    normparams_average,
):
    devices = lax.axis_size("seq")
    rows, width = frames.shape
    total = devices * rows
    first = lax.axis_index("seq") * rows
    index = lax.axis_index("heads")
    odd = lax.axis_index("seq") % 2
    local = project.shape[0]
    hidden_units = expand.shape[1]

    w_kernel = gathered(jnp.transpose(kernel, (2, 1, 0)).astype(bf16))
    small = jnp.concatenate(
        [unitbias, chanbias.reshape(-1), outbias.reshape(-1), normparams.reshape(-1)]
    ).astype(bf16)
    w_small = gathered(small[None])
    w_first = gathered(
        jnp.concatenate(
            [project[:, 0]]
            + [project[:, c, 128 * h : 128 * h + 128] for h in range(PAIRS) for c in (1, 2)]
            + [combine.T],
            axis=1,
        ).astype(bf16)
    )
    w_second = gathered(jnp.concatenate([expand, shrink.T], axis=1).astype(bf16))
    w_combine = w_first[:, 3 * HALF :]
    w_combine_far = exchange(w_combine)
    cuts = [unitbias.size, chanbias.size, outbias.size, normparams.size]
    parts, at = [], 0
    for size in cuts:
        parts.append(w_small[:, at : at + size].astype(f32))
        at += size
    b_unit = parts[0].reshape(-1)
    b_chan = jnp.transpose(parts[1].reshape(devices, 3, -1), (1, 0, 2)).reshape(3, -1)
    b_out = jnp.transpose(parts[2].reshape(devices, 2, -1), (1, 0, 2)).reshape(2, -1)
    norms = jnp.transpose(parts[3].reshape(devices, 3, 2, -1), (1, 2, 0, 3)).reshape(3, 2, -1)

    count = lengths.shape[0]
    order = jnp.arange(count, dtype=i32)
    ends = jnp.sum(jnp.where(order[None, :] <= order[:, None], lengths[None, :], 0), axis=1).astype(i32)
    starts = ends - lengths
    plan = block_plan(starts, ends, first)
    reach = attention_plan(starts, ends, first, odd)

    x_half = lax.dynamic_slice_in_dim(frames, index * HALF, HALF, 1).astype(bf16)
    window = jnp.concatenate(
        [passed(x_half[rows - HALO :], 1), x_half, passed(x_half[:HALO], -1)], axis=0
    )
    pre = conv(plan, window, w_kernel, False) + b_chan[0]
    spread_part = gelu_exact(pre).astype(bf16)
    spread = side_by_side(spread_part, exchange(spread_part), index)
    h1, norm0_back = jax.vjp(layer_norm, frames + spread.astype(f32), norms[0, 0], norms[0, 1])
    h1_half = h1.astype(bf16)
    proj = dot(h1_half, w_first[:, : 3 * HALF], 1, 0)
    scale = HEAD ** (-0.5)
    queries = ((proj[:, :HALF] + b_chan[1]) * scale).astype(bf16)
    kv_bias = b_chan[2].reshape(PAIRS, 1, 128)
    kv_bias = jnp.concatenate([jnp.zeros_like(kv_bias), kv_bias], axis=1).reshape(-1)
    both = (proj[:, HALF:] + kv_bias).astype(bf16)
    near = NEAR
    beside = across_chips(both)
    further = chip_along(jnp.where(odd == 1, both[:near], both[rows - near :]), 1)
    pieces = (
        both,
        across_cores(both),
        beside,
        further,
        across_cores(jnp.where(odd == 1, beside[:near], beside[rows - near :])),
    )
    mixed, attended, attended_far, lse = [], [], [], []
    for h in range(PAIRS):
        if h == 0:
            q_part, w_combine_far = lax.optimization_barrier((queries, w_combine_far))
        if h >= 2:
            q_part, attended_far[h - 2] = lax.optimization_barrier((queries, attended_far[h - 2]))
        mixed_part, half, lse_part = attend(reach, h, q_part, pieces)
        mixed.append(mixed_part)
        lse.append(lse_part)
        attended.append(half)
        attended_far.append(exchange(half))
    attended = jnp.concatenate(attended, axis=1)
    attended_all = side_by_side(attended, jnp.concatenate(attended_far, axis=1), index)
    branch = dot(attended_all, side_by_side(w_combine, w_combine_far, index), 1, 1)
    h2, norm1_back = jax.vjp(layer_norm, h1 + branch + b_out[0], norms[1, 0], norms[1, 1])
    h2_half = h2.astype(bf16)
    w_expand = w_second[:, :hidden_units]
    w_shrink = w_second[:, hidden_units:]
    inner = dot(h2_half, w_expand, 1, 0) + b_unit
    hidden, gelu_inner_back = jax.vjp(gelu_exact, inner)
    hidden_half = hidden.astype(bf16)
    outer = pair_sum(dot(hidden_half, w_shrink, 1, 1))
    layer_out, norm2_back = jax.vjp(layer_norm, h2 + outer + b_out[1], norms[2, 0], norms[2, 1])
    dx3, gain2_grad, shift2_grad = norm2_back(cotangent)
    outer_bias_grad = jnp.sum(dx3, axis=0)
    d_out = dx3.astype(bf16)
    d_hidden = dot(d_out, w_shrink, 1, 0)
    d_inner = gelu_inner_back(d_hidden)[0]
    unit_grad = jnp.sum(d_inner, axis=0)
    d_inner_half = d_inner.astype(bf16)
    dh2 = dx3 + pair_sum(dot(d_inner_half, w_expand, 1, 1))
    second_part = jnp.concatenate(
        [dot(h2_half, d_inner_half, 0, 0).astype(bf16), dot(d_out, hidden_half, 0, 0).astype(bf16)],
        axis=1,
    )
    dx2, gain1_grad, shift1_grad = norm1_back(dh2)
    branch_bias_grad = jnp.sum(dx2, axis=0)
    d_branch = dx2.astype(bf16)
    d_att = dot(d_branch, w_combine, 1, 0).astype(bf16)
    d_att, second_part = lax.optimization_barrier((d_att, second_part))
    second_sum = scattered(second_part).astype(f32)
    dq_parts, kv_parts = [], []
    arrived = {}
    for h in range(PAIRS):
        d_part = d_att
        if h >= 1:
            d_part, passed_on = lax.optimization_barrier((d_part, passed_on))
            chip = (chip.astype(f32) + passed_on).astype(bf16)
            arrived[h - 1] = (across_cores(core), across_chips(chip), chip_along(far, -1), own)
        if h >= 2:
            d_part, arrived[h - 2] = lax.optimization_barrier((d_part, arrived[h - 2]))
        dq_part, own, core, chip, far, near_far = attend_back(
            reach, h, queries, pieces, d_part, mixed[h], lse[h]
        )
        passed_on = across_cores(near_far).astype(f32)
        none = jnp.zeros_like(passed_on)
        passed_on = jnp.concatenate(
            [jnp.where(odd == 1, passed_on, none), jnp.where(odd == 1, none, passed_on)], axis=0
        )
        dq_parts.append(dq_part)
    chip = (chip.astype(f32) + passed_on).astype(bf16)
    arrived[PAIRS - 1] = (across_cores(core), across_chips(chip), chip_along(far, -1), own)
    for h in range(PAIRS):
        core, chip, far, own = arrived[h]
        far = far.astype(f32)
        none = jnp.zeros_like(far)
        far = jnp.concatenate([jnp.where(odd == 1, far, none), jnp.where(odd == 1, none, far)], axis=0)
        kv_parts.append((own + core.astype(f32) + chip.astype(f32) + far).astype(bf16))
    dq_half = jnp.concatenate(dq_parts, axis=1)
    d_both_half = jnp.concatenate(kv_parts, axis=1)
    stacked = jnp.concatenate([dq_half, d_both_half], axis=1)
    query_bias_grad = jnp.sum(dq_half.astype(f32), axis=0)
    value_bias_grad = jnp.sum(
        d_both_half.astype(f32), axis=0
    ).reshape(PAIRS, 2, 128)[:, 1].reshape(-1)
    dh1 = dx2 + pair_sum(dot(stacked, w_first[:, : 3 * HALF], 1, 1))
    first_part = (
        jnp.concatenate(
            [dot(h1_half, stacked, 0, 0).astype(bf16), dot(d_branch, attended, 0, 0).astype(bf16)],
            axis=1,
        )
    )
    first_part, second_sum = lax.optimization_barrier((first_part, second_sum))
    first_sum = scattered(first_part).astype(f32)
    dx1, gain0_grad, shift0_grad = norm0_back(dh1)
    d_spread = lax.dynamic_slice_in_dim(dx1, index * HALF, HALF, 1)
    d_conv = jax.vjp(gelu_exact, pre)[1](d_spread)[0]
    conv_bias_grad = jnp.sum(d_conv, axis=0)
    d_conv_half = d_conv.astype(bf16)
    spread_out = lambda grad, lead: jnp.transpose(
        grad.reshape(lead, devices, -1), (1, 0, 2)
    ).reshape(devices, -1)
    small_part = jnp.concatenate(
            [
                unit_grad.reshape(devices, -1),
                spread_out(jnp.stack([conv_bias_grad, query_bias_grad, value_bias_grad]), 3),
                spread_out(jnp.stack([branch_bias_grad, outer_bias_grad]), 2),
                spread_out(
                    jnp.stack(
                        [gain0_grad, shift0_grad, gain1_grad, shift1_grad, gain2_grad, shift2_grad]
                    ),
                    6,
                ),
            ],
            axis=1,
        )
    small_part = jnp.pad(small_part, ((0, 0), (0, EXTRA * HALF - small_part.shape[1])))
    small_part = small_part.astype(bf16).reshape(devices, EXTRA, HALF)
    tap_part = tap_grad(plan, window, d_conv_half, small_part)
    tap_part, first_sum = lax.optimization_barrier((tap_part, first_sum))
    tap_sum = scattered(tap_part)[0].astype(f32)
    kernel_sum = tap_sum[:-EXTRA].reshape(TAPS // devices, CG, HALF)
    small_sum = tap_sum[-EXTRA:].reshape(-1)
    d_window = jnp.concatenate(
        [passed(d_conv_half[rows - HALO :], 1), d_conv_half, passed(d_conv_half[:HALO], -1)], axis=0
    )
    d_input = conv(plan, d_window, w_kernel, True).astype(bf16)
    frames_grad = dx1 + side_by_side(d_input, exchange(d_input), index).astype(f32)

    pieces, at = [], 0
    for size in cuts:
        pieces.append(small_sum[at : at + size])
        at += size
    unit_sum = pieces[0]
    chan_sum = pieces[1].reshape(chanbias.shape)
    out_sum = pieces[2].reshape(outbias.shape)
    norm_sum = pieces[3].reshape(normparams.shape)
    kv_sum = first_sum[:, HALF : 3 * HALF].reshape(local, PAIRS, 2, 128)
    project_sum = jnp.stack(
        [first_sum[:, :HALF]] + [kv_sum[:, :, c].reshape(local, HALF) for c in range(2)], axis=1
    )

    root = total**0.5
    small_rate = 0.1 / root
    out = [layer_out, frames_grad]
    for weight, grad, moment, average, rate in (
        (kernel, jnp.transpose(kernel_sum, (2, 1, 0)), kernel_moment, kernel_average, (CG * TAPS) ** (-0.5) / root),
        (project, project_sum, project_moment, project_average, width ** (-0.5) / root),
        (combine, first_sum[:, 3 * HALF :].T, combine_moment, combine_average, (width // 16) ** (-0.5) / root),
        (expand, second_sum[:, :hidden_units], expand_moment, expand_average, width ** (-0.5) / root),
        (shrink, second_sum[:, hidden_units:].T, shrink_moment, shrink_average, (2 * hidden_units) ** (-0.5) / root),
        (unitbias, unit_sum, unitbias_moment, unitbias_average, 0.5 / root),
        (chanbias, chan_sum, chanbias_moment, chanbias_average, small_rate),
        (outbias, out_sum, outbias_moment, outbias_average, small_rate),
        (normparams, norm_sum, normparams_moment, normparams_average, small_rate),
    ):
        out.extend(nesterov(weight, grad, moment, average, rate))
    return tuple(out)


def solution(mesh):
    kernel_spec = P("heads", None, "seq")
    project_spec = P("seq", None, "heads")
    tall = P("heads", "seq")
    wide = P("seq", "heads")
    unit = P(("heads", "seq"))
    chan = P(None, ("heads", "seq"))
    outb = P(None, "seq")
    norm = P(None, None, "seq")
    weights = (kernel_spec, project_spec, tall, wide, tall, unit, chan, outb, norm)
    rows = P("seq", None)
    return jax.shard_map(
        body,
        mesh=mesh,
        in_specs=(rows, rows, P()) + tuple(s for s in weights for _ in range(3)),
        out_specs=(rows, rows) + tuple(s for s in weights for _ in range(5)),
        check_vma=False,
    )
```

```python
import functools

import jax
import jax.numpy as jnp
from jax import lax
from jax.experimental import pallas as pl
from jax.experimental.pallas import tpu as pltpu
from jax.sharding import PartitionSpec as P

HEAD = 64
PAIRS = 3
CHUNKS = 2
EPSILON = 1e-05

bf16, f32, i32 = jnp.bfloat16, jnp.float32, jnp.int32
CG, TAPS, GROUPS, HALO = 48, 128, 8, 64
ROWS, WIN, HALF = 1024, 1152, 384
CM, XM = 272, 304
NQ = 33
LCAP = 1408
PJ = 134
EXTRA = 16
VLIM = 58 << 20


def iota(shape, dim):
    return lax.broadcasted_iota(i32, shape, dim)


def block_plan(starts, ends, first):
    w0 = first - HALO
    b = jnp.clip(starts - w0, 0, WIN)
    e = jnp.clip(ends - w0, 0, WIN)
    nblk = (e - b + 3) // 4
    n = starts.shape[0]
    before = jnp.arange(n)[None, :] < jnp.arange(n)[:, None]
    bs = jnp.sum(jnp.where(before, nblk[None, :], 0), axis=1).astype(i32)
    bs = bs + (jnp.clip(-w0, 0, WIN) + 3) // 4
    w = jnp.arange(WIN, dtype=i32)
    inside = (b[None, :] <= w[:, None]) & (w[:, None] < e[None, :])
    p = jnp.sum(jnp.where(inside, 4 * bs - b + w[:, None] + 1, 0), axis=1).astype(i32) - 1
    m = jnp.arange(LCAP, dtype=i32)
    hit = (bs[None, :] <= m[:, None]) & (m[:, None] < (bs + nblk)[None, :])
    bseg = jnp.sum(jnp.where(hit, jnp.arange(1, n + 1, dtype=i32)[None, :], 0), axis=1).astype(i32) - 1
    chunks = jnp.maximum((p[HALO + ROWS - 1] // 4 - 16) // CM + 1, 1)
    return (
        jnp.reshape(chunks, (1,)).astype(i32),
        jnp.broadcast_to(p[None, :], (8, WIN)),
        jnp.broadcast_to(p[:, None], (WIN, 128)),
        jnp.broadcast_to(bseg[:, None], (LCAP, 128)),
    )


def select_pair(h, rows, base):
    lane = iota((rows, 256), 1)
    src = CG * (2 * h + (lane >> 7)) + (lane & 63) - base
    ok = ((lane & 63) < CG) & (iota((rows, 256), 0) == src)
    return jnp.where(ok, 1.0, 0.0).astype(bf16)


def build_selector(s_ref, prow, c, first, rows):
    for t in range(4):
        pos = 4 * (iota((rows, prow.shape[1]), 0) + (CM * c + first)) + t
        s_ref[t] = jnp.where(pos == prow, 1.0, 0.0).astype(bf16)


def build_blocks(s_ref, dup, rows):
    y = [
        jnp.dot(s_ref[t], dup, preferred_element_type=f32).astype(bf16) for t in range(4)
    ]
    low = iota((rows, 128), 1) < 64
    out = []
    for g in range(2):
        tiles = [v[:, 128 * g : 128 * g + 128] for v in y]
        out.append(
            jnp.concatenate(
                [jnp.where(low, tiles[0], tiles[1]), jnp.where(low, tiles[2], tiles[3])], axis=1
            )
        )
    return out


def build_taps(k_ref, sel, p_ref, base_tile):
    p_ref[...] = jnp.zeros_like(p_ref)
    step = 16
    for j0 in range(0, TAPS, step):
        part = k_ref[pl.ds(j0, step), :, pl.ds(pl.multiple_of(base_tile * 128, 128), 256)]
        d = jnp.dot(part.reshape(step * CG, 256), sel, preferred_element_type=f32)
        d = d.astype(bf16).reshape(step, CG, 256)
        for g in range(2):
            p_ref[g, pl.ds(j0 + 2, step), 0:CG, 0:64] = d[:, :, 128 * g : 128 * g + 64]
            p_ref[g, pl.ds(j0 + 3, step), 0:CG, 64:128] = d[:, :, 128 * g + 64 : 128 * g + 128]


def conv_kernel(
    back, chunks_ref, prow_ref, pcol_ref, bseg_ref, x_ref, k_ref, out_ref, s_ref, mask_ref, p_ref, xb_ref
):
    h = pl.program_id(0)
    base_tile = h // 2
    chunks = chunks_ref[0]

    @pl.when(h == 0)
    def _():
        out_ref[...] = jnp.zeros_like(out_ref)

    sel = select_pair(h, 256, 128 * base_tile)
    build_taps(k_ref, sel, p_ref, base_tile)
    lanes = pl.ds(pl.multiple_of(base_tile * 128, 128), 256)
    dup = jnp.dot(x_ref[:, lanes], sel, preferred_element_type=f32).astype(bf16)

    def chunk(c, carry):
        @pl.when((h == 0) | (chunks > 1))
        def _():
            build_selector(s_ref, prow_ref[0:1, :], c, 0, XM)
            seg = bseg_ref[pl.ds(pl.multiple_of(CM * c, 16), XM), :]
            for q in range(NQ):
                same = seg[q : q + CM] == seg[16 : 16 + CM]
                mask_ref[q] = jnp.where(same, 1.0, 0.0).astype(bf16)

        xb = build_blocks(s_ref, dup, XM)
        for g in range(2):
            xb_ref[g] = xb[g]
        pcol = pcol_ref[pl.ds(HALO, ROWS), :]
        local = (pcol >> 2) - (16 + CM * c)
        place = jnp.where(
            jnp.concatenate([local] * 3, axis=1)[:, :CM] == iota((ROWS, CM), 1), 1.0, 0.0
        ).astype(bf16)
        phase = pcol & 3
        hi = iota((ROWS, 128), 1) >> 6
        pick = jnp.concatenate([phase == hi, phase == hi + 2], axis=1)
        total = jnp.zeros((ROWS, 256), f32)
        for g in range(2):
            acc = jnp.zeros((CM, 256), f32)
            for q in range(NQ):
                m = mask_ref[q]
                xs = xb_ref[g, q : q + CM, :] * jnp.concatenate([m, m], axis=1)
                if back:
                    a, b = 130 - 4 * q, 128 - 4 * q
                else:
                    a, b = 4 * q + 2, 4 * q
                w = jnp.concatenate(
                    [
                        p_ref[g, a : a + 4].reshape(256, 128),
                        p_ref[g, b : b + 4].reshape(256, 128),
                    ],
                    axis=1,
                )
                dims = (((1,), (1 if back else 0,)), ((), ()))
                acc = acc + lax.dot_general(xs, w, dims, preferred_element_type=f32)
            y = jnp.dot(place, acc.astype(bf16), preferred_element_type=f32)
            y = jnp.where(pick, y, 0.0).astype(bf16)
            lane = iota((256, 256), 1)
            row = iota((256, 256), 0) & 63
            fold = (row < CG) & (lane == CG * (2 * h + g) - 128 * base_tile + row)
            total = total + jnp.dot(
                y, jnp.where(fold, 1.0, 0.0).astype(bf16), preferred_element_type=f32
            )
        out_ref[:, lanes] += total
        return carry

    lax.fori_loop(0, chunks, chunk, 0)


def smem():
    return pl.BlockSpec(memory_space=pltpu.SMEM)


def whole(shape):
    return pl.BlockSpec(shape, lambda h: (0,) * len(shape))


def conv(plan, window, taps, back):
    chunks, prow, pcol, bseg = plan
    return pl.pallas_call(
        functools.partial(conv_kernel, back),
        grid=(4,),
        out_shape=jax.ShapeDtypeStruct((ROWS, HALF), f32),
        in_specs=[
            smem(),
            whole((8, WIN)),
            whole((WIN, 128)),
            whole((LCAP, 128)),
            whole((WIN, HALF)),
            whole((TAPS, CG, HALF)),
        ],
        out_specs=whole((ROWS, HALF)),
        scratch_shapes=[
            pltpu.VMEM((4, XM, WIN), bf16),
            pltpu.VMEM((NQ, CM, 128), bf16),
            pltpu.VMEM((2, PJ, 64, 128), bf16),
            pltpu.VMEM((2, XM, 256), bf16),
        ],
        compiler_params=pltpu.CompilerParams(vmem_limit_bytes=VLIM),
        cost_estimate=pl.CostEstimate(flops=30_000_000_000, bytes_accessed=9_000_000, transcendentals=0),
        name="conv_back" if back else "conv_forward",
    )(chunks, prow, pcol, bseg, window, taps)


def tap_grad_kernel(
    chunks_ref, prow_ref, bseg_ref, x_ref, d_ref, small_ref, out_ref, s_ref, sd_ref, mask_ref, xt_ref, dp_ref, acc_ref
):
    h = pl.program_id(0)
    base_tile = h // 2
    chunks = chunks_ref[0]

    @pl.when(h == 0)
    def _():
        out_ref[...] = jnp.zeros_like(out_ref)
        out_ref[:, out_ref.shape[1] - EXTRA :, :] = small_ref[...]
        dp_ref[...] = jnp.zeros_like(dp_ref)

    acc_ref[...] = jnp.zeros_like(acc_ref)
    sel = select_pair(h, 256, 128 * base_tile)
    lanes = pl.ds(pl.multiple_of(base_tile * 128, 128), 256)
    xdup = jnp.dot(x_ref[:, lanes], sel, preferred_element_type=f32).astype(bf16)
    ddup = jnp.dot(d_ref[:, lanes], sel, preferred_element_type=f32).astype(bf16)

    def chunk(c, carry):
        @pl.when((h == 0) | (chunks > 1))
        def _():
            build_selector(s_ref, prow_ref[0:1, :], c, 0, XM)
            build_selector(sd_ref, prow_ref[0:1, HALO : HALO + ROWS], c, 16, CM)
            seg = bseg_ref[pl.ds(pl.multiple_of(CM * c, 16), XM), :]
            none = jnp.full((32, 128), -7, i32)
            own = jnp.concatenate([none, seg[16 : 16 + CM], none], axis=0)
            for q in range(NQ):
                same = seg == own[32 - q : 32 - q + XM]
                mask_ref[q] = jnp.where(same, 1.0, 0.0).astype(bf16)

        xb = build_blocks(s_ref, xdup, XM)
        db = build_blocks(sd_ref, ddup, CM)
        for g in range(2):
            xt_ref[g] = xb[g].T
            dp_ref[g, 32 : 32 + CM, :] = db[g]
        for g in range(2):
            for q in range(NQ):
                m = mask_ref[q]
                ds = dp_ref[g, 32 - q : 32 - q + XM, :] * jnp.concatenate([m, m], axis=1)
                part = jnp.dot(xt_ref[g], ds, preferred_element_type=f32)
                acc_ref[g, 4 * q + 2 : 4 * q + 6] += part[:, 0:128].reshape(4, 64, 128)
                acc_ref[g, 4 * q : 4 * q + 4] += part[:, 128:256].reshape(4, 64, 128)
        return carry

    lax.fori_loop(0, chunks, chunk, 0)
    per = TAPS // out_ref.shape[0]
    low = iota((1, 1, 128), 2) < 64
    row = iota((128, 256), 0)
    lane = iota((128, 256), 1)
    src = CG * (2 * h + (row >> 6)) + (row & 63) - 128 * base_tile
    back = jnp.where(((row & 63) < CG) & (lane == src), 1.0, 0.0).astype(bf16)
    step = 16
    for j0 in range(0, TAPS, step):
        now = [acc_ref[g, j0 + 2 : j0 + 2 + step, 0:CG, :] for g in range(2)]
        nxt = [acc_ref[g, j0 + 3 : j0 + 3 + step, 0:CG, :] for g in range(2)]
        here = jnp.where(low, now[0], nxt[1]).reshape(step * CG, 128)
        far = jnp.where(low, now[1], nxt[0]).reshape(step * CG, 128)
        both = (here + pltpu.roll(far, 64, 1)).astype(bf16)
        o = jnp.dot(both, back, preferred_element_type=f32).astype(bf16)
        o = o.reshape(step // per, per * CG, 256)
        out_ref[j0 // per : (j0 + step) // per, 0 : per * CG, lanes] += o


def tap_grad(plan, window, d_conv, small):
    chunks, prow, pcol, bseg = plan
    devices = small.shape[0]
    shape = (devices, TAPS // devices * CG + EXTRA, HALF)
    return pl.pallas_call(
        tap_grad_kernel,
        grid=(4,),
        out_shape=jax.ShapeDtypeStruct(shape, bf16),
        in_specs=[
            smem(),
            whole((8, WIN)),
            whole((LCAP, 128)),
            whole((WIN, HALF)),
            whole((ROWS, HALF)),
            whole(small.shape),
        ],
        out_specs=whole(shape),
        scratch_shapes=[
            pltpu.VMEM((4, XM, WIN), bf16),
            pltpu.VMEM((4, CM, ROWS), bf16),
            pltpu.VMEM((NQ, XM, 128), bf16),
            pltpu.VMEM((2, 256, XM), bf16),
            pltpu.VMEM((2, 32 + CM + 32, 256), bf16),
            pltpu.VMEM((2, PJ, 64, 128), f32),
        ],
        compiler_params=pltpu.CompilerParams(vmem_limit_bytes=VLIM),
        cost_estimate=pl.CostEstimate(flops=8_000_000_000, bytes_accessed=9_000_000, transcendentals=0),
        name="tap_gradient",
    )(chunks, prow, bseg, window, d_conv, small)
REACH = 1536
SPAN = ROWS + 2 * REACH
QT, KT = 128, 1664
NEAR = REACH - ROWS
NEG = -1e30


def segment_count(ends, positions):
    return jnp.sum((ends[None, :] <= positions[:, None]).astype(i32), axis=1).astype(i32)

def attention_plan(starts, ends, first, odd):
    w = first - REACH + jnp.arange(SPAN, dtype=i32)
    kseg = segment_count(ends, w)
    kseg = jnp.where(w < 0, -1, kseg)
    qseg = kseg[REACH : REACH + ROWS]
    edge = qseg.reshape(ROWS // QT, QT)
    n = jnp.arange(starts.shape[0], dtype=i32)
    head = jnp.sum(jnp.where(n[None] == edge[:, :1], starts[None], 0), axis=1) - (first - REACH)
    tail = jnp.sum(jnp.where(n[None] == edge[:, -1:], ends[None], 0), axis=1) - (first - REACH)
    lo = jnp.clip(head // 128, 0, SPAN // 128)
    hi = jnp.clip((tail + 127) // 128, 1, SPAN // 128)
    tiles = jnp.maximum((hi - lo + KT // 128 - 1) // (KT // 128), 1)
    lo = jnp.minimum(lo, SPAN // 128 - tiles * (KT // 128))
    return (
        jnp.stack([lo, tiles, jnp.full_like(lo, odd)]).astype(i32),
        jnp.broadcast_to(qseg[None], (8, ROWS)),
        jnp.broadcast_to(kseg[:, None], (SPAN, 128)),
    )

def split_heads(a):
    low = iota(a.shape, 1) < 64
    zero = jnp.zeros((), a.dtype)
    return jnp.where(low, a, zero), jnp.where(low, zero, a)

def spots(range_ref):
    odd = range_ref[2, 0] == 1
    right, end = REACH + ROWS, SPAN - NEAR
    at = [
        jnp.where(odd, NEAR, right),
        jnp.where(odd, right, NEAR),
        jnp.where(odd, end, 0),
        jnp.where(odd, 0, end),
    ]
    return [pl.multiple_of(x, NEAR) for x in at]


def fill_span(range_ref, span_ref, own, others):
    span_ref[REACH : REACH + ROWS, :] = own[...]
    for at, piece in zip(spots(range_ref), others):
        span_ref[pl.ds(at, piece.shape[0]), :] = piece[...]


def flip_span(src_ref, dst_ref, lane):
    for at in range(0, SPAN, 512):
        dst_ref[:, at : at + 512] = src_ref[at : at + 512, lane : lane + 128].T


def same_segment(kseg_ref, qseg_ref, at):
    ks = kseg_ref[at, :]
    ks = jnp.concatenate([ks] * (QT // 128), axis=1) if QT > 128 else ks
    return ks == qseg_ref[0:1, :]


def forward_kernel(range_ref, qseg_ref, kseg_ref, q_ref, k0, k1, k2, k3, k4, o_ref, half_ref, lse_ref, span_ref, vt_ref):
    qi = pl.program_id(0)

    @pl.when(qi == 0)
    def _():
        fill_span(range_ref, span_ref, k0, (k1, k2, k3, k4))
        flip_span(span_ref, vt_ref, 128)

    qs = split_heads(q_ref[...])

    first, count = range_ref[0, qi], range_ref[1, qi]

    def tile(t, carry):
        at = pl.ds(pl.multiple_of((first + t * (KT // 128)) * 128, 128), KT)
        same = same_segment(kseg_ref, qseg_ref, at)
        k = span_ref[at, 0:128]
        out = []
        for e in range(2):
            m, l, acc = carry[e]
            s = lax.dot_general(k, qs[e], (((1,), (1,)), ((), ())), preferred_element_type=f32)
            s = jnp.where(same, s, NEG)
            new = jnp.maximum(m, jnp.max(s, axis=0, keepdims=True))
            p = jnp.exp(s - new)
            alpha = jnp.exp(m - new)
            l = l * alpha + jnp.sum(p, axis=0, keepdims=True)
            vt = vt_ref[64 * e : 64 * e + 64, at]
            acc = acc * alpha + jnp.dot(vt, p.astype(bf16), preferred_element_type=f32)
            out.append((new, l, acc))
        return tuple(out)

    start = (jnp.full((1, QT), NEG, f32), jnp.zeros((1, QT), f32), jnp.zeros((64, QT), f32))
    ends = lax.fori_loop(0, count, tile, (start, start))
    o = jnp.concatenate([acc / l for _, l, acc in ends], axis=0).T
    o_ref[...] = o
    half_ref[...] = o.astype(bf16)
    for e in range(2):
        lse_ref[e : e + 1, :] = ends[e][0] + jnp.log(ends[e][1])


def piece_specs(h, pieces):
    at = [h - (PAIRS - p.shape[1] // 256) if p.shape[1] > 256 else 0 for p in pieces]
    return [pl.BlockSpec((p.shape[0], 256), lambda i, c=c: (0, c)) for p, c in zip(pieces, at)]


def attend(plan, h, q, pieces):
    ranges, qseg, kseg = plan
    return pl.pallas_call(
        forward_kernel,
        grid=(ROWS // QT,),
        out_shape=(
            jax.ShapeDtypeStruct((ROWS, 128), f32),
            jax.ShapeDtypeStruct((ROWS, 128), bf16),
            jax.ShapeDtypeStruct((8, ROWS), f32),
        ),
        in_specs=[
            pl.BlockSpec(memory_space=pltpu.SMEM),
            pl.BlockSpec((8, QT), lambda i: (0, i)),
            pl.BlockSpec((SPAN, 128), lambda i: (0, 0)),
            pl.BlockSpec((QT, 128), lambda i: (i, h)),
        ]
        + piece_specs(h, pieces),
        out_specs=(
            pl.BlockSpec((QT, 128), lambda i: (i, 0)),
            pl.BlockSpec((QT, 128), lambda i: (i, 0)),
            pl.BlockSpec((8, QT), lambda i: (0, i)),
        ),
        scratch_shapes=[pltpu.VMEM((SPAN, 256), bf16), pltpu.VMEM((128, SPAN), bf16)],
        compiler_params=pltpu.CompilerParams(vmem_limit_bytes=VLIM),
        cost_estimate=pl.CostEstimate(flops=8_000_000_000, bytes_accessed=8_000_000, transcendentals=0),
        name="attention_forward",
    )(ranges, qseg, kseg, q, *pieces)


def backward_kernel(range_ref, qseg_ref, kseg_ref, q_ref, k0, k1, k2, k3, k4, do_ref, o_ref, lse_ref,
                    dq_ref, own_ref, f1, f2, f3, f4, span_ref, kt_ref, dkv_ref):
    qi = pl.program_id(0)
    last = ROWS // QT - 1

    @pl.when(qi == 0)
    def _():
        dkv_ref[...] = jnp.zeros_like(dkv_ref)
        fill_span(range_ref, span_ref, k0, (k1, k2, k3, k4))
        flip_span(span_ref, kt_ref, 0)

    qs = split_heads(q_ref[...])
    dos = split_heads(do_ref[...])
    qcat = jnp.concatenate(qs, axis=0)
    docat = jnp.concatenate(dos, axis=0)
    dm = (do_ref[...].astype(f32) * o_ref[...]).T
    delta = [jnp.sum(dm[64 * e : 64 * e + 64], axis=0, keepdims=True) for e in range(2)]

    first, count = range_ref[0, qi], range_ref[1, qi]

    def tile(t, carry):
        at = pl.ds(pl.multiple_of((first + t * (KT // 128)) * 128, 128), KT)
        same = same_segment(kseg_ref, qseg_ref, at)
        k = span_ref[at, 0:128]
        v = span_ref[at, 128:256]
        ps, dss, out = [], [], []
        for e in range(2):
            dims = (((1,), (1,)), ((), ()))
            s = lax.dot_general(k, qs[e], dims, preferred_element_type=f32)
            p = jnp.exp(jnp.where(same, s - lse_ref[e : e + 1, :], NEG))
            dp = lax.dot_general(v, dos[e], dims, preferred_element_type=f32)
            ds = (p * (dp - delta[e])).astype(bf16)
            kt = kt_ref[64 * e : 64 * e + 64, at]
            out.append(carry[e] + jnp.dot(kt, ds, preferred_element_type=f32))
            ps.append(p.astype(bf16))
            dss.append(ds)
        dkv_ref[at, 0:128] += jnp.dot(jnp.concatenate(dss, axis=1), qcat, preferred_element_type=f32)
        dkv_ref[at, 128:256] += jnp.dot(jnp.concatenate(ps, axis=1), docat, preferred_element_type=f32)
        return tuple(out)

    zero = jnp.zeros((64, QT), f32)
    dqt = lax.fori_loop(0, count, tile, (zero, zero))
    dq = jnp.concatenate(dqt, axis=0).T
    dq_ref[...] = dq.astype(bf16) * jnp.asarray(0.125, bf16)

    @pl.when(qi == last)
    def _():
        for at, far in zip(spots(range_ref), (f1, f2, f3, f4)):
            far[...] = dkv_ref[pl.ds(at, far.shape[0]), :].astype(bf16)
        own_ref[...] = dkv_ref[REACH : REACH + ROWS, :]


def attend_back(plan, h, q, pieces, d_att, mixed, lse):
    ranges, qseg, kseg = plan
    rowspec = pl.BlockSpec((QT, 128), lambda i: (i, 0))
    colspec = pl.BlockSpec((QT, 128), lambda i: (i, h))
    return pl.pallas_call(
        backward_kernel,
        grid=(ROWS // QT,),
        out_shape=(
            jax.ShapeDtypeStruct((ROWS, 128), bf16),
            jax.ShapeDtypeStruct((ROWS, 256), f32),
        )
        + tuple(jax.ShapeDtypeStruct((n, 256), bf16) for n in (ROWS, ROWS, NEAR, NEAR)),
        in_specs=[
            pl.BlockSpec(memory_space=pltpu.SMEM),
            pl.BlockSpec((8, QT), lambda i: (0, i)),
            pl.BlockSpec((SPAN, 128), lambda i: (0, 0)),
            colspec,
        ]
        + piece_specs(h, pieces)
        + [colspec, rowspec, pl.BlockSpec((8, QT), lambda i: (0, i))],
        out_specs=(
            rowspec,
            pl.BlockSpec((ROWS, 256), lambda i: (0, 0)),
        )
        + tuple(pl.BlockSpec((n, 256), lambda i: (0, 0)) for n in (ROWS, ROWS, NEAR, NEAR)),
        scratch_shapes=[
            pltpu.VMEM((SPAN, 256), bf16),
            pltpu.VMEM((128, SPAN), bf16),
            pltpu.VMEM((SPAN, 256), f32),
        ],
        compiler_params=pltpu.CompilerParams(vmem_limit_bytes=VLIM),
        cost_estimate=pl.CostEstimate(flops=8_000_000_000, bytes_accessed=12_000_000, transcendentals=0),
        name="attention_backward",
    )(ranges, qseg, kseg, q, *pieces, d_att, mixed, lse)


def exchange(part):
    return lax.ppermute(part, "heads", [(0, 1), (1, 0)])


def pair_sum(part):
    half = part.astype(bf16)
    return half.astype(f32) + exchange(half).astype(f32)


def side_by_side(own, other, index):
    return jnp.where(
        index == 0,
        jnp.concatenate([own, other], axis=1),
        jnp.concatenate([other, own], axis=1),
    )


def passed(block, distance):
    count = lax.axis_size("seq")
    route = [(i - distance, i) for i in range(count) if 0 <= i - distance < count]
    return lax.ppermute(block, "seq", route)


def across_cores(block):
    return lax.ppermute(block, "seq", [(i, i ^ 1) for i in range(lax.axis_size("seq"))])


def across_chips(block):
    count = lax.axis_size("seq")
    route = [(i, i + 1 if i % 2 else i - 1) for i in range(count)]
    return lax.ppermute(block, "seq", [(i, j) for i, j in route if 0 <= j < count])


def chip_along(block, step):
    count = lax.axis_size("seq")
    route = [(i, i - 2 * step if i % 2 else i + 2 * step) for i in range(count)]
    return lax.ppermute(block, "seq", [(i, j) for i, j in route if 0 <= j < count])


def layer_norm(values, gain, shift):
    centered = values - jnp.mean(values, axis=-1, keepdims=True)
    scale = lax.rsqrt(jnp.mean(centered * centered, axis=-1, keepdims=True) + EPSILON)
    return centered * scale * gain + shift


def gelu_exact(values):
    return jax.nn.gelu(values, approximate=False)


def nesterov(weight, grad, moment, average, rate):
    moment_new = 0.5 * moment + grad
    weight_new = weight - rate * (grad + 0.5 * moment_new)
    average_new = 0.5 * average + 0.5 * weight_new
    return (grad, weight_new, moment_new, average_new, weight_new.astype(bf16))


def dot(a, b, ca, cb):
    return lax.dot_general(a, b, (((ca,), (cb,)), ((), ())), preferred_element_type=f32)


def gathered(shard):
    return lax.all_gather(shard, "seq", axis=0, tiled=True)


def scattered(whole_sum):
    return lax.psum_scatter(whole_sum, "seq", scatter_dimension=0, tiled=True)


def body(
    frames,
    cotangent,
    lengths,
    kernel,
    kernel_moment,
    kernel_average,
    project,
    project_moment,
    project_average,
    combine,
    combine_moment,
    combine_average,
    expand,
    expand_moment,
    expand_average,
    shrink,
    shrink_moment,
    shrink_average,
    unitbias,
    unitbias_moment,
    unitbias_average,
    chanbias,
    chanbias_moment,
    chanbias_average,
    outbias,
    outbias_moment,
    outbias_average,
    normparams,
    normparams_moment,
    normparams_average,
):
    devices = lax.axis_size("seq")
    rows, width = frames.shape
    total = devices * rows
    first = lax.axis_index("seq") * rows
    index = lax.axis_index("heads")
    odd = lax.axis_index("seq") % 2
    local = project.shape[0]
    hidden_units = expand.shape[1]

    w_kernel = gathered(jnp.transpose(kernel, (2, 1, 0)).astype(bf16))
    small = jnp.concatenate(
        [unitbias, chanbias.reshape(-1), outbias.reshape(-1), normparams.reshape(-1)]
    ).astype(bf16)
    w_small = gathered(small[None])
    w_first = gathered(
        jnp.concatenate(
            [project[:, 0]]
            + [project[:, c, 128 * h : 128 * h + 128] for h in range(PAIRS) for c in (1, 2)]
            + [combine.T],
            axis=1,
        ).astype(bf16)
    )
    w_second = gathered(jnp.concatenate([expand, shrink.T], axis=1).astype(bf16))
    w_combine = w_first[:, 3 * HALF :]
    w_combine_far = exchange(w_combine)
    cuts = [unitbias.size, chanbias.size, outbias.size, normparams.size]
    parts, at = [], 0
    for size in cuts:
        parts.append(w_small[:, at : at + size].astype(f32))
        at += size
    b_unit = parts[0].reshape(-1)
    b_chan = jnp.transpose(parts[1].reshape(devices, 3, -1), (1, 0, 2)).reshape(3, -1)
    b_out = jnp.transpose(parts[2].reshape(devices, 2, -1), (1, 0, 2)).reshape(2, -1)
    norms = jnp.transpose(parts[3].reshape(devices, 3, 2, -1), (1, 2, 0, 3)).reshape(3, 2, -1)

    count = lengths.shape[0]
    order = jnp.arange(count, dtype=i32)
    ends = jnp.sum(jnp.where(order[None, :] <= order[:, None], lengths[None, :], 0), axis=1).astype(i32)
    starts = ends - lengths
    plan = block_plan(starts, ends, first)
    reach = attention_plan(starts, ends, first, odd)

    x_half = lax.dynamic_slice_in_dim(frames, index * HALF, HALF, 1).astype(bf16)
    window = jnp.concatenate(
        [passed(x_half[rows - HALO :], 1), x_half, passed(x_half[:HALO], -1)], axis=0
    )
    pre = conv(plan, window, w_kernel, False) + b_chan[0]
    spread_part = gelu_exact(pre).astype(bf16)
    spread = side_by_side(spread_part, exchange(spread_part), index)
    h1, norm0_back = jax.vjp(layer_norm, frames + spread.astype(f32), norms[0, 0], norms[0, 1])
    h1_half = h1.astype(bf16)
    proj = dot(h1_half, w_first[:, : 3 * HALF], 1, 0)
    scale = HEAD ** (-0.5)
    queries = ((proj[:, :HALF] + b_chan[1]) * scale).astype(bf16)
    kv_bias = b_chan[2].reshape(PAIRS, 1, 128)
    kv_bias = jnp.concatenate([jnp.zeros_like(kv_bias), kv_bias], axis=1).reshape(-1)
    both = (proj[:, HALF:] + kv_bias).astype(bf16)
    near = NEAR

    def fetched(lo, hi):
        block = both[:, lo:hi]
        head, tail = block[:near], block[rows - near :]
        return (
            across_cores(block),
            across_chips(block),
            chip_along(jnp.where(odd == 1, head, tail), 1),
            chip_along(jnp.where(odd == 1, tail, head), -1),
        )

    early = fetched(0, 256)
    both, early = lax.optimization_barrier((both, early))
    late = fetched(256, 256 * PAIRS)
    pieces = [(both,) + (early if h == 0 else late) for h in range(PAIRS)]
    mixed, attended, attended_far, lse = [], [], [], []
    for h in range(PAIRS):
        if h == 0:
            q_part, w_combine_far = lax.optimization_barrier((queries, w_combine_far))
        if h >= 2:
            q_part, attended_far[h - 2] = lax.optimization_barrier((queries, attended_far[h - 2]))
        mixed_part, half, lse_part = attend(reach, h, q_part, pieces[h])
        mixed.append(mixed_part)
        lse.append(lse_part)
        attended.append(half)
        attended_far.append(exchange(half))
    attended = jnp.concatenate(attended, axis=1)
    attended_all = side_by_side(attended, jnp.concatenate(attended_far, axis=1), index)
    w_combine_all = side_by_side(w_combine, w_combine_far, index)
    w_expand = w_second[:, :hidden_units]
    w_shrink = w_second[:, hidden_units:]
    step = rows // CHUNKS
    cuts_of = [slice(c * step, (c + 1) * step) for c in range(CHUNKS)]
    first_half, second_half = [], []
    for cut in cuts_of:
        branch = dot(attended_all[cut], w_combine_all, 1, 1)
        h2, norm1_back = jax.vjp(layer_norm, h1[cut] + branch + b_out[0], norms[1, 0], norms[1, 1])
        h2_half = h2.astype(bf16)
        inner = dot(h2_half, w_expand, 1, 0) + b_unit
        hidden, gelu_inner_back = jax.vjp(gelu_exact, inner)
        hidden_half = hidden.astype(bf16)
        sent = dot(hidden_half, w_shrink, 1, 1).astype(bf16)
        first_half.append((h2, norm1_back, h2_half, gelu_inner_back, hidden_half, sent, exchange(sent)))
    sent_back = None
    for cut, (h2, norm1_back, h2_half, gelu_inner_back, hidden_half, sent, came) in zip(
        cuts_of, first_half
    ):
        if sent_back is not None:
            came, _ = lax.optimization_barrier((came, sent_back))
        outer = sent.astype(f32) + came.astype(f32)
        out_part, norm2_back = jax.vjp(layer_norm, h2 + outer + b_out[1], norms[2, 0], norms[2, 1])
        dx3, gain2_grad, shift2_grad = norm2_back(cotangent[cut])
        d_out = dx3.astype(bf16)
        d_hidden = dot(d_out, w_shrink, 1, 0)
        d_inner = gelu_inner_back(d_hidden)[0]
        d_inner_half = d_inner.astype(bf16)
        sent_back = dot(d_inner_half, w_expand, 1, 1).astype(bf16)
        sums = [gain2_grad, shift2_grad, jnp.sum(dx3, axis=0), jnp.sum(d_inner, axis=0)]
        second_half.append(
            [out_part, (sent_back, exchange(sent_back)), norm1_back, h2_half, d_inner_half, d_out, hidden_half, dx3, sums]
        )
    layer_out = jnp.concatenate([part[0] for part in second_half], axis=0)
    gain2_grad, shift2_grad, outer_bias_grad, unit_grad = map(sum, zip(*[p[-1] for p in second_half]))
    second_part = jnp.concatenate(
        [
            sum(dot(p[a], p[b], 0, 0) for p in second_half).astype(bf16)
            for a, b in ((3, 4), (5, 6))
        ],
        axis=1,
    )
    dx2_parts, gain1_parts, shift1_parts = zip(
        *[p[2](p[7] + (p[1][0].astype(f32) + p[1][1].astype(f32))) for p in second_half]
    )
    gain1_grad, shift1_grad = sum(gain1_parts), sum(shift1_parts)
    dx2 = jnp.concatenate(dx2_parts, axis=0)
    branch_bias_grad = jnp.sum(dx2, axis=0)
    d_branch = dx2.astype(bf16)
    d_att = dot(d_branch, w_combine, 1, 0).astype(bf16)
    d_att, second_part = lax.optimization_barrier((d_att, second_part))
    second_sum = scattered(second_part).astype(f32)
    dq_parts, kv_parts = [], []
    arrived = {}
    for h in range(PAIRS):
        d_part = d_att
        if h >= 2:
            d_part, arrived[h - 2] = lax.optimization_barrier((d_att, arrived[h - 2]))
        dq_part, own, core, chip, far, beyond = attend_back(
            reach, h, queries, pieces[h], d_part, mixed[h], lse[h]
        )
        arrived[h] = (
            across_cores(core),
            across_chips(chip),
            chip_along(far, -1),
            chip_along(beyond, 1),
            own,
        )
        dq_parts.append(dq_part)
    for h in range(PAIRS):
        core, chip, far, beyond, own = [a.astype(f32) for a in arrived[h]]
        ends_of = jnp.concatenate(
            [jnp.where(odd == 1, far, beyond), jnp.where(odd == 1, beyond, far)], axis=0
        )
        kv_parts.append((own + core + chip + ends_of).astype(bf16))
    dq_half = jnp.concatenate(dq_parts, axis=1)
    d_both_half = jnp.concatenate(kv_parts, axis=1)
    stacked = jnp.concatenate([dq_half, d_both_half], axis=1)
    query_bias_grad = jnp.sum(dq_half.astype(f32), axis=0)
    value_bias_grad = jnp.sum(
        d_both_half.astype(f32), axis=0
    ).reshape(PAIRS, 2, 128)[:, 1].reshape(-1)
    dh1 = dx2 + pair_sum(dot(stacked, w_first[:, : 3 * HALF], 1, 1))
    first_part = (
        jnp.concatenate(
            [dot(h1_half, stacked, 0, 0).astype(bf16), dot(d_branch, attended, 0, 0).astype(bf16)],
            axis=1,
        )
    )
    first_part, second_sum = lax.optimization_barrier((first_part, second_sum))
    first_sum = scattered(first_part).astype(f32)
    dx1, gain0_grad, shift0_grad = norm0_back(dh1)
    d_spread = lax.dynamic_slice_in_dim(dx1, index * HALF, HALF, 1)
    d_conv = jax.vjp(gelu_exact, pre)[1](d_spread)[0]
    conv_bias_grad = jnp.sum(d_conv, axis=0)
    d_conv_half = d_conv.astype(bf16)
    spread_out = lambda grad, lead: jnp.transpose(
        grad.reshape(lead, devices, -1), (1, 0, 2)
    ).reshape(devices, -1)
    small_part = jnp.concatenate(
            [
                unit_grad.reshape(devices, -1),
                spread_out(jnp.stack([conv_bias_grad, query_bias_grad, value_bias_grad]), 3),
                spread_out(jnp.stack([branch_bias_grad, outer_bias_grad]), 2),
                spread_out(
                    jnp.stack(
                        [gain0_grad, shift0_grad, gain1_grad, shift1_grad, gain2_grad, shift2_grad]
                    ),
                    6,
                ),
            ],
            axis=1,
        )
    small_part = jnp.pad(small_part, ((0, 0), (0, EXTRA * HALF - small_part.shape[1])))
    small_part = small_part.astype(bf16).reshape(devices, EXTRA, HALF)
    tap_part = tap_grad(plan, window, d_conv_half, small_part)
    tap_part, first_sum = lax.optimization_barrier((tap_part, first_sum))
    tap_sum = scattered(tap_part)[0].astype(f32)
    kernel_sum = tap_sum[:-EXTRA].reshape(TAPS // devices, CG, HALF)
    small_sum = tap_sum[-EXTRA:].reshape(-1)
    d_window = jnp.concatenate(
        [passed(d_conv_half[rows - HALO :], 1), d_conv_half, passed(d_conv_half[:HALO], -1)], axis=0
    )
    d_input = conv(plan, d_window, w_kernel, True).astype(bf16)
    frames_grad = dx1 + side_by_side(d_input, exchange(d_input), index).astype(f32)

    pieces, at = [], 0
    for size in cuts:
        pieces.append(small_sum[at : at + size])
        at += size
    unit_sum = pieces[0]
    chan_sum = pieces[1].reshape(chanbias.shape)
    out_sum = pieces[2].reshape(outbias.shape)
    norm_sum = pieces[3].reshape(normparams.shape)
    kv_sum = first_sum[:, HALF : 3 * HALF].reshape(local, PAIRS, 2, 128)
    project_sum = jnp.stack(
        [first_sum[:, :HALF]] + [kv_sum[:, :, c].reshape(local, HALF) for c in range(2)], axis=1
    )

    root = total**0.5
    small_rate = 0.1 / root
    out = [layer_out, frames_grad]
    for weight, grad, moment, average, rate in (
        (kernel, jnp.transpose(kernel_sum, (2, 1, 0)), kernel_moment, kernel_average, (CG * TAPS) ** (-0.5) / root),
        (project, project_sum, project_moment, project_average, width ** (-0.5) / root),
        (combine, first_sum[:, 3 * HALF :].T, combine_moment, combine_average, (width // 16) ** (-0.5) / root),
        (expand, second_sum[:, :hidden_units], expand_moment, expand_average, width ** (-0.5) / root),
        (shrink, second_sum[:, hidden_units:].T, shrink_moment, shrink_average, (2 * hidden_units) ** (-0.5) / root),
        (unitbias, unit_sum, unitbias_moment, unitbias_average, 0.5 / root),
        (chanbias, chan_sum, chanbias_moment, chanbias_average, small_rate),
        (outbias, out_sum, outbias_moment, outbias_average, small_rate),
        (normparams, norm_sum, normparams_moment, normparams_average, small_rate),
    ):
        out.extend(nesterov(weight, grad, moment, average, rate))
    return tuple(out)


def solution(mesh):
    kernel_spec = P("heads", None, "seq")
    project_spec = P("seq", None, "heads")
    tall = P("heads", "seq")
    wide = P("seq", "heads")
    unit = P(("heads", "seq"))
    chan = P(None, ("heads", "seq"))
    outb = P(None, "seq")
    norm = P(None, None, "seq")
    weights = (kernel_spec, project_spec, tall, wide, tall, unit, chan, outb, norm)
    rows = P("seq", None)
    return jax.shard_map(
        body,
        mesh=mesh,
        in_specs=(rows, rows, P()) + tuple(s for s in weights for _ in range(3)),
        out_specs=(rows, rows) + tuple(s for s in weights for _ in range(5)),
        check_vma=False,
    )
```

```python
import functools

import jax
import jax.numpy as jnp
from jax import lax
from jax.experimental import pallas as pl
from jax.experimental.pallas import tpu as pltpu
from jax.sharding import PartitionSpec as P

HEAD = 64
PAIRS = 3
CHUNKS = 2
EPSILON = 1e-05

bf16, f32, i32 = jnp.bfloat16, jnp.float32, jnp.int32
CG, TAPS, GROUPS, HALO = 48, 128, 8, 64
ROWS, WIN, HALF = 1024, 1152, 384
CM, XM = 272, 304
NQ = 33
PJ = 134
EXTRA = 16
VLIM = 58 << 20


def iota(shape, dim):
    return lax.broadcasted_iota(i32, shape, dim)


def block_plan(starts, ends, first):
    w0 = first - HALO
    b = jnp.clip(starts - w0, 0, WIN)
    e = jnp.clip(ends - w0, 0, WIN)
    nblk = (e - b + 3) // 4
    n = starts.shape[0]
    before = jnp.arange(n)[None, :] < jnp.arange(n)[:, None]
    bs = jnp.sum(jnp.where(before, nblk[None, :], 0), axis=1).astype(i32)
    bs = bs + (jnp.clip(-w0, 0, WIN) + 3) // 4
    w = jnp.arange(WIN, dtype=i32)
    inside = (b[None, :] <= w[:, None]) & (w[:, None] < e[None, :])
    p = jnp.sum(jnp.where(inside, 4 * bs - b + w[:, None] + 1, 0), axis=1).astype(i32) - 1
    most = min(WIN, WIN // 4 + n)
    maxc = -((16 - most) // CM)
    lcap = CM * (maxc - 1) + XM
    m = jnp.arange(lcap, dtype=i32)
    hit = (bs[None, :] <= m[:, None]) & (m[:, None] < (bs + nblk)[None, :])
    bseg = jnp.sum(jnp.where(hit, jnp.arange(1, n + 1, dtype=i32)[None, :], 0), axis=1).astype(i32) - 1
    chunks = jnp.maximum((p[HALO + ROWS - 1] // 4 - 16) // CM + 1, 1)
    return (
        jnp.reshape(chunks, (1,)).astype(i32),
        jnp.broadcast_to(p[None, :], (8, WIN)),
        jnp.broadcast_to(p[:, None], (WIN, 128)),
        jnp.broadcast_to(bseg[:, None], (lcap, 128)),
    )


def select_pair(h, rows, base):
    lane = iota((rows, 256), 1)
    src = CG * (2 * h + (lane >> 7)) + (lane & 63) - base
    ok = ((lane & 63) < CG) & (iota((rows, 256), 0) == src)
    return jnp.where(ok, 1.0, 0.0).astype(bf16)


def build_blocks(s_ref, dup):
    y = [jnp.dot(s_ref[0, t], dup, preferred_element_type=f32).astype(bf16) for t in range(4)]
    low = iota((XM, 128), 1) < 64
    out = []
    for g in range(2):
        tiles = [v[:, 128 * g : 128 * g + 128] for v in y]
        out.append(
            jnp.concatenate(
                [jnp.where(low, tiles[0], tiles[1]), jnp.where(low, tiles[2], tiles[3])], axis=1
            )
        )
    return out


def build_taps(k_ref, sel, p_ref, base_tile):
    p_ref[...] = jnp.zeros_like(p_ref)
    step = 16
    for j0 in range(0, TAPS, step):
        part = k_ref[pl.ds(j0, step), :, pl.ds(pl.multiple_of(base_tile * 128, 128), 256)]
        d = jnp.dot(part.reshape(step * CG, 256), sel, preferred_element_type=f32)
        d = d.astype(bf16).reshape(step, CG, 256)
        for g in range(2):
            p_ref[g, pl.ds(j0 + 2, step), 0:CG, 0:64] = d[:, :, 128 * g : 128 * g + 64]
            p_ref[g, pl.ds(j0 + 3, step), 0:CG, 64:128] = d[:, :, 128 * g + 64 : 128 * g + 128]


def pair_lanes(h):
    base_tile = h >> 1
    return base_tile, pl.ds(pl.multiple_of(base_tile * 128, 128), 256)


def prepare_kernel(n_ref, *refs):
    @pl.when(pl.program_id(0) < n_ref[0])
    def _():
        prepare_chunk(pl.program_id(0), *refs)


def prepare_chunk(c, prow_ref, pcol_ref, bseg_ref, x_ref, s_ref, r_ref, mask_ref, tmask_ref, xb_ref, xt_ref):
    prow = prow_ref[0:1, :]
    for t in range(4):
        pos = 4 * (iota((XM, WIN), 0) + CM * c) + t
        s_ref[0, t] = jnp.where(pos == prow, 1.0, 0.0).astype(bf16)
    pcol = pcol_ref[HALO : HALO + ROWS, :]
    lane = iota((ROWS, 4 * CM), 1)
    phase = sum([(lane >= CM * t).astype(i32) for t in range(1, 4)])
    spot = 4 * (16 + CM * c) + 4 * lane - (4 * CM - 1) * phase
    wide = jnp.concatenate([pcol] * 9, axis=1)[:, : 4 * CM]
    r_ref[0] = jnp.where(wide == spot, 1.0, 0.0).astype(bf16)
    seg = bseg_ref[pl.ds(pl.multiple_of(CM * c, 16), XM), :]
    none = jnp.full((32, 128), -7, i32)
    own = jnp.concatenate([none, seg[16 : 16 + CM], none], axis=0)
    for q in range(NQ):
        same = seg[q : q + CM] == seg[16 : 16 + CM]
        mask_ref[0, q] = jnp.where(same, 1.0, 0.0).astype(bf16)
        same = seg == own[32 - q : 32 - q + XM]
        tmask_ref[0, q] = jnp.where(same, 1.0, 0.0).astype(bf16)
    for h in range(4):
        base = 128 * (h // 2)
        sel = select_pair(h, 256, base)
        dup = jnp.dot(x_ref[:, base : base + 256], sel, preferred_element_type=f32).astype(bf16)
        for g, block in enumerate(build_blocks(s_ref, dup)):
            xb_ref[0, 2 * h + g] = block
            xt_ref[0, 2 * h + g] = block.T


def fixed(shape):
    return pl.BlockSpec(shape, lambda *_: (0,) * len(shape))


def chunk_count(plan):
    return (plan[3].shape[0] - XM) // CM + 1


def call(kernel, name, grid, plan, in_specs, out_specs, out_shape, scratch, flops, args):
    return pl.pallas_call(
        kernel,
        grid_spec=pltpu.PrefetchScalarGridSpec(
            num_scalar_prefetch=1,
            grid=grid,
            in_specs=in_specs,
            out_specs=out_specs,
            scratch_shapes=scratch,
        ),
        out_shape=out_shape,
        compiler_params=pltpu.CompilerParams(vmem_limit_bytes=VLIM),
        cost_estimate=pl.CostEstimate(flops=flops, bytes_accessed=15_000_000, transcendentals=0),
        name=name,
    )(plan[0], *args)


def prepare(plan, window):
    chunks, prow, pcol, bseg = plan
    shapes = ((4, XM, WIN), (ROWS, 4 * CM), (NQ, CM, 128), (NQ, XM, 128), (8, XM, 256), (8, 256, XM))
    maxc = chunk_count(plan)
    return call(
        prepare_kernel,
        "conv_prepare",
        (maxc,),
        plan,
        [fixed(a.shape) for a in (prow, pcol, bseg, window)],
        tuple(
            pl.BlockSpec((1,) + s, lambda c, n, k=len(s): (jnp.minimum(c, n[0] - 1),) + (0,) * k)
            for s in shapes
        ),
        tuple(jax.ShapeDtypeStruct((maxc,) + s, bf16) for s in shapes),
        [],
        10_000_000_000,
        (prow, pcol, bseg, window),
    )


def conv_forward_kernel(n_ref, *refs):
    c, h = pl.program_id(0), pl.program_id(1)

    @pl.when(c < n_ref[0])
    def _():
        conv_chunk(False, c, h, *refs)


def conv_back_kernel(n_ref, d_ref, s_ref, *refs):
    c, h = pl.program_id(0), pl.program_id(1)

    @pl.when(c < n_ref[0])
    def _():
        conv_chunk(True, c, h, (d_ref, s_ref), *refs)


def conv_chunk(back, c, h, x_ref, mask_ref, r_ref, k_ref, out_ref, *rest):
    base_tile, lanes = pair_lanes(h)
    if back:
        s_ref, (xb_ref, o_ref) = x_ref[1], rest
        p_ref = k_ref
        sel = select_pair(h, 256, 128 * base_tile)
        dup = jnp.dot(x_ref[0][:, lanes], sel, preferred_element_type=f32).astype(bf16)
        for g, block in enumerate(build_blocks(s_ref, dup)):
            xb_ref[0, g] = block
    else:
        xb_ref = x_ref
        p_ref, o_ref = rest
        build_taps(k_ref, select_pair(h, 256, 128 * base_tile), p_ref, base_tile)

    @pl.when(h == 0)
    def _():
        o_ref[...] = jnp.zeros_like(o_ref)

    total = [jnp.zeros((CM, 256), f32) for _ in range(4)]
    for g in range(2):
        acc = jnp.zeros((CM, 256), f32)
        for q in range(NQ):
            m = mask_ref[0, q]
            xs = xb_ref[0, g, q : q + CM, :] * jnp.concatenate([m, m], axis=1)
            if back:
                a, b = 130 - 4 * q, 128 - 4 * q
            else:
                a, b = 4 * q + 2, 4 * q
            w = jnp.concatenate(
                [p_ref[g, a : a + 4].reshape(256, 128), p_ref[g, b : b + 4].reshape(256, 128)],
                axis=1,
            )
            dims = (((1,), (1 if back else 0,)), ((), ()))
            acc = acc + lax.dot_general(xs, w, dims, preferred_element_type=f32)
        acc = acc.astype(bf16)
        row = iota((256, 256), 0)
        target = CG * (2 * h + g) - 128 * base_tile + (row & 63)
        hit = ((row & 63) < CG) & (iota((256, 256), 1) == target)
        for t in range(4):
            fold = jnp.where(hit & ((row >> 6) == t), 1.0, 0.0).astype(bf16)
            total[t] = total[t] + jnp.dot(acc, fold, preferred_element_type=f32)
    for t in range(4):
        o_ref[CM * t : CM * t + CM, lanes] += total[t].astype(bf16)

    @pl.when(h == 3)
    def _():
        y = jnp.dot(r_ref[0], o_ref[...], preferred_element_type=f32)

        @pl.when(c == 0)
        def _():
            out_ref[...] = y

        @pl.when(c > 0)
        def _():
            out_ref[...] += y


def by_chunk(shape):
    return pl.BlockSpec(
        (1,) + shape, lambda c, h, n: (jnp.minimum(c, n[0] - 1),) + (0,) * len(shape)
    )


def by_pair(shape):
    return pl.BlockSpec(
        (2,) + shape, lambda c, h, n: (jnp.where(c < n[0], h, 3),) + (0,) * len(shape)
    )


def conv(plan, ready, taps):
    _, r, mask, _, xb, _ = ready
    x_spec = pl.BlockSpec(
        (1, 2, XM, 256),
        lambda c, h, n: (jnp.minimum(c, n[0] - 1), jnp.where(c < n[0], h, 3), 0, 0),
    )
    return call(
        conv_forward_kernel,
        "conv_forward",
        (chunk_count(plan), 4),
        plan,
        [x_spec, by_chunk((NQ, CM, 128)), by_chunk((ROWS, 4 * CM)), fixed((TAPS, CG, HALF))],
        (fixed((ROWS, HALF)), by_pair((PJ, 64, 128))),
        (
            jax.ShapeDtypeStruct((ROWS, HALF), f32),
            jax.ShapeDtypeStruct((8, PJ, 64, 128), bf16),
        ),
        [pltpu.VMEM((4 * CM, HALF), bf16)],
        25_000_000_000,
        (xb, mask, r, taps),
    )


def conv_back(plan, ready, window, spread_taps):
    s, r, mask, _, _, _ = ready
    return call(
        conv_back_kernel,
        "conv_back",
        (chunk_count(plan), 4),
        plan,
        [
            fixed((WIN, HALF)),
            by_chunk((4, XM, WIN)),
            by_chunk((NQ, CM, 128)),
            by_chunk((ROWS, 4 * CM)),
            by_pair((PJ, 64, 128)),
        ],
        fixed((ROWS, HALF)),
        jax.ShapeDtypeStruct((ROWS, HALF), f32),
        [pltpu.VMEM((1, 2, XM, 256), bf16), pltpu.VMEM((4 * CM, HALF), bf16)],
        25_000_000_000,
        (window, s, mask, r, spread_taps),
    )


def tap_grad_kernel(n_ref, xt_ref, s_ref, mask_ref, d_ref, small_ref, out_ref, dp_ref, acc_ref):
    h, c = pl.program_id(0), pl.program_id(1)
    base_tile, lanes = pair_lanes(h)

    @pl.when((h == 0) & (c == 0))
    def _():
        out_ref[...] = jnp.zeros_like(out_ref)
        out_ref[:, out_ref.shape[1] - EXTRA :, :] = small_ref[...]
        dp_ref[...] = jnp.zeros_like(dp_ref)

    @pl.when(c == 0)
    def _():
        acc_ref[...] = jnp.zeros_like(acc_ref)

    @pl.when(c < n_ref[0])
    def _():
        sel = select_pair(h, 256, 128 * base_tile)
        ddup = jnp.dot(d_ref[:, lanes], sel, preferred_element_type=f32).astype(bf16)
        for g, block in enumerate(build_blocks(s_ref, ddup)):
            dp_ref[g, 32 : 32 + CM, :] = block[16 : 16 + CM]
        for g in range(2):
            for q in range(NQ):
                m = mask_ref[0, q]
                ds = dp_ref[g, 32 - q : 32 - q + XM, :] * jnp.concatenate([m, m], axis=1)
                part = jnp.dot(xt_ref[0, g], ds, preferred_element_type=f32)
                acc_ref[g, 4 * q + 2 : 4 * q + 6] += part[:, 0:128].reshape(4, 64, 128)
                acc_ref[g, 4 * q : 4 * q + 4] += part[:, 128:256].reshape(4, 64, 128)

    @pl.when(c == pl.num_programs(1) - 1)
    def _():
        per = TAPS // out_ref.shape[0]
        low = iota((1, 1, 128), 2) < 64
        row = iota((128, 256), 0)
        src = CG * (2 * h + (row >> 6)) + (row & 63) - 128 * base_tile
        back = jnp.where(((row & 63) < CG) & (iota((128, 256), 1) == src), 1.0, 0.0).astype(bf16)
        step = 16
        for j0 in range(0, TAPS, step):
            now = [acc_ref[g, j0 + 2 : j0 + 2 + step, 0:CG, :] for g in range(2)]
            nxt = [acc_ref[g, j0 + 3 : j0 + 3 + step, 0:CG, :] for g in range(2)]
            here = jnp.where(low, now[0], nxt[1]).reshape(step * CG, 128)
            far = jnp.where(low, now[1], nxt[0]).reshape(step * CG, 128)
            both = (here + pltpu.roll(far, 64, 1)).astype(bf16)
            o = jnp.dot(both, back, preferred_element_type=f32).astype(bf16)
            o = o.reshape(step // per, per * CG, 256)
            out_ref[j0 // per : (j0 + step) // per, 0 : per * CG, lanes] += o


def tap_grad(plan, ready, d_own, small):
    s, _, _, tmask, _, xt = ready
    devices = small.shape[0]
    shape = (devices, TAPS // devices * CG + EXTRA, HALF)
    chunked = lambda sh: pl.BlockSpec(
        (1,) + sh, lambda h, c, n: (jnp.minimum(c, n[0] - 1),) + (0,) * len(sh)
    )
    x_spec = pl.BlockSpec((1, 2, 256, XM), lambda h, c, n: (jnp.minimum(c, n[0] - 1), h, 0, 0))
    return call(
        tap_grad_kernel,
        "tap_gradient",
        (4, chunk_count(plan)),
        plan,
        [
            x_spec,
            chunked((4, XM, WIN)),
            chunked((NQ, XM, 128)),
            fixed((WIN, HALF)),
            fixed(small.shape),
        ],
        fixed(shape),
        jax.ShapeDtypeStruct(shape, bf16),
        [
            pltpu.VMEM((2, 32 + CM + 32, 256), bf16),
            pltpu.VMEM((2, PJ, 64, 128), f32),
        ],
        1_000_000_000,
        (xt, s, tmask, d_own, small),
    )
REACH = 1536
SPAN = ROWS + 2 * REACH
QT, KT = 128, 1664
NEAR = REACH - ROWS
NEG = -1e30


def segment_count(ends, positions):
    return jnp.sum((ends[None, :] <= positions[:, None]).astype(i32), axis=1).astype(i32)

def attention_plan(starts, ends, first, odd):
    w = first - REACH + jnp.arange(SPAN, dtype=i32)
    kseg = segment_count(ends, w)
    kseg = jnp.where(w < 0, -1, kseg)
    qseg = kseg[REACH : REACH + ROWS]
    edge = qseg.reshape(ROWS // QT, QT)
    n = jnp.arange(starts.shape[0], dtype=i32)
    head = jnp.sum(jnp.where(n[None] == edge[:, :1], starts[None], 0), axis=1) - (first - REACH)
    tail = jnp.sum(jnp.where(n[None] == edge[:, -1:], ends[None], 0), axis=1) - (first - REACH)
    lo = jnp.clip(head // 128, 0, SPAN // 128)
    hi = jnp.clip((tail + 127) // 128, 1, SPAN // 128)
    tiles = jnp.maximum((hi - lo + KT // 128 - 1) // (KT // 128), 1)
    lo = jnp.minimum(lo, SPAN // 128 - tiles * (KT // 128))
    return (
        jnp.stack([lo, tiles, jnp.full_like(lo, odd)]).astype(i32),
        jnp.broadcast_to(qseg[None], (8, ROWS)),
        jnp.broadcast_to(kseg[:, None], (SPAN, 128)),
    )

def split_heads(a):
    low = iota(a.shape, 1) < 64
    zero = jnp.zeros((), a.dtype)
    return jnp.where(low, a, zero), jnp.where(low, zero, a)

def spots(range_ref):
    odd = range_ref[2, 0] == 1
    right, end = REACH + ROWS, SPAN - NEAR
    at = [
        jnp.where(odd, NEAR, right),
        jnp.where(odd, right, NEAR),
        jnp.where(odd, end, 0),
        jnp.where(odd, 0, end),
    ]
    return [pl.multiple_of(x, NEAR) for x in at]


def fill_span(range_ref, span_ref, own, others):
    span_ref[REACH : REACH + ROWS, :] = own[...]
    for at, piece in zip(spots(range_ref), others):
        span_ref[pl.ds(at, piece.shape[0]), :] = piece[...]


def flip_span(src_ref, dst_ref, lane):
    for at in range(0, SPAN, 512):
        dst_ref[:, at : at + 512] = src_ref[at : at + 512, lane : lane + 128].T


def same_segment(kseg_ref, qseg_ref, at):
    ks = kseg_ref[at, :]
    ks = jnp.concatenate([ks] * (QT // 128), axis=1) if QT > 128 else ks
    return ks == qseg_ref[0:1, :]


def forward_kernel(range_ref, qseg_ref, kseg_ref, q_ref, k0, k1, k2, k3, k4, o_ref, half_ref, lse_ref, span_ref, vt_ref):
    qi = pl.program_id(0)

    @pl.when(qi == 0)
    def _():
        fill_span(range_ref, span_ref, k0, (k1, k2, k3, k4))
        flip_span(span_ref, vt_ref, 128)

    qs = split_heads(q_ref[...])

    first, count = range_ref[0, qi], range_ref[1, qi]

    def tile(t, carry):
        at = pl.ds(pl.multiple_of((first + t * (KT // 128)) * 128, 128), KT)
        same = same_segment(kseg_ref, qseg_ref, at)
        k = span_ref[at, 0:128]
        out = []
        for e in range(2):
            m, l, acc = carry[e]
            s = lax.dot_general(k, qs[e], (((1,), (1,)), ((), ())), preferred_element_type=f32)
            s = jnp.where(same, s, NEG)
            new = jnp.maximum(m, jnp.max(s, axis=0, keepdims=True))
            p = jnp.exp(s - new)
            alpha = jnp.exp(m - new)
            l = l * alpha + jnp.sum(p, axis=0, keepdims=True)
            vt = vt_ref[64 * e : 64 * e + 64, at]
            acc = acc * alpha + jnp.dot(vt, p.astype(bf16), preferred_element_type=f32)
            out.append((new, l, acc))
        return tuple(out)

    start = (jnp.full((1, QT), NEG, f32), jnp.zeros((1, QT), f32), jnp.zeros((64, QT), f32))
    ends = lax.fori_loop(0, count, tile, (start, start))
    o = jnp.concatenate([acc / l for _, l, acc in ends], axis=0).T
    o_ref[...] = o
    half_ref[...] = o.astype(bf16)
    for e in range(2):
        lse_ref[e : e + 1, :] = ends[e][0] + jnp.log(ends[e][1])


def piece_specs(h, pieces):
    at = [h - (PAIRS - p.shape[1] // 256) if p.shape[1] > 256 else 0 for p in pieces]
    return [pl.BlockSpec((p.shape[0], 256), lambda i, c=c: (0, c)) for p, c in zip(pieces, at)]


def attend(plan, h, q, pieces):
    ranges, qseg, kseg = plan
    return pl.pallas_call(
        forward_kernel,
        grid=(ROWS // QT,),
        out_shape=(
            jax.ShapeDtypeStruct((ROWS, 128), f32),
            jax.ShapeDtypeStruct((ROWS, 128), bf16),
            jax.ShapeDtypeStruct((8, ROWS), f32),
        ),
        in_specs=[
            pl.BlockSpec(memory_space=pltpu.SMEM),
            pl.BlockSpec((8, QT), lambda i: (0, i)),
            pl.BlockSpec((SPAN, 128), lambda i: (0, 0)),
            pl.BlockSpec((QT, 128), lambda i: (i, h)),
        ]
        + piece_specs(h, pieces),
        out_specs=(
            pl.BlockSpec((QT, 128), lambda i: (i, 0)),
            pl.BlockSpec((QT, 128), lambda i: (i, 0)),
            pl.BlockSpec((8, QT), lambda i: (0, i)),
        ),
        scratch_shapes=[pltpu.VMEM((SPAN, 256), bf16), pltpu.VMEM((128, SPAN), bf16)],
        compiler_params=pltpu.CompilerParams(vmem_limit_bytes=VLIM),
        cost_estimate=pl.CostEstimate(flops=8_000_000_000, bytes_accessed=8_000_000, transcendentals=0),
        name="attention_forward",
    )(ranges, qseg, kseg, q, *pieces)


def backward_kernel(range_ref, qseg_ref, kseg_ref, q_ref, k0, k1, k2, k3, k4, do_ref, o_ref, lse_ref,
                    dq_ref, own_ref, f1, f2, f3, f4, span_ref, kt_ref, dkv_ref):
    qi = pl.program_id(0)
    last = ROWS // QT - 1

    @pl.when(qi == 0)
    def _():
        dkv_ref[...] = jnp.zeros_like(dkv_ref)
        fill_span(range_ref, span_ref, k0, (k1, k2, k3, k4))
        flip_span(span_ref, kt_ref, 0)

    qs = split_heads(q_ref[...])
    dos = split_heads(do_ref[...])
    qcat = jnp.concatenate(qs, axis=0)
    docat = jnp.concatenate(dos, axis=0)
    dm = (do_ref[...].astype(f32) * o_ref[...]).T
    delta = [jnp.sum(dm[64 * e : 64 * e + 64], axis=0, keepdims=True) for e in range(2)]

    first, count = range_ref[0, qi], range_ref[1, qi]

    def tile(t, carry):
        at = pl.ds(pl.multiple_of((first + t * (KT // 128)) * 128, 128), KT)
        same = same_segment(kseg_ref, qseg_ref, at)
        k = span_ref[at, 0:128]
        v = span_ref[at, 128:256]
        ps, dss, out = [], [], []
        for e in range(2):
            dims = (((1,), (1,)), ((), ()))
            s = lax.dot_general(k, qs[e], dims, preferred_element_type=f32)
            p = jnp.exp(jnp.where(same, s - lse_ref[e : e + 1, :], NEG))
            dp = lax.dot_general(v, dos[e], dims, preferred_element_type=f32)
            ds = (p * (dp - delta[e])).astype(bf16)
            kt = kt_ref[64 * e : 64 * e + 64, at]
            out.append(carry[e] + jnp.dot(kt, ds, preferred_element_type=f32))
            ps.append(p.astype(bf16))
            dss.append(ds)
        dkv_ref[at, 0:128] += jnp.dot(jnp.concatenate(dss, axis=1), qcat, preferred_element_type=f32)
        dkv_ref[at, 128:256] += jnp.dot(jnp.concatenate(ps, axis=1), docat, preferred_element_type=f32)
        return tuple(out)

    zero = jnp.zeros((64, QT), f32)
    dqt = lax.fori_loop(0, count, tile, (zero, zero))
    dq = jnp.concatenate(dqt, axis=0).T
    dq_ref[...] = dq.astype(bf16) * jnp.asarray(0.125, bf16)

    @pl.when(qi == last)
    def _():
        for at, far in zip(spots(range_ref), (f1, f2, f3, f4)):
            far[...] = dkv_ref[pl.ds(at, far.shape[0]), :].astype(bf16)
        own_ref[...] = dkv_ref[REACH : REACH + ROWS, :]


def attend_back(plan, h, q, pieces, d_att, mixed, lse):
    ranges, qseg, kseg = plan
    rowspec = pl.BlockSpec((QT, 128), lambda i: (i, 0))
    colspec = pl.BlockSpec((QT, 128), lambda i: (i, h))
    return pl.pallas_call(
        backward_kernel,
        grid=(ROWS // QT,),
        out_shape=(
            jax.ShapeDtypeStruct((ROWS, 128), bf16),
            jax.ShapeDtypeStruct((ROWS, 256), f32),
        )
        + tuple(jax.ShapeDtypeStruct((n, 256), bf16) for n in (ROWS, ROWS, NEAR, NEAR)),
        in_specs=[
            pl.BlockSpec(memory_space=pltpu.SMEM),
            pl.BlockSpec((8, QT), lambda i: (0, i)),
            pl.BlockSpec((SPAN, 128), lambda i: (0, 0)),
            colspec,
        ]
        + piece_specs(h, pieces)
        + [colspec, rowspec, pl.BlockSpec((8, QT), lambda i: (0, i))],
        out_specs=(
            rowspec,
            pl.BlockSpec((ROWS, 256), lambda i: (0, 0)),
        )
        + tuple(pl.BlockSpec((n, 256), lambda i: (0, 0)) for n in (ROWS, ROWS, NEAR, NEAR)),
        scratch_shapes=[
            pltpu.VMEM((SPAN, 256), bf16),
            pltpu.VMEM((128, SPAN), bf16),
            pltpu.VMEM((SPAN, 256), f32),
        ],
        compiler_params=pltpu.CompilerParams(vmem_limit_bytes=VLIM),
        cost_estimate=pl.CostEstimate(flops=8_000_000_000, bytes_accessed=12_000_000, transcendentals=0),
        name="attention_backward",
    )(ranges, qseg, kseg, q, *pieces, d_att, mixed, lse)


def exchange(part):
    return lax.ppermute(part, "heads", [(0, 1), (1, 0)])


def pair_sum(part):
    half = part.astype(bf16)
    return half.astype(f32) + exchange(half).astype(f32)


def side_by_side(own, other, index):
    return jnp.where(
        index == 0,
        jnp.concatenate([own, other], axis=1),
        jnp.concatenate([other, own], axis=1),
    )


def passed(block, distance):
    count = lax.axis_size("seq")
    route = [(i - distance, i) for i in range(count) if 0 <= i - distance < count]
    return lax.ppermute(block, "seq", route)


def across_cores(block):
    return lax.ppermute(block, "seq", [(i, i ^ 1) for i in range(lax.axis_size("seq"))])


def across_chips(block):
    count = lax.axis_size("seq")
    route = [(i, i + 1 if i % 2 else i - 1) for i in range(count)]
    return lax.ppermute(block, "seq", [(i, j) for i, j in route if 0 <= j < count])


def chip_along(block, step):
    count = lax.axis_size("seq")
    route = [(i, i - 2 * step if i % 2 else i + 2 * step) for i in range(count)]
    return lax.ppermute(block, "seq", [(i, j) for i, j in route if 0 <= j < count])


def layer_norm(values, gain, shift):
    centered = values - jnp.mean(values, axis=-1, keepdims=True)
    scale = lax.rsqrt(jnp.mean(centered * centered, axis=-1, keepdims=True) + EPSILON)
    return centered * scale * gain + shift


def gelu_exact(values):
    return jax.nn.gelu(values, approximate=False)


def nesterov(weight, grad, moment, average, rate):
    moment_new = 0.5 * moment + grad
    weight_new = weight - rate * (grad + 0.5 * moment_new)
    average_new = 0.5 * average + 0.5 * weight_new
    return (grad, weight_new, moment_new, average_new, weight_new.astype(bf16))


def dot(a, b, ca, cb):
    return lax.dot_general(a, b, (((ca,), (cb,)), ((), ())), preferred_element_type=f32)


def gathered(shard):
    return lax.all_gather(shard, "seq", axis=0, tiled=True)


def scattered(whole_sum):
    return lax.psum_scatter(whole_sum, "seq", scatter_dimension=0, tiled=True)


def body(
    frames,
    cotangent,
    lengths,
    kernel,
    kernel_moment,
    kernel_average,
    project,
    project_moment,
    project_average,
    combine,
    combine_moment,
    combine_average,
    expand,
    expand_moment,
    expand_average,
    shrink,
    shrink_moment,
    shrink_average,
    unitbias,
    unitbias_moment,
    unitbias_average,
    chanbias,
    chanbias_moment,
    chanbias_average,
    outbias,
    outbias_moment,
    outbias_average,
    normparams,
    normparams_moment,
    normparams_average,
):
    devices = lax.axis_size("seq")
    rows, width = frames.shape
    total = devices * rows
    first = lax.axis_index("seq") * rows
    index = lax.axis_index("heads")
    odd = lax.axis_index("seq") % 2
    local = project.shape[0]
    hidden_units = expand.shape[1]

    w_kernel = gathered(jnp.transpose(kernel, (2, 1, 0)).astype(bf16))
    small = jnp.concatenate(
        [unitbias, chanbias.reshape(-1), outbias.reshape(-1), normparams.reshape(-1)]
    ).astype(bf16)
    w_small = gathered(small[None])
    w_first = gathered(
        jnp.concatenate(
            [project[:, 0]]
            + [project[:, c, 128 * h : 128 * h + 128] for h in range(PAIRS) for c in (1, 2)]
            + [combine.T],
            axis=1,
        ).astype(bf16)
    )
    w_second = gathered(jnp.concatenate([expand, shrink.T], axis=1).astype(bf16))
    w_combine = w_first[:, 3 * HALF :]
    w_combine_far = exchange(w_combine)
    cuts = [unitbias.size, chanbias.size, outbias.size, normparams.size]
    parts, at = [], 0
    for size in cuts:
        parts.append(w_small[:, at : at + size].astype(f32))
        at += size
    b_unit = parts[0].reshape(-1)
    b_chan = jnp.transpose(parts[1].reshape(devices, 3, -1), (1, 0, 2)).reshape(3, -1)
    b_out = jnp.transpose(parts[2].reshape(devices, 2, -1), (1, 0, 2)).reshape(2, -1)
    norms = jnp.transpose(parts[3].reshape(devices, 3, 2, -1), (1, 2, 0, 3)).reshape(3, 2, -1)

    count = lengths.shape[0]
    order = jnp.arange(count, dtype=i32)
    ends = jnp.sum(jnp.where(order[None, :] <= order[:, None], lengths[None, :], 0), axis=1).astype(i32)
    starts = ends - lengths
    plan = block_plan(starts, ends, first)
    reach = attention_plan(starts, ends, first, odd)

    x_half = lax.dynamic_slice_in_dim(frames, index * HALF, HALF, 1).astype(bf16)
    window = jnp.concatenate(
        [passed(x_half[rows - HALO :], 1), x_half, passed(x_half[:HALO], -1)], axis=0
    )
    ready = prepare(plan, window)
    conv_out, spread_taps = conv(plan, ready, w_kernel)
    pre = conv_out + b_chan[0]
    spread_part = gelu_exact(pre).astype(bf16)
    spread = side_by_side(spread_part, exchange(spread_part), index)
    h1, norm0_back = jax.vjp(layer_norm, frames + spread.astype(f32), norms[0, 0], norms[0, 1])
    h1_half = h1.astype(bf16)
    proj = dot(h1_half, w_first[:, : 3 * HALF], 1, 0)
    scale = HEAD ** (-0.5)
    queries = ((proj[:, :HALF] + b_chan[1]) * scale).astype(bf16)
    kv_bias = b_chan[2].reshape(PAIRS, 1, 128)
    kv_bias = jnp.concatenate([jnp.zeros_like(kv_bias), kv_bias], axis=1).reshape(-1)
    both = (proj[:, HALF:] + kv_bias).astype(bf16)
    near = NEAR

    def fetched(lo, hi):
        block = both[:, lo:hi]
        head, tail = block[:near], block[rows - near :]
        return (
            across_cores(block),
            across_chips(block),
            chip_along(jnp.where(odd == 1, head, tail), 1),
            chip_along(jnp.where(odd == 1, tail, head), -1),
        )

    early = fetched(0, 256)
    both, early = lax.optimization_barrier((both, early))
    late = fetched(256, 256 * PAIRS)
    pieces = [(both,) + (early if h == 0 else late) for h in range(PAIRS)]
    mixed, attended, attended_far, lse = [], [], [], []
    for h in range(PAIRS):
        if h == 0:
            q_part, w_combine_far = lax.optimization_barrier((queries, w_combine_far))
        if h >= 2:
            q_part, attended_far[h - 2] = lax.optimization_barrier((queries, attended_far[h - 2]))
        mixed_part, half, lse_part = attend(reach, h, q_part, pieces[h])
        mixed.append(mixed_part)
        lse.append(lse_part)
        attended.append(half)
        attended_far.append(exchange(half))
    attended = jnp.concatenate(attended, axis=1)
    attended_all = side_by_side(attended, jnp.concatenate(attended_far, axis=1), index)
    w_combine_all = side_by_side(w_combine, w_combine_far, index)
    w_expand = w_second[:, :hidden_units]
    w_shrink = w_second[:, hidden_units:]
    step = rows // CHUNKS
    cuts_of = [slice(c * step, (c + 1) * step) for c in range(CHUNKS)]
    first_half, second_half = [], []
    for cut in cuts_of:
        branch = dot(attended_all[cut], w_combine_all, 1, 1)
        h2, norm1_back = jax.vjp(layer_norm, h1[cut] + branch + b_out[0], norms[1, 0], norms[1, 1])
        h2_half = h2.astype(bf16)
        inner = dot(h2_half, w_expand, 1, 0) + b_unit
        hidden, gelu_inner_back = jax.vjp(gelu_exact, inner)
        hidden_half = hidden.astype(bf16)
        sent = dot(hidden_half, w_shrink, 1, 1).astype(bf16)
        first_half.append((h2, norm1_back, h2_half, gelu_inner_back, hidden_half, sent, exchange(sent)))
    sent_back = None
    for cut, (h2, norm1_back, h2_half, gelu_inner_back, hidden_half, sent, came) in zip(
        cuts_of, first_half
    ):
        if sent_back is not None:
            came, _ = lax.optimization_barrier((came, sent_back))
        outer = sent.astype(f32) + came.astype(f32)
        out_part, norm2_back = jax.vjp(layer_norm, h2 + outer + b_out[1], norms[2, 0], norms[2, 1])
        dx3, gain2_grad, shift2_grad = norm2_back(cotangent[cut])
        d_out = dx3.astype(bf16)
        d_hidden = dot(d_out, w_shrink, 1, 0)
        d_inner = gelu_inner_back(d_hidden)[0]
        d_inner_half = d_inner.astype(bf16)
        sent_back = dot(d_inner_half, w_expand, 1, 1).astype(bf16)
        sums = [gain2_grad, shift2_grad, jnp.sum(dx3, axis=0), jnp.sum(d_inner, axis=0)]
        second_half.append(
            [out_part, (sent_back, exchange(sent_back)), norm1_back, h2_half, d_inner_half, d_out, hidden_half, dx3, sums]
        )
    layer_out = jnp.concatenate([part[0] for part in second_half], axis=0)
    gain2_grad, shift2_grad, outer_bias_grad, unit_grad = map(sum, zip(*[p[-1] for p in second_half]))
    second_part = jnp.concatenate(
        [
            sum(dot(p[a], p[b], 0, 0) for p in second_half).astype(bf16)
            for a, b in ((3, 4), (5, 6))
        ],
        axis=1,
    )
    dx2_parts, gain1_parts, shift1_parts = zip(
        *[p[2](p[7] + (p[1][0].astype(f32) + p[1][1].astype(f32))) for p in second_half]
    )
    gain1_grad, shift1_grad = sum(gain1_parts), sum(shift1_parts)
    dx2 = jnp.concatenate(dx2_parts, axis=0)
    branch_bias_grad = jnp.sum(dx2, axis=0)
    d_branch = dx2.astype(bf16)
    d_att = dot(d_branch, w_combine, 1, 0).astype(bf16)
    d_att, second_part = lax.optimization_barrier((d_att, second_part))
    second_sum = scattered(second_part).astype(f32)
    dq_parts, kv_parts = [], []
    arrived = {}
    for h in range(PAIRS):
        d_part = d_att
        if h >= 2:
            two = arrived[h - 2][:2]
            d_part, two = lax.optimization_barrier((d_att, two))
            arrived[h - 2] = two + arrived[h - 2][2:]
        dq_part, own, core, chip, far, beyond = attend_back(
            reach, h, queries, pieces[h], d_part, mixed[h], lse[h]
        )
        arrived[h] = (
            across_cores(core),
            across_chips(chip),
            chip_along(far, -1),
            chip_along(beyond, 1),
            own,
        )
        dq_parts.append(dq_part)
    for h in range(PAIRS):
        core, chip, far, beyond, own = [a.astype(f32) for a in arrived[h]]
        ends_of = jnp.concatenate(
            [jnp.where(odd == 1, far, beyond), jnp.where(odd == 1, beyond, far)], axis=0
        )
        kv_parts.append((own + core + chip + ends_of).astype(bf16))
    dq_half = jnp.concatenate(dq_parts, axis=1)
    d_both_half = jnp.concatenate(kv_parts, axis=1)
    stacked = jnp.concatenate([dq_half, d_both_half], axis=1)
    query_bias_grad = jnp.sum(dq_half.astype(f32), axis=0)
    value_bias_grad = jnp.sum(
        d_both_half.astype(f32), axis=0
    ).reshape(PAIRS, 2, 128)[:, 1].reshape(-1)
    dh1_half = dot(stacked, w_first[:, : 3 * HALF], 1, 1).astype(bf16)
    dh1_half, second_sum = lax.optimization_barrier((dh1_half, second_sum))
    dh1 = dx2 + (dh1_half.astype(f32) + exchange(dh1_half).astype(f32))
    first_part = (
        jnp.concatenate(
            [dot(h1_half, stacked, 0, 0).astype(bf16), dot(d_branch, attended, 0, 0).astype(bf16)],
            axis=1,
        )
    )
    first_part, second_sum = lax.optimization_barrier((first_part, second_sum))
    first_sum = scattered(first_part).astype(f32)
    dx1, gain0_grad, shift0_grad = norm0_back(dh1)
    d_spread = lax.dynamic_slice_in_dim(dx1, index * HALF, HALF, 1)
    d_conv = jax.vjp(gelu_exact, pre)[1](d_spread)[0]
    conv_bias_grad = jnp.sum(d_conv, axis=0)
    d_conv_half = d_conv.astype(bf16)
    spread_out = lambda grad, lead: jnp.transpose(
        grad.reshape(lead, devices, -1), (1, 0, 2)
    ).reshape(devices, -1)
    small_part = jnp.concatenate(
            [
                unit_grad.reshape(devices, -1),
                spread_out(jnp.stack([conv_bias_grad, query_bias_grad, value_bias_grad]), 3),
                spread_out(jnp.stack([branch_bias_grad, outer_bias_grad]), 2),
                spread_out(
                    jnp.stack(
                        [gain0_grad, shift0_grad, gain1_grad, shift1_grad, gain2_grad, shift2_grad]
                    ),
                    6,
                ),
            ],
            axis=1,
        )
    small_part = jnp.pad(small_part, ((0, 0), (0, EXTRA * HALF - small_part.shape[1])))
    small_part = small_part.astype(bf16).reshape(devices, EXTRA, HALF)
    d_own = jnp.pad(d_conv_half, ((HALO, HALO), (0, 0)))
    tap_part = tap_grad(plan, ready, d_own, small_part)
    tap_part, first_sum = lax.optimization_barrier((tap_part, first_sum))
    tap_sum = scattered(tap_part)[0].astype(f32)
    kernel_sum = tap_sum[:-EXTRA].reshape(TAPS // devices, CG, HALF)
    small_sum = tap_sum[-EXTRA:].reshape(-1)
    d_window = jnp.concatenate(
        [passed(d_conv_half[rows - HALO :], 1), d_conv_half, passed(d_conv_half[:HALO], -1)], axis=0
    )
    d_input = conv_back(plan, ready, d_window, spread_taps).astype(bf16)
    frames_grad = dx1 + side_by_side(d_input, exchange(d_input), index).astype(f32)

    pieces, at = [], 0
    for size in cuts:
        pieces.append(small_sum[at : at + size])
        at += size
    unit_sum = pieces[0]
    chan_sum = pieces[1].reshape(chanbias.shape)
    out_sum = pieces[2].reshape(outbias.shape)
    norm_sum = pieces[3].reshape(normparams.shape)
    kv_sum = first_sum[:, HALF : 3 * HALF].reshape(local, PAIRS, 2, 128)
    project_sum = jnp.stack(
        [first_sum[:, :HALF]] + [kv_sum[:, :, c].reshape(local, HALF) for c in range(2)], axis=1
    )

    root = total**0.5
    small_rate = 0.1 / root
    out = [layer_out, frames_grad]
    for weight, grad, moment, average, rate in (
        (kernel, jnp.transpose(kernel_sum, (2, 1, 0)), kernel_moment, kernel_average, (CG * TAPS) ** (-0.5) / root),
        (project, project_sum, project_moment, project_average, width ** (-0.5) / root),
        (combine, first_sum[:, 3 * HALF :].T, combine_moment, combine_average, (width // 16) ** (-0.5) / root),
        (expand, second_sum[:, :hidden_units], expand_moment, expand_average, width ** (-0.5) / root),
        (shrink, second_sum[:, hidden_units:].T, shrink_moment, shrink_average, (2 * hidden_units) ** (-0.5) / root),
        (unitbias, unit_sum, unitbias_moment, unitbias_average, 0.5 / root),
        (chanbias, chan_sum, chanbias_moment, chanbias_average, small_rate),
        (outbias, out_sum, outbias_moment, outbias_average, small_rate),
        (normparams, norm_sum, normparams_moment, normparams_average, small_rate),
    ):
        out.extend(nesterov(weight, grad, moment, average, rate))
    return tuple(out)


def solution(mesh):
    kernel_spec = P("heads", None, "seq")
    project_spec = P("seq", None, "heads")
    tall = P("heads", "seq")
    wide = P("seq", "heads")
    unit = P(("heads", "seq"))
    chan = P(None, ("heads", "seq"))
    outb = P(None, "seq")
    norm = P(None, None, "seq")
    weights = (kernel_spec, project_spec, tall, wide, tall, unit, chan, outb, norm)
    rows = P("seq", None)
    return jax.shard_map(
        body,
        mesh=mesh,
        in_specs=(rows, rows, P()) + tuple(s for s in weights for _ in range(3)),
        out_specs=(rows, rows) + tuple(s for s in weights for _ in range(5)),
        check_vma=False,
    )
```

```python
import functools

import jax
import jax.numpy as jnp
from jax import lax
from jax.experimental import pallas as pl
from jax.experimental.pallas import tpu as pltpu
from jax.sharding import PartitionSpec as P

HEAD = 64
PAIRS = 3
CHUNKS = 2
EPSILON = 1e-05

bf16, f32, i32 = jnp.bfloat16, jnp.float32, jnp.int32
CG, TAPS, GROUPS, HALO = 48, 128, 8, 64
ROWS, WIN, HALF = 1024, 1152, 384
CM, XM = 272, 304
NQ = 33
PJ = 134
EXTRA = 16
VLIM = 58 << 20


def iota(shape, dim):
    return lax.broadcasted_iota(i32, shape, dim)


def block_plan(starts, ends, first):
    w0 = first - HALO
    b = jnp.clip(starts - w0, 0, WIN)
    e = jnp.clip(ends - w0, 0, WIN)
    nblk = (e - b + 3) // 4
    n = starts.shape[0]
    before = jnp.arange(n)[None, :] < jnp.arange(n)[:, None]
    bs = jnp.sum(jnp.where(before, nblk[None, :], 0), axis=1).astype(i32)
    bs = bs + (jnp.clip(-w0, 0, WIN) + 3) // 4
    w = jnp.arange(WIN, dtype=i32)
    inside = (b[None, :] <= w[:, None]) & (w[:, None] < e[None, :])
    p = jnp.sum(jnp.where(inside, 4 * bs - b + w[:, None] + 1, 0), axis=1).astype(i32) - 1
    most = min(WIN, WIN // 4 + n)
    maxc = -((16 - most) // CM)
    lcap = CM * (maxc - 1) + XM
    m = jnp.arange(lcap, dtype=i32)
    hit = (bs[None, :] <= m[:, None]) & (m[:, None] < (bs + nblk)[None, :])
    bseg = jnp.sum(jnp.where(hit, jnp.arange(1, n + 1, dtype=i32)[None, :], 0), axis=1).astype(i32) - 1
    chunks = jnp.maximum((p[HALO + ROWS - 1] // 4 - 16) // CM + 1, 1)
    return (
        jnp.reshape(chunks, (1,)).astype(i32),
        jnp.broadcast_to(p[None, :], (8, WIN)),
        jnp.broadcast_to(p[:, None], (WIN, 128)),
        jnp.broadcast_to(bseg[:, None], (lcap, 128)),
    )


def select_pair(h, rows, base):
    lane = iota((rows, 256), 1)
    src = CG * (2 * h + (lane >> 7)) + (lane & 63) - base
    ok = ((lane & 63) < CG) & (iota((rows, 256), 0) == src)
    return jnp.where(ok, 1.0, 0.0).astype(bf16)


def build_blocks(s_ref, dup):
    y = [jnp.dot(s_ref[0, t], dup, preferred_element_type=f32).astype(bf16) for t in range(4)]
    low = iota((XM, 128), 1) < 64
    out = []
    for g in range(2):
        tiles = [v[:, 128 * g : 128 * g + 128] for v in y]
        out.append(
            jnp.concatenate(
                [jnp.where(low, tiles[0], tiles[1]), jnp.where(low, tiles[2], tiles[3])], axis=1
            )
        )
    return out


def build_taps(k_ref, sel, p_ref, base_tile):
    p_ref[...] = jnp.zeros_like(p_ref)
    step = 16
    for j0 in range(0, TAPS, step):
        part = k_ref[pl.ds(j0, step), :, pl.ds(pl.multiple_of(base_tile * 128, 128), 256)]
        d = jnp.dot(part.reshape(step * CG, 256), sel, preferred_element_type=f32)
        d = d.astype(bf16).reshape(step, CG, 256)
        for g in range(2):
            p_ref[g, pl.ds(j0 + 2, step), 0:CG, 0:64] = d[:, :, 128 * g : 128 * g + 64]
            p_ref[g, pl.ds(j0 + 3, step), 0:CG, 64:128] = d[:, :, 128 * g + 64 : 128 * g + 128]


def pair_lanes(h):
    base_tile = h >> 1
    return base_tile, pl.ds(pl.multiple_of(base_tile * 128, 128), 256)


def prepare_kernel(n_ref, *refs):
    @pl.when(pl.program_id(0) < n_ref[0])
    def _():
        prepare_chunk(pl.program_id(0), *refs)


def prepare_chunk(c, prow_ref, pcol_ref, bseg_ref, x_ref, s_ref, r_ref, mask_ref, tmask_ref, xb_ref, xt_ref):
    prow = prow_ref[0:1, :]
    for t in range(4):
        pos = 4 * (iota((XM, WIN), 0) + CM * c) + t
        s_ref[0, t] = jnp.where(pos == prow, 1.0, 0.0).astype(bf16)
    pcol = pcol_ref[HALO : HALO + ROWS, :]
    lane = iota((ROWS, 4 * CM), 1)
    phase = sum([(lane >= CM * t).astype(i32) for t in range(1, 4)])
    spot = 4 * (16 + CM * c) + 4 * lane - (4 * CM - 1) * phase
    wide = jnp.concatenate([pcol] * 9, axis=1)[:, : 4 * CM]
    r_ref[0] = jnp.where(wide == spot, 1.0, 0.0).astype(bf16)
    seg = bseg_ref[pl.ds(pl.multiple_of(CM * c, 16), XM), :]
    none = jnp.full((32, 128), -7, i32)
    own = jnp.concatenate([none, seg[16 : 16 + CM], none], axis=0)
    for q in range(NQ):
        same = seg[q : q + CM] == seg[16 : 16 + CM]
        mask_ref[0, q] = jnp.where(same, 1.0, 0.0).astype(bf16)
        same = seg == own[32 - q : 32 - q + XM]
        tmask_ref[0, q] = jnp.where(same, 1.0, 0.0).astype(bf16)
    for h in range(4):
        base = 128 * (h // 2)
        sel = select_pair(h, 256, base)
        dup = jnp.dot(x_ref[:, base : base + 256], sel, preferred_element_type=f32).astype(bf16)
        for g, block in enumerate(build_blocks(s_ref, dup)):
            xb_ref[0, 2 * h + g] = block
            xt_ref[0, 2 * h + g] = block.T


def fixed(shape):
    return pl.BlockSpec(shape, lambda *_: (0,) * len(shape))


def chunk_count(plan):
    return (plan[3].shape[0] - XM) // CM + 1


def call(kernel, name, grid, plan, in_specs, out_specs, out_shape, scratch, flops, args):
    return pl.pallas_call(
        kernel,
        grid_spec=pltpu.PrefetchScalarGridSpec(
            num_scalar_prefetch=1,
            grid=grid,
            in_specs=in_specs,
            out_specs=out_specs,
            scratch_shapes=scratch,
        ),
        out_shape=out_shape,
        compiler_params=pltpu.CompilerParams(vmem_limit_bytes=VLIM),
        cost_estimate=pl.CostEstimate(flops=flops, bytes_accessed=15_000_000, transcendentals=0),
        name=name,
    )(plan[0], *args)


def prepare(plan, window):
    chunks, prow, pcol, bseg = plan
    shapes = ((4, XM, WIN), (ROWS, 4 * CM), (NQ, CM, 128), (NQ, XM, 128), (8, XM, 256), (8, 256, XM))
    maxc = chunk_count(plan)
    return call(
        prepare_kernel,
        "conv_prepare",
        (maxc,),
        plan,
        [fixed(a.shape) for a in (prow, pcol, bseg, window)],
        tuple(
            pl.BlockSpec((1,) + s, lambda c, n, k=len(s): (jnp.minimum(c, n[0] - 1),) + (0,) * k)
            for s in shapes
        ),
        tuple(jax.ShapeDtypeStruct((maxc,) + s, bf16) for s in shapes),
        [],
        10_000_000_000,
        (prow, pcol, bseg, window),
    )


def conv_forward_kernel(n_ref, *refs):
    c, h = pl.program_id(0), pl.program_id(1)

    @pl.when(c < n_ref[0])
    def _():
        conv_chunk(False, c, h, *refs)


def conv_back_kernel(n_ref, d_ref, s_ref, *refs):
    c, h = pl.program_id(0), pl.program_id(1)

    @pl.when(c < n_ref[0])
    def _():
        conv_chunk(True, c, h, (d_ref, s_ref), *refs)


def conv_chunk(back, c, h, x_ref, mask_ref, r_ref, k_ref, out_ref, *rest):
    base_tile, lanes = pair_lanes(h)
    if back:
        s_ref, (xb_ref, o_ref) = x_ref[1], rest
        p_ref = k_ref
        sel = select_pair(h, 256, 128 * base_tile)
        dup = jnp.dot(x_ref[0][:, lanes], sel, preferred_element_type=f32).astype(bf16)
        for g, block in enumerate(build_blocks(s_ref, dup)):
            xb_ref[0, g] = block
    else:
        xb_ref = x_ref
        p_ref, o_ref = rest
        build_taps(k_ref, select_pair(h, 256, 128 * base_tile), p_ref, base_tile)

    @pl.when(h == 0)
    def _():
        o_ref[...] = jnp.zeros_like(o_ref)

    total = [jnp.zeros((CM, 256), f32) for _ in range(4)]
    for g in range(2):
        acc = jnp.zeros((CM, 256), f32)
        for q in range(NQ):
            m = mask_ref[0, q]
            xs = xb_ref[0, g, q : q + CM, :] * jnp.concatenate([m, m], axis=1)
            if back:
                a, b = 130 - 4 * q, 128 - 4 * q
            else:
                a, b = 4 * q + 2, 4 * q
            w = jnp.concatenate(
                [p_ref[g, a : a + 4].reshape(256, 128), p_ref[g, b : b + 4].reshape(256, 128)],
                axis=1,
            )
            dims = (((1,), (1 if back else 0,)), ((), ()))
            acc = acc + lax.dot_general(xs, w, dims, preferred_element_type=f32)
        acc = acc.astype(bf16)
        row = iota((256, 256), 0)
        target = CG * (2 * h + g) - 128 * base_tile + (row & 63)
        hit = ((row & 63) < CG) & (iota((256, 256), 1) == target)
        for t in range(4):
            fold = jnp.where(hit & ((row >> 6) == t), 1.0, 0.0).astype(bf16)
            total[t] = total[t] + jnp.dot(acc, fold, preferred_element_type=f32)
    for t in range(4):
        o_ref[CM * t : CM * t + CM, lanes] += total[t].astype(bf16)

    @pl.when(h == 3)
    def _():
        y = jnp.dot(r_ref[0], o_ref[...], preferred_element_type=f32)

        @pl.when(c == 0)
        def _():
            out_ref[...] = y

        @pl.when(c > 0)
        def _():
            out_ref[...] += y


def by_chunk(shape):
    return pl.BlockSpec(
        (1,) + shape, lambda c, h, n: (jnp.minimum(c, n[0] - 1),) + (0,) * len(shape)
    )


def by_pair(shape):
    return pl.BlockSpec(
        (2,) + shape, lambda c, h, n: (jnp.where(c < n[0], h, 3),) + (0,) * len(shape)
    )


def conv(plan, ready, taps):
    _, r, mask, _, xb, _ = ready
    x_spec = pl.BlockSpec(
        (1, 2, XM, 256),
        lambda c, h, n: (jnp.minimum(c, n[0] - 1), jnp.where(c < n[0], h, 3), 0, 0),
    )
    return call(
        conv_forward_kernel,
        "conv_forward",
        (chunk_count(plan), 4),
        plan,
        [x_spec, by_chunk((NQ, CM, 128)), by_chunk((ROWS, 4 * CM)), fixed((TAPS, CG, HALF))],
        (fixed((ROWS, HALF)), by_pair((PJ, 64, 128))),
        (
            jax.ShapeDtypeStruct((ROWS, HALF), f32),
            jax.ShapeDtypeStruct((8, PJ, 64, 128), bf16),
        ),
        [pltpu.VMEM((4 * CM, HALF), bf16)],
        25_000_000_000,
        (xb, mask, r, taps),
    )


def conv_back(plan, ready, window, spread_taps):
    s, r, mask, _, _, _ = ready
    return call(
        conv_back_kernel,
        "conv_back",
        (chunk_count(plan), 4),
        plan,
        [
            fixed((WIN, HALF)),
            by_chunk((4, XM, WIN)),
            by_chunk((NQ, CM, 128)),
            by_chunk((ROWS, 4 * CM)),
            by_pair((PJ, 64, 128)),
        ],
        fixed((ROWS, HALF)),
        jax.ShapeDtypeStruct((ROWS, HALF), f32),
        [pltpu.VMEM((1, 2, XM, 256), bf16), pltpu.VMEM((4 * CM, HALF), bf16)],
        25_000_000_000,
        (window, s, mask, r, spread_taps),
    )


def tap_grad_kernel(n_ref, xt_ref, s_ref, mask_ref, d_ref, small_ref, out_ref, dp_ref, acc_ref, sum_ref):
    h, c = pl.program_id(0), pl.program_id(1)
    base_tile, lanes = pair_lanes(h)

    @pl.when((h == 0) & (c == 0))
    def _():
        out_ref[...] = jnp.zeros_like(out_ref)
        out_ref[:, out_ref.shape[1] - EXTRA :, :] = small_ref[...]
        dp_ref[...] = jnp.zeros_like(dp_ref)

    @pl.when(c < n_ref[0])
    def _():
        sel = select_pair(h, 256, 128 * base_tile)
        ddup = jnp.dot(d_ref[:, lanes], sel, preferred_element_type=f32).astype(bf16)
        for g, block in enumerate(build_blocks(s_ref, ddup)):
            dp_ref[g, 32 : 32 + CM, :] = block[16 : 16 + CM]
        for g in range(2):
            carry = jnp.zeros((128, 128), f32)
            for q in range(NQ):
                m = mask_ref[0, q]
                ds = dp_ref[g, 32 - q : 32 - q + XM, :] * jnp.concatenate([m, m], axis=1)
                part = jnp.dot(xt_ref[0, g], ds, preferred_element_type=f32)
                left, right = part[:, 0:128], part[:, 128:256]
                acc_ref[g, 4 * q : 4 * q + 2] = (right[0:128] + carry).reshape(2, 64, 128)
                acc_ref[g, 4 * q + 2 : 4 * q + 4] = (left[0:128] + right[128:256]).reshape(2, 64, 128)
                carry = left[128:256]
            acc_ref[g, 4 * NQ : 4 * NQ + 2] = carry.reshape(2, 64, 128)

        @pl.when(c > 0)
        def _():
            acc_ref[...] += sum_ref[...]

        @pl.when(c < n_ref[0] - 1)
        def _():
            sum_ref[...] = acc_ref[...]

    @pl.when(c == pl.num_programs(1) - 1)
    def _():
        per = TAPS // out_ref.shape[0]
        low = iota((1, 1, 128), 2) < 64
        row = iota((128, 256), 0)
        src = CG * (2 * h + (row >> 6)) + (row & 63) - 128 * base_tile
        back = jnp.where(((row & 63) < CG) & (iota((128, 256), 1) == src), 1.0, 0.0).astype(bf16)
        step = 16
        for j0 in range(0, TAPS, step):
            now = [acc_ref[g, j0 + 2 : j0 + 2 + step, 0:CG, :] for g in range(2)]
            nxt = [acc_ref[g, j0 + 3 : j0 + 3 + step, 0:CG, :] for g in range(2)]
            here = jnp.where(low, now[0], nxt[1]).reshape(step * CG, 128)
            far = jnp.where(low, now[1], nxt[0]).reshape(step * CG, 128)
            both = (here + pltpu.roll(far, 64, 1)).astype(bf16)
            o = jnp.dot(both, back, preferred_element_type=f32).astype(bf16)
            o = o.reshape(step // per, per * CG, 256)
            out_ref[j0 // per : (j0 + step) // per, 0 : per * CG, lanes] += o


def tap_grad(plan, ready, d_own, small):
    s, _, _, tmask, _, xt = ready
    devices = small.shape[0]
    shape = (devices, TAPS // devices * CG + EXTRA, HALF)
    chunked = lambda sh: pl.BlockSpec(
        (1,) + sh, lambda h, c, n: (jnp.minimum(c, n[0] - 1),) + (0,) * len(sh)
    )
    x_spec = pl.BlockSpec((1, 2, 256, XM), lambda h, c, n: (jnp.minimum(c, n[0] - 1), h, 0, 0))
    return call(
        tap_grad_kernel,
        "tap_gradient",
        (4, chunk_count(plan)),
        plan,
        [
            x_spec,
            chunked((4, XM, WIN)),
            chunked((NQ, XM, 128)),
            fixed((WIN, HALF)),
            fixed(small.shape),
        ],
        fixed(shape),
        jax.ShapeDtypeStruct(shape, bf16),
        [
            pltpu.VMEM((2, 32 + CM + 32, 256), bf16),
            pltpu.VMEM((2, PJ, 64, 128), f32),
            pltpu.VMEM((2, PJ, 64, 128), f32),
        ],
        1_000_000_000,
        (xt, s, tmask, d_own, small),
    )
REACH = 1536
SPAN = ROWS + 2 * REACH
QT_AHEAD, QT_BACK, KT = 512, 256, 1664
NEAR = REACH - ROWS
NEG = -1e30


def segment_count(ends, positions):
    return jnp.sum((ends[None, :] <= positions[:, None]).astype(i32), axis=1).astype(i32)

def attention_plan(starts, ends, first, odd):
    w = first - REACH + jnp.arange(SPAN, dtype=i32)
    kseg = segment_count(ends, w)
    kseg = jnp.where(w < 0, -1, kseg)
    qseg = kseg[REACH : REACH + ROWS]
    n = jnp.arange(starts.shape[0], dtype=i32)

    def tiles_of(rows):
        edge = qseg.reshape(ROWS // rows, rows)
        head = jnp.sum(jnp.where(n[None] == edge[:, :1], starts[None], 0), axis=1) - (first - REACH)
        tail = jnp.sum(jnp.where(n[None] == edge[:, -1:], ends[None], 0), axis=1) - (first - REACH)
        lo = jnp.clip(head // 128, 0, SPAN // 128)
        hi = jnp.clip((tail + 127) // 128, 1, SPAN // 128)
        tiles = jnp.maximum((hi - lo + KT // 128 - 1) // (KT // 128), 1)
        lo = jnp.minimum(lo, SPAN // 128 - tiles * (KT // 128))
        return jnp.stack([lo, tiles, jnp.full_like(lo, odd)]).astype(i32)

    return (
        tiles_of(QT_AHEAD),
        tiles_of(QT_BACK),
        jnp.broadcast_to(qseg[None], (8, ROWS)),
        jnp.broadcast_to(kseg[:, None], (SPAN, 128)),
    )


def split_heads(a):
    low = iota(a.shape, 1) < 64
    zero = jnp.zeros((), a.dtype)
    return jnp.where(low, a, zero), jnp.where(low, zero, a)

def spots(range_ref):
    odd = range_ref[2, 0] == 1
    right, end = REACH + ROWS, SPAN - NEAR
    at = [
        jnp.where(odd, NEAR, right),
        jnp.where(odd, right, NEAR),
        jnp.where(odd, end, 0),
        jnp.where(odd, 0, end),
    ]
    return [pl.multiple_of(x, NEAR) for x in at]


def fill_span(range_ref, span_ref, own, others):
    span_ref[REACH : REACH + ROWS, :] = own[...]
    for at, piece in zip(spots(range_ref), others):
        span_ref[pl.ds(at, piece.shape[0]), :] = piece[...]


def flip_span(src_ref, dst_ref, lane):
    for at in range(0, SPAN, 512):
        dst_ref[:, at : at + 512] = src_ref[at : at + 512, lane : lane + 128].T


def same_segment(kseg_ref, qseg_ref, at):
    ks = kseg_ref[at, :]
    ks = jnp.concatenate([ks] * (qseg_ref.shape[1] // 128), axis=1)
    return ks == qseg_ref[0:1, :]


def forward_kernel(range_ref, qseg_ref, kseg_ref, q_ref, k0, k1, k2, k3, k4, o_ref, half_ref, lse_ref, span_ref, vt_ref):
    qi = pl.program_id(0)

    @pl.when(qi == 0)
    def _():
        fill_span(range_ref, span_ref, k0, (k1, k2, k3, k4))
        flip_span(span_ref, vt_ref, 128)

    qs = split_heads(q_ref[...])

    first, count = range_ref[0, qi], range_ref[1, qi]

    def tile(t, carry):
        at = pl.ds(pl.multiple_of((first + t * (KT // 128)) * 128, 128), KT)
        same = same_segment(kseg_ref, qseg_ref, at)
        k = span_ref[at, 0:128]
        out = []
        for e in range(2):
            m, l, acc = carry[e]
            s = lax.dot_general(k, qs[e], (((1,), (1,)), ((), ())), preferred_element_type=f32)
            s = jnp.where(same, s, NEG)
            new = jnp.maximum(m, jnp.max(s, axis=0, keepdims=True))
            p = jnp.exp(s - new)
            alpha = jnp.exp(m - new)
            l = l * alpha + jnp.sum(p, axis=0, keepdims=True)
            vt = vt_ref[64 * e : 64 * e + 64, at]
            acc = acc * alpha + jnp.dot(vt, p.astype(bf16), preferred_element_type=f32)
            out.append((new, l, acc))
        return tuple(out)

    start = (jnp.full((1, QT_AHEAD), NEG, f32), jnp.zeros((1, QT_AHEAD), f32), jnp.zeros((64, QT_AHEAD), f32))
    ends = lax.fori_loop(0, count, tile, (start, start))
    o = jnp.concatenate([acc / l for _, l, acc in ends], axis=0).T
    o_ref[...] = o
    half_ref[...] = o.astype(bf16)
    for e in range(2):
        lse_ref[e : e + 1, :] = ends[e][0] + jnp.log(ends[e][1])


def piece_specs(h, pieces):
    at = [h - (PAIRS - p.shape[1] // 256) if p.shape[1] > 256 else 0 for p in pieces]
    return [pl.BlockSpec((p.shape[0], 256), lambda i, c=c: (0, c)) for p, c in zip(pieces, at)]


def attend(plan, h, q, pieces):
    ranges, _, qseg, kseg = plan
    return pl.pallas_call(
        forward_kernel,
        grid=(ROWS // QT_AHEAD,),
        out_shape=(
            jax.ShapeDtypeStruct((ROWS, 128), f32),
            jax.ShapeDtypeStruct((ROWS, 128), bf16),
            jax.ShapeDtypeStruct((8, ROWS), f32),
        ),
        in_specs=[
            pl.BlockSpec(memory_space=pltpu.SMEM),
            pl.BlockSpec((8, QT_AHEAD), lambda i: (0, i)),
            pl.BlockSpec((SPAN, 128), lambda i: (0, 0)),
            pl.BlockSpec((QT_AHEAD, 128), lambda i: (i, h)),
        ]
        + piece_specs(h, pieces),
        out_specs=(
            pl.BlockSpec((QT_AHEAD, 128), lambda i: (i, 0)),
            pl.BlockSpec((QT_AHEAD, 128), lambda i: (i, 0)),
            pl.BlockSpec((8, QT_AHEAD), lambda i: (0, i)),
        ),
        scratch_shapes=[pltpu.VMEM((SPAN, 256), bf16), pltpu.VMEM((128, SPAN), bf16)],
        compiler_params=pltpu.CompilerParams(vmem_limit_bytes=VLIM),
        cost_estimate=pl.CostEstimate(flops=8_000_000_000, bytes_accessed=8_000_000, transcendentals=0),
        name="attention_forward",
    )(ranges, qseg, kseg, q, *pieces)


def backward_kernel(range_ref, qseg_ref, kseg_ref, q_ref, k0, k1, k2, k3, k4, do_ref, o_ref, lse_ref,
                    dq_ref, own_ref, f1, f2, f3, f4, span_ref, kt_ref, dkv_ref):
    qi = pl.program_id(0)
    last = ROWS // QT_BACK - 1

    @pl.when(qi == 0)
    def _():
        dkv_ref[...] = jnp.zeros_like(dkv_ref)
        fill_span(range_ref, span_ref, k0, (k1, k2, k3, k4))
        flip_span(span_ref, kt_ref, 0)

    qs = split_heads(q_ref[...])
    dos = split_heads(do_ref[...])
    qcat = jnp.concatenate(qs, axis=0)
    docat = jnp.concatenate(dos, axis=0)
    dm = (do_ref[...].astype(f32) * o_ref[...]).T
    delta = [jnp.sum(dm[64 * e : 64 * e + 64], axis=0, keepdims=True) for e in range(2)]

    first, count = range_ref[0, qi], range_ref[1, qi]

    def tile(t, carry):
        at = pl.ds(pl.multiple_of((first + t * (KT // 128)) * 128, 128), KT)
        same = same_segment(kseg_ref, qseg_ref, at)
        k = span_ref[at, 0:128]
        v = span_ref[at, 128:256]
        ps, dss, out = [], [], []
        for e in range(2):
            dims = (((1,), (1,)), ((), ()))
            s = lax.dot_general(k, qs[e], dims, preferred_element_type=f32)
            p = jnp.exp(jnp.where(same, s - lse_ref[e : e + 1, :], NEG))
            dp = lax.dot_general(v, dos[e], dims, preferred_element_type=f32)
            ds = (p * (dp - delta[e])).astype(bf16)
            kt = kt_ref[64 * e : 64 * e + 64, at]
            out.append(carry[e] + jnp.dot(kt, ds, preferred_element_type=f32))
            ps.append(p.astype(bf16))
            dss.append(ds)
        dkv_ref[at, 0:128] += jnp.dot(jnp.concatenate(dss, axis=1), qcat, preferred_element_type=f32)
        dkv_ref[at, 128:256] += jnp.dot(jnp.concatenate(ps, axis=1), docat, preferred_element_type=f32)
        return tuple(out)

    zero = jnp.zeros((64, QT_BACK), f32)
    dqt = lax.fori_loop(0, count, tile, (zero, zero))
    dq = jnp.concatenate(dqt, axis=0).T
    dq_ref[...] = dq.astype(bf16) * jnp.asarray(0.125, bf16)

    @pl.when(qi == last)
    def _():
        for at, far in zip(spots(range_ref), (f1, f2, f3, f4)):
            far[...] = dkv_ref[pl.ds(at, far.shape[0]), :].astype(bf16)
        own_ref[...] = dkv_ref[REACH : REACH + ROWS, :]


def attend_back(plan, h, q, pieces, d_att, mixed, lse):
    _, ranges, qseg, kseg = plan
    rowspec = pl.BlockSpec((QT_BACK, 128), lambda i: (i, 0))
    colspec = pl.BlockSpec((QT_BACK, 128), lambda i: (i, h))
    return pl.pallas_call(
        backward_kernel,
        grid=(ROWS // QT_BACK,),
        out_shape=(
            jax.ShapeDtypeStruct((ROWS, 128), bf16),
            jax.ShapeDtypeStruct((ROWS, 256), f32),
        )
        + tuple(jax.ShapeDtypeStruct((n, 256), bf16) for n in (ROWS, ROWS, NEAR, NEAR)),
        in_specs=[
            pl.BlockSpec(memory_space=pltpu.SMEM),
            pl.BlockSpec((8, QT_BACK), lambda i: (0, i)),
            pl.BlockSpec((SPAN, 128), lambda i: (0, 0)),
            colspec,
        ]
        + piece_specs(h, pieces)
        + [colspec, rowspec, pl.BlockSpec((8, QT_BACK), lambda i: (0, i))],
        out_specs=(
            rowspec,
            pl.BlockSpec((ROWS, 256), lambda i: (0, 0)),
        )
        + tuple(pl.BlockSpec((n, 256), lambda i: (0, 0)) for n in (ROWS, ROWS, NEAR, NEAR)),
        scratch_shapes=[
            pltpu.VMEM((SPAN, 256), bf16),
            pltpu.VMEM((128, SPAN), bf16),
            pltpu.VMEM((SPAN, 256), f32),
        ],
        compiler_params=pltpu.CompilerParams(vmem_limit_bytes=VLIM),
        cost_estimate=pl.CostEstimate(flops=8_000_000_000, bytes_accessed=12_000_000, transcendentals=0),
        name="attention_backward",
    )(ranges, qseg, kseg, q, *pieces, d_att, mixed, lse)


def exchange(part):
    return lax.ppermute(part, "heads", [(0, 1), (1, 0)])


def pair_sum(part):
    half = part.astype(bf16)
    return half.astype(f32) + exchange(half).astype(f32)


def side_by_side(own, other, index):
    return jnp.where(
        index == 0,
        jnp.concatenate([own, other], axis=1),
        jnp.concatenate([other, own], axis=1),
    )


def passed(block, distance):
    count = lax.axis_size("seq")
    route = [(i - distance, i) for i in range(count) if 0 <= i - distance < count]
    return lax.ppermute(block, "seq", route)


def across_cores(block):
    return lax.ppermute(block, "seq", [(i, i ^ 1) for i in range(lax.axis_size("seq"))])


def across_chips(block):
    count = lax.axis_size("seq")
    route = [(i, i + 1 if i % 2 else i - 1) for i in range(count)]
    return lax.ppermute(block, "seq", [(i, j) for i, j in route if 0 <= j < count])


def chip_along(block, step):
    count = lax.axis_size("seq")
    route = [(i, i - 2 * step if i % 2 else i + 2 * step) for i in range(count)]
    return lax.ppermute(block, "seq", [(i, j) for i, j in route if 0 <= j < count])


def layer_norm(values, gain, shift):
    centered = values - jnp.mean(values, axis=-1, keepdims=True)
    scale = lax.rsqrt(jnp.mean(centered * centered, axis=-1, keepdims=True) + EPSILON)
    return centered * scale * gain + shift


def gelu_exact(values):
    return jax.nn.gelu(values, approximate=False)


def nesterov(weight, grad, moment, average, rate):
    moment_new = 0.5 * moment + grad
    weight_new = weight - rate * (grad + 0.5 * moment_new)
    average_new = 0.5 * average + 0.5 * weight_new
    return (grad, weight_new, moment_new, average_new, weight_new.astype(bf16))


def dot(a, b, ca, cb):
    return lax.dot_general(a, b, (((ca,), (cb,)), ((), ())), preferred_element_type=f32)


def gathered(shard):
    return lax.all_gather(shard, "seq", axis=0, tiled=True)


def scattered(whole_sum):
    return lax.psum_scatter(whole_sum, "seq", scatter_dimension=0, tiled=True)


def body(
    frames,
    cotangent,
    lengths,
    kernel,
    kernel_moment,
    kernel_average,
    project,
    project_moment,
    project_average,
    combine,
    combine_moment,
    combine_average,
    expand,
    expand_moment,
    expand_average,
    shrink,
    shrink_moment,
    shrink_average,
    unitbias,
    unitbias_moment,
    unitbias_average,
    chanbias,
    chanbias_moment,
    chanbias_average,
    outbias,
    outbias_moment,
    outbias_average,
    normparams,
    normparams_moment,
    normparams_average,
):
    devices = lax.axis_size("seq")
    rows, width = frames.shape
    total = devices * rows
    first = lax.axis_index("seq") * rows
    index = lax.axis_index("heads")
    odd = lax.axis_index("seq") % 2
    local = project.shape[0]
    hidden_units = expand.shape[1]

    w_kernel = gathered(jnp.transpose(kernel, (2, 1, 0)).astype(bf16))
    small = jnp.concatenate(
        [unitbias, chanbias.reshape(-1), outbias.reshape(-1), normparams.reshape(-1)]
    ).astype(bf16)
    w_small = gathered(small[None])
    w_first = gathered(
        jnp.concatenate(
            [project[:, 0]]
            + [project[:, c, 128 * h : 128 * h + 128] for h in range(PAIRS) for c in (1, 2)]
            + [combine.T],
            axis=1,
        ).astype(bf16)
    )
    w_second = gathered(jnp.concatenate([expand, shrink.T], axis=1).astype(bf16))
    w_combine = w_first[:, 3 * HALF :]
    w_combine_far = exchange(w_combine)
    cuts = [unitbias.size, chanbias.size, outbias.size, normparams.size]
    parts, at = [], 0
    for size in cuts:
        parts.append(w_small[:, at : at + size].astype(f32))
        at += size
    b_unit = parts[0].reshape(-1)
    b_chan = jnp.transpose(parts[1].reshape(devices, 3, -1), (1, 0, 2)).reshape(3, -1)
    b_out = jnp.transpose(parts[2].reshape(devices, 2, -1), (1, 0, 2)).reshape(2, -1)
    norms = jnp.transpose(parts[3].reshape(devices, 3, 2, -1), (1, 2, 0, 3)).reshape(3, 2, -1)

    count = lengths.shape[0]
    order = jnp.arange(count, dtype=i32)
    ends = jnp.sum(jnp.where(order[None, :] <= order[:, None], lengths[None, :], 0), axis=1).astype(i32)
    starts = ends - lengths
    plan = block_plan(starts, ends, first)
    reach = attention_plan(starts, ends, first, odd)

    x_half = lax.dynamic_slice_in_dim(frames, index * HALF, HALF, 1).astype(bf16)
    window = jnp.concatenate(
        [passed(x_half[rows - HALO :], 1), x_half, passed(x_half[:HALO], -1)], axis=0
    )
    window, reach = lax.optimization_barrier((window, reach))
    ready = prepare(plan, window)
    conv_out, spread_taps = conv(plan, ready, w_kernel)
    pre = conv_out + b_chan[0]
    spread_part = gelu_exact(pre).astype(bf16)
    spread = side_by_side(spread_part, exchange(spread_part), index)
    h1, norm0_back = jax.vjp(layer_norm, frames + spread.astype(f32), norms[0, 0], norms[0, 1])
    h1_half = h1.astype(bf16)
    proj = dot(h1_half, w_first[:, : 3 * HALF], 1, 0)
    scale = HEAD ** (-0.5)
    queries = ((proj[:, :HALF] + b_chan[1]) * scale).astype(bf16)
    kv_bias = b_chan[2].reshape(PAIRS, 1, 128)
    kv_bias = jnp.concatenate([jnp.zeros_like(kv_bias), kv_bias], axis=1).reshape(-1)
    both = (proj[:, HALF:] + kv_bias).astype(bf16)
    near = NEAR

    def fetched(lo, hi):
        block = both[:, lo:hi]
        head, tail = block[:near], block[rows - near :]
        return (
            across_cores(block),
            across_chips(block),
            chip_along(jnp.where(odd == 1, head, tail), 1),
            chip_along(jnp.where(odd == 1, tail, head), -1),
        )

    early = fetched(0, 256)
    both, early = lax.optimization_barrier((both, early))
    late = fetched(256, 256 * PAIRS)
    pieces = [(both,) + (early if h == 0 else late) for h in range(PAIRS)]
    mixed, attended, attended_far, lse = [], [], [], []
    for h in range(PAIRS):
        q_part = queries
        if h == 1:
            q_part, w_combine_far = lax.optimization_barrier((queries, w_combine_far))
        if h >= 2:
            q_part, attended_far[h - 2] = lax.optimization_barrier((queries, attended_far[h - 2]))
        mixed_part, half, lse_part = attend(reach, h, q_part, pieces[h])
        mixed.append(mixed_part)
        lse.append(lse_part)
        attended.append(half)
        attended_far.append(exchange(half))
    attended = jnp.concatenate(attended, axis=1)
    attended_all = side_by_side(attended, jnp.concatenate(attended_far, axis=1), index)
    w_combine_all = side_by_side(w_combine, w_combine_far, index)
    w_expand = w_second[:, :hidden_units]
    w_shrink = w_second[:, hidden_units:]
    step = rows // CHUNKS
    cuts_of = [slice(c * step, (c + 1) * step) for c in range(CHUNKS)]
    first_half, second_half = [], []
    for cut in cuts_of:
        branch = dot(attended_all[cut], w_combine_all, 1, 1)
        h2, norm1_back = jax.vjp(layer_norm, h1[cut] + branch + b_out[0], norms[1, 0], norms[1, 1])
        h2_half = h2.astype(bf16)
        inner = dot(h2_half, w_expand, 1, 0) + b_unit
        hidden, gelu_inner_back = jax.vjp(gelu_exact, inner)
        hidden_half = hidden.astype(bf16)
        sent = dot(hidden_half, w_shrink, 1, 1).astype(bf16)
        first_half.append((h2, norm1_back, h2_half, gelu_inner_back, hidden_half, sent, exchange(sent)))
    sent_back = None
    for cut, (h2, norm1_back, h2_half, gelu_inner_back, hidden_half, sent, came) in zip(
        cuts_of, first_half
    ):
        if sent_back is not None:
            came, _ = lax.optimization_barrier((came, sent_back))
        outer = sent.astype(f32) + came.astype(f32)
        out_part, norm2_back = jax.vjp(layer_norm, h2 + outer + b_out[1], norms[2, 0], norms[2, 1])
        dx3, gain2_grad, shift2_grad = norm2_back(cotangent[cut])
        d_out = dx3.astype(bf16)
        d_hidden = dot(d_out, w_shrink, 1, 0)
        d_inner = gelu_inner_back(d_hidden)[0]
        d_inner_half = d_inner.astype(bf16)
        sent_back = dot(d_inner_half, w_expand, 1, 1).astype(bf16)
        sums = [gain2_grad, shift2_grad, jnp.sum(dx3, axis=0), jnp.sum(d_inner, axis=0)]
        second_half.append(
            [out_part, (sent_back, exchange(sent_back)), norm1_back, h2_half, d_inner_half, d_out, hidden_half, dx3, sums]
        )
    layer_out = jnp.concatenate([part[0] for part in second_half], axis=0)
    gain2_grad, shift2_grad, outer_bias_grad, unit_grad = map(sum, zip(*[p[-1] for p in second_half]))
    second_part = jnp.concatenate(
        [
            sum(dot(p[a], p[b], 0, 0) for p in second_half).astype(bf16)
            for a, b in ((3, 4), (5, 6))
        ],
        axis=1,
    )
    dx2_parts, gain1_parts, shift1_parts = zip(
        *[p[2](p[7] + (p[1][0].astype(f32) + p[1][1].astype(f32))) for p in second_half]
    )
    gain1_grad, shift1_grad = sum(gain1_parts), sum(shift1_parts)
    dx2 = jnp.concatenate(dx2_parts, axis=0)
    branch_bias_grad = jnp.sum(dx2, axis=0)
    d_branch = dx2.astype(bf16)
    d_att = dot(d_branch, w_combine, 1, 0).astype(bf16)
    d_att, second_part = lax.optimization_barrier((d_att, second_part))
    second_sum = scattered(second_part).astype(f32)
    dq_parts, kv_parts = [], []
    arrived = {}
    for h in range(PAIRS):
        d_part = d_att
        if h >= 2:
            two = arrived[h - 2][:2]
            d_part, two = lax.optimization_barrier((d_att, two))
            arrived[h - 2] = two + arrived[h - 2][2:]
        dq_part, own, core, chip, far, beyond = attend_back(
            reach, h, queries, pieces[h], d_part, mixed[h], lse[h]
        )
        arrived[h] = (
            across_cores(core),
            across_chips(chip),
            chip_along(far, -1),
            chip_along(beyond, 1),
            own,
        )
        dq_parts.append(dq_part)
    for h in range(PAIRS):
        core, chip, far, beyond, own = [a.astype(f32) for a in arrived[h]]
        ends_of = jnp.concatenate(
            [jnp.where(odd == 1, far, beyond), jnp.where(odd == 1, beyond, far)], axis=0
        )
        kv_parts.append((own + core + chip + ends_of).astype(bf16))
    dq_half = jnp.concatenate(dq_parts, axis=1)
    d_both_half = jnp.concatenate(kv_parts, axis=1)
    stacked = jnp.concatenate([dq_half, d_both_half], axis=1)
    query_bias_grad = jnp.sum(dq_half.astype(f32), axis=0)
    value_bias_grad = jnp.sum(
        d_both_half.astype(f32), axis=0
    ).reshape(PAIRS, 2, 128)[:, 1].reshape(-1)
    dh1_half = dot(stacked, w_first[:, : 3 * HALF], 1, 1).astype(bf16)
    dh1_half, second_sum = lax.optimization_barrier((dh1_half, second_sum))
    dh1 = dx2 + (dh1_half.astype(f32) + exchange(dh1_half).astype(f32))
    first_part = (
        jnp.concatenate(
            [dot(h1_half, stacked, 0, 0).astype(bf16), dot(d_branch, attended, 0, 0).astype(bf16)],
            axis=1,
        )
    )
    first_part, second_sum = lax.optimization_barrier((first_part, second_sum))
    first_sum = scattered(first_part).astype(f32)
    dx1, gain0_grad, shift0_grad = norm0_back(dh1)
    d_spread = lax.dynamic_slice_in_dim(dx1, index * HALF, HALF, 1)
    d_conv = jax.vjp(gelu_exact, pre)[1](d_spread)[0]
    conv_bias_grad = jnp.sum(d_conv, axis=0)
    d_conv_half = d_conv.astype(bf16)
    spread_out = lambda grad, lead: jnp.transpose(
        grad.reshape(lead, devices, -1), (1, 0, 2)
    ).reshape(devices, -1)
    small_part = jnp.concatenate(
            [
                unit_grad.reshape(devices, -1),
                spread_out(jnp.stack([conv_bias_grad, query_bias_grad, value_bias_grad]), 3),
                spread_out(jnp.stack([branch_bias_grad, outer_bias_grad]), 2),
                spread_out(
                    jnp.stack(
                        [gain0_grad, shift0_grad, gain1_grad, shift1_grad, gain2_grad, shift2_grad]
                    ),
                    6,
                ),
            ],
            axis=1,
        )
    small_part = jnp.pad(small_part, ((0, 0), (0, EXTRA * HALF - small_part.shape[1])))
    small_part = small_part.astype(bf16).reshape(devices, EXTRA, HALF)
    d_own = jnp.pad(d_conv_half, ((HALO, HALO), (0, 0)))
    tap_raw = tap_grad(plan, ready, d_own, small_part)
    tap_part, first_sum = lax.optimization_barrier((tap_raw, first_sum))
    tap_sum = scattered(tap_part)[0].astype(f32)
    kernel_sum = tap_sum[:-EXTRA].reshape(TAPS // devices, CG, HALF)
    small_sum = tap_sum[-EXTRA:].reshape(-1)
    d_rim = jnp.concatenate([d_conv_half[:HALO], d_conv_half[rows - HALO :]], axis=0)
    d_rim, _ = lax.optimization_barrier((d_rim, tap_raw))
    d_window = jnp.concatenate(
        [passed(d_rim[HALO:], 1), d_conv_half, passed(d_rim[:HALO], -1)], axis=0
    )
    d_input = conv_back(plan, ready, d_window, spread_taps).astype(bf16)
    frames_grad = dx1 + side_by_side(d_input, exchange(d_input), index).astype(f32)

    pieces, at = [], 0
    for size in cuts:
        pieces.append(small_sum[at : at + size])
        at += size
    unit_sum = pieces[0]
    chan_sum = pieces[1].reshape(chanbias.shape)
    out_sum = pieces[2].reshape(outbias.shape)
    norm_sum = pieces[3].reshape(normparams.shape)
    kv_sum = first_sum[:, HALF : 3 * HALF].reshape(local, PAIRS, 2, 128)
    project_sum = jnp.stack(
        [first_sum[:, :HALF]] + [kv_sum[:, :, c].reshape(local, HALF) for c in range(2)], axis=1
    )

    root = total**0.5
    small_rate = 0.1 / root
    out = [layer_out, frames_grad]
    for weight, grad, moment, average, rate in (
        (kernel, jnp.transpose(kernel_sum, (2, 1, 0)), kernel_moment, kernel_average, (CG * TAPS) ** (-0.5) / root),
        (project, project_sum, project_moment, project_average, width ** (-0.5) / root),
        (combine, first_sum[:, 3 * HALF :].T, combine_moment, combine_average, (width // 16) ** (-0.5) / root),
        (expand, second_sum[:, :hidden_units], expand_moment, expand_average, width ** (-0.5) / root),
        (shrink, second_sum[:, hidden_units:].T, shrink_moment, shrink_average, (2 * hidden_units) ** (-0.5) / root),
        (unitbias, unit_sum, unitbias_moment, unitbias_average, 0.5 / root),
        (chanbias, chan_sum, chanbias_moment, chanbias_average, small_rate),
        (outbias, out_sum, outbias_moment, outbias_average, small_rate),
        (normparams, norm_sum, normparams_moment, normparams_average, small_rate),
    ):
        out.extend(nesterov(weight, grad, moment, average, rate))
    return tuple(out)


def solution(mesh):
    kernel_spec = P("heads", None, "seq")
    project_spec = P("seq", None, "heads")
    tall = P("heads", "seq")
    wide = P("seq", "heads")
    unit = P(("heads", "seq"))
    chan = P(None, ("heads", "seq"))
    outb = P(None, "seq")
    norm = P(None, None, "seq")
    weights = (kernel_spec, project_spec, tall, wide, tall, unit, chan, outb, norm)
    rows = P("seq", None)
    return jax.shard_map(
        body,
        mesh=mesh,
        in_specs=(rows, rows, P()) + tuple(s for s in weights for _ in range(3)),
        out_specs=(rows, rows) + tuple(s for s in weights for _ in range(5)),
        check_vma=False,
    )
```

```python
import functools

import jax
import jax.numpy as jnp
from jax import lax
from jax.experimental import pallas as pl
from jax.experimental.pallas import tpu as pltpu
from jax.sharding import PartitionSpec as P

HEAD = 64
PAIRS = 3
CHUNKS = 2
EPSILON = 1e-05

bf16, f32, i32 = jnp.bfloat16, jnp.float32, jnp.int32
CG, TAPS, GROUPS, HALO = 48, 128, 8, 64
ROWS, WIN, HALF = 1024, 1152, 384
CM, XM = 272, 304
NQ = 33
PJ = 134
EXTRA = 16
VLIM = 58 << 20


def iota(shape, dim):
    return lax.broadcasted_iota(i32, shape, dim)


def block_plan(starts, ends, first):
    w0 = first - HALO
    b = jnp.clip(starts - w0, 0, WIN)
    e = jnp.clip(ends - w0, 0, WIN)
    nblk = (e - b + 3) // 4
    n = starts.shape[0]
    before = jnp.arange(n)[None, :] < jnp.arange(n)[:, None]
    bs = jnp.sum(jnp.where(before, nblk[None, :], 0), axis=1).astype(i32)
    bs = bs + (jnp.clip(-w0, 0, WIN) + 3) // 4
    w = jnp.arange(WIN, dtype=i32)
    inside = (b[None, :] <= w[:, None]) & (w[:, None] < e[None, :])
    p = jnp.sum(jnp.where(inside, 4 * bs - b + w[:, None] + 1, 0), axis=1).astype(i32) - 1
    most = min(WIN, WIN // 4 + n)
    maxc = -((16 - most) // CM)
    lcap = CM * (maxc - 1) + XM
    m = jnp.arange(lcap, dtype=i32)
    hit = (bs[None, :] <= m[:, None]) & (m[:, None] < (bs + nblk)[None, :])
    bseg = jnp.sum(jnp.where(hit, jnp.arange(1, n + 1, dtype=i32)[None, :], 0), axis=1).astype(i32) - 1
    chunks = jnp.maximum((p[HALO + ROWS - 1] // 4 - 16) // CM + 1, 1)
    return (
        jnp.reshape(chunks, (1,)).astype(i32),
        jnp.broadcast_to(p[None, :], (8, WIN)),
        jnp.broadcast_to(p[:, None], (WIN, 128)),
        jnp.broadcast_to(bseg[:, None], (lcap, 128)),
    )


def select_pair(h, rows, base):
    lane = iota((rows, 256), 1)
    src = CG * (2 * h + (lane >> 7)) + (lane & 63) - base
    ok = ((lane & 63) < CG) & (iota((rows, 256), 0) == src)
    return jnp.where(ok, 1.0, 0.0).astype(bf16)


def build_blocks(s_ref, dup):
    y = [jnp.dot(s_ref[0, t], dup, preferred_element_type=f32).astype(bf16) for t in range(4)]
    low = iota((XM, 128), 1) < 64
    out = []
    for g in range(2):
        tiles = [v[:, 128 * g : 128 * g + 128] for v in y]
        out.append(
            jnp.concatenate(
                [jnp.where(low, tiles[0], tiles[1]), jnp.where(low, tiles[2], tiles[3])], axis=1
            )
        )
    return out


def build_taps(k_ref, sel, p_ref, base_tile):
    p_ref[...] = jnp.zeros_like(p_ref)
    step = 16
    for j0 in range(0, TAPS, step):
        part = k_ref[pl.ds(j0, step), :, pl.ds(pl.multiple_of(base_tile * 128, 128), 256)]
        d = jnp.dot(part.reshape(step * CG, 256), sel, preferred_element_type=f32)
        d = d.astype(bf16).reshape(step, CG, 256)
        for g in range(2):
            p_ref[g, pl.ds(j0 + 2, step), 0:CG, 0:64] = d[:, :, 128 * g : 128 * g + 64]
            p_ref[g, pl.ds(j0 + 3, step), 0:CG, 64:128] = d[:, :, 128 * g + 64 : 128 * g + 128]


def pair_lanes(h):
    base_tile = h >> 1
    return base_tile, pl.ds(pl.multiple_of(base_tile * 128, 128), 256)


def prepare_kernel(n_ref, *refs):
    @pl.when(pl.program_id(0) < n_ref[0])
    def _():
        prepare_chunk(pl.program_id(0), *refs)


def prepare_chunk(c, prow_ref, pcol_ref, bseg_ref, x_ref, s_ref, r_ref, mask_ref, tmask_ref, xb_ref, xt_ref):
    prow = prow_ref[0:1, :]
    for t in range(4):
        pos = 4 * (iota((XM, WIN), 0) + CM * c) + t
        s_ref[0, t] = jnp.where(pos == prow, 1.0, 0.0).astype(bf16)
    pcol = pcol_ref[HALO : HALO + ROWS, :]
    lane = iota((ROWS, 4 * CM), 1)
    phase = sum([(lane >= CM * t).astype(i32) for t in range(1, 4)])
    spot = 4 * (16 + CM * c) + 4 * lane - (4 * CM - 1) * phase
    wide = jnp.concatenate([pcol] * 9, axis=1)[:, : 4 * CM]
    r_ref[0] = jnp.where(wide == spot, 1.0, 0.0).astype(bf16)
    seg = bseg_ref[pl.ds(pl.multiple_of(CM * c, 16), XM), :]
    none = jnp.full((32, 128), -7, i32)
    own = jnp.concatenate([none, seg[16 : 16 + CM], none], axis=0)
    for q in range(NQ):
        same = seg[q : q + CM] == seg[16 : 16 + CM]
        mask_ref[0, q] = jnp.where(same, 1.0, 0.0).astype(bf16)
        same = seg == own[32 - q : 32 - q + XM]
        tmask_ref[0, q] = jnp.where(same, 1.0, 0.0).astype(bf16)
    for h in range(4):
        base = 128 * (h // 2)
        sel = select_pair(h, 256, base)
        dup = jnp.dot(x_ref[:, base : base + 256], sel, preferred_element_type=f32).astype(bf16)
        for g, block in enumerate(build_blocks(s_ref, dup)):
            xb_ref[0, 2 * h + g] = block
            xt_ref[0, 2 * h + g] = block.T


def fixed(shape):
    return pl.BlockSpec(shape, lambda *_: (0,) * len(shape))


def chunk_count(plan):
    return (plan[3].shape[0] - XM) // CM + 1


def call(kernel, name, grid, plan, in_specs, out_specs, out_shape, scratch, flops, args):
    return pl.pallas_call(
        kernel,
        grid_spec=pltpu.PrefetchScalarGridSpec(
            num_scalar_prefetch=1,
            grid=grid,
            in_specs=in_specs,
            out_specs=out_specs,
            scratch_shapes=scratch,
        ),
        out_shape=out_shape,
        compiler_params=pltpu.CompilerParams(vmem_limit_bytes=VLIM),
        cost_estimate=pl.CostEstimate(flops=flops, bytes_accessed=15_000_000, transcendentals=0),
        name=name,
    )(plan[0], *args)


def prepare(plan, window):
    chunks, prow, pcol, bseg = plan
    shapes = ((4, XM, WIN), (ROWS, 4 * CM), (NQ, CM, 128), (NQ, XM, 128), (8, XM, 256), (8, 256, XM))
    maxc = chunk_count(plan)
    return call(
        prepare_kernel,
        "conv_prepare",
        (maxc,),
        plan,
        [fixed(a.shape) for a in (prow, pcol, bseg, window)],
        tuple(
            pl.BlockSpec((1,) + s, lambda c, n, k=len(s): (jnp.minimum(c, n[0] - 1),) + (0,) * k)
            for s in shapes
        ),
        tuple(jax.ShapeDtypeStruct((maxc,) + s, bf16) for s in shapes),
        [],
        10_000_000_000,
        (prow, pcol, bseg, window),
    )


def conv_forward_kernel(n_ref, *refs):
    c, h = pl.program_id(0), pl.program_id(1)

    @pl.when(c < n_ref[0])
    def _():
        conv_chunk(False, c, h, *refs)


def conv_back_kernel(n_ref, d_ref, s_ref, *refs):
    c, h = pl.program_id(0), pl.program_id(1)

    @pl.when(c < n_ref[0])
    def _():
        conv_chunk(True, c, h, (d_ref, s_ref), *refs)


def conv_chunk(back, c, h, x_ref, mask_ref, r_ref, k_ref, out_ref, *rest):
    base_tile, lanes = pair_lanes(h)
    if back:
        s_ref, (xb_ref, o_ref) = x_ref[1], rest
        p_ref = k_ref
        sel = select_pair(h, 256, 128 * base_tile)
        dup = jnp.dot(x_ref[0][:, lanes], sel, preferred_element_type=f32).astype(bf16)
        for g, block in enumerate(build_blocks(s_ref, dup)):
            xb_ref[0, g] = block
    else:
        xb_ref = x_ref
        p_ref, o_ref = rest
        build_taps(k_ref, select_pair(h, 256, 128 * base_tile), p_ref, base_tile)

    @pl.when(h == 0)
    def _():
        o_ref[...] = jnp.zeros_like(o_ref)

    total = [jnp.zeros((CM, 256), f32) for _ in range(4)]
    for g in range(2):
        acc = jnp.zeros((CM, 256), f32)
        for q in range(NQ):
            m = mask_ref[0, q]
            xs = xb_ref[0, g, q : q + CM, :] * jnp.concatenate([m, m], axis=1)
            if back:
                a, b = 130 - 4 * q, 128 - 4 * q
            else:
                a, b = 4 * q + 2, 4 * q
            w = jnp.concatenate(
                [p_ref[g, a : a + 4].reshape(256, 128), p_ref[g, b : b + 4].reshape(256, 128)],
                axis=1,
            )
            dims = (((1,), (1 if back else 0,)), ((), ()))
            acc = acc + lax.dot_general(xs, w, dims, preferred_element_type=f32)
        acc = acc.astype(bf16)
        row = iota((256, 256), 0)
        target = CG * (2 * h + g) - 128 * base_tile + (row & 63)
        hit = ((row & 63) < CG) & (iota((256, 256), 1) == target)
        for t in range(4):
            fold = jnp.where(hit & ((row >> 6) == t), 1.0, 0.0).astype(bf16)
            total[t] = total[t] + jnp.dot(acc, fold, preferred_element_type=f32)
    for t in range(4):
        o_ref[CM * t : CM * t + CM, lanes] += total[t].astype(bf16)

    @pl.when(h == 3)
    def _():
        y = jnp.dot(r_ref[0], o_ref[...], preferred_element_type=f32)

        @pl.when(c == 0)
        def _():
            out_ref[...] = y

        @pl.when(c > 0)
        def _():
            out_ref[...] += y


def by_chunk(shape):
    return pl.BlockSpec(
        (1,) + shape, lambda c, h, n: (jnp.minimum(c, n[0] - 1),) + (0,) * len(shape)
    )


def by_pair(shape):
    return pl.BlockSpec(
        (2,) + shape, lambda c, h, n: (jnp.where(c < n[0], h, 3),) + (0,) * len(shape)
    )


def conv(plan, ready, taps):
    _, r, mask, _, xb, _ = ready
    x_spec = pl.BlockSpec(
        (1, 2, XM, 256),
        lambda c, h, n: (jnp.minimum(c, n[0] - 1), jnp.where(c < n[0], h, 3), 0, 0),
    )
    return call(
        conv_forward_kernel,
        "conv_forward",
        (chunk_count(plan), 4),
        plan,
        [x_spec, by_chunk((NQ, CM, 128)), by_chunk((ROWS, 4 * CM)), fixed((TAPS, CG, HALF))],
        (fixed((ROWS, HALF)), by_pair((PJ, 64, 128))),
        (
            jax.ShapeDtypeStruct((ROWS, HALF), f32),
            jax.ShapeDtypeStruct((8, PJ, 64, 128), bf16),
        ),
        [pltpu.VMEM((4 * CM, HALF), bf16)],
        25_000_000_000,
        (xb, mask, r, taps),
    )


def conv_back(plan, ready, window, spread_taps):
    s, r, mask, _, _, _ = ready
    return call(
        conv_back_kernel,
        "conv_back",
        (chunk_count(plan), 4),
        plan,
        [
            fixed((WIN, HALF)),
            by_chunk((4, XM, WIN)),
            by_chunk((NQ, CM, 128)),
            by_chunk((ROWS, 4 * CM)),
            by_pair((PJ, 64, 128)),
        ],
        fixed((ROWS, HALF)),
        jax.ShapeDtypeStruct((ROWS, HALF), f32),
        [pltpu.VMEM((1, 2, XM, 256), bf16), pltpu.VMEM((4 * CM, HALF), bf16)],
        25_000_000_000,
        (window, s, mask, r, spread_taps),
    )


def tap_grad_kernel(n_ref, xt_ref, s_ref, mask_ref, d_ref, small_ref, out_ref, dp_ref, acc_ref, sum_ref):
    h, c = pl.program_id(0), pl.program_id(1)
    base_tile, lanes = pair_lanes(h)

    @pl.when((h == 0) & (c == 0))
    def _():
        out_ref[...] = jnp.zeros_like(out_ref)
        out_ref[:, out_ref.shape[1] - EXTRA :, :] = small_ref[...]
        dp_ref[...] = jnp.zeros_like(dp_ref)

    @pl.when(c < n_ref[0])
    def _():
        sel = select_pair(h, 256, 128 * base_tile)
        ddup = jnp.dot(d_ref[:, lanes], sel, preferred_element_type=f32).astype(bf16)
        for g, block in enumerate(build_blocks(s_ref, ddup)):
            dp_ref[g, 32 : 32 + CM, :] = block[16 : 16 + CM]
        for g in range(2):
            carry = jnp.zeros((128, 128), f32)
            for q in range(NQ):
                m = mask_ref[0, q]
                ds = dp_ref[g, 32 - q : 32 - q + XM, :] * jnp.concatenate([m, m], axis=1)
                part = jnp.dot(xt_ref[0, g], ds, preferred_element_type=f32)
                left, right = part[:, 0:128], part[:, 128:256]
                acc_ref[g, 4 * q : 4 * q + 2] = (right[0:128] + carry).reshape(2, 64, 128)
                acc_ref[g, 4 * q + 2 : 4 * q + 4] = (left[0:128] + right[128:256]).reshape(2, 64, 128)
                carry = left[128:256]
            acc_ref[g, 4 * NQ : 4 * NQ + 2] = carry.reshape(2, 64, 128)

        @pl.when(c > 0)
        def _():
            acc_ref[...] += sum_ref[...]

        @pl.when(c < n_ref[0] - 1)
        def _():
            sum_ref[...] = acc_ref[...]

    @pl.when(c == pl.num_programs(1) - 1)
    def _():
        per = TAPS // out_ref.shape[0]
        low = iota((1, 1, 128), 2) < 64
        row = iota((128, 256), 0)
        src = CG * (2 * h + (row >> 6)) + (row & 63) - 128 * base_tile
        back = jnp.where(((row & 63) < CG) & (iota((128, 256), 1) == src), 1.0, 0.0).astype(bf16)
        step = 16
        for j0 in range(0, TAPS, step):
            now = [acc_ref[g, j0 + 2 : j0 + 2 + step, 0:CG, :] for g in range(2)]
            nxt = [acc_ref[g, j0 + 3 : j0 + 3 + step, 0:CG, :] for g in range(2)]
            here = jnp.where(low, now[0], nxt[1]).reshape(step * CG, 128)
            far = jnp.where(low, now[1], nxt[0]).reshape(step * CG, 128)
            both = (here + pltpu.roll(far, 64, 1)).astype(bf16)
            o = jnp.dot(both, back, preferred_element_type=f32).astype(bf16)
            o = o.reshape(step // per, per * CG, 256)
            out_ref[j0 // per : (j0 + step) // per, 0 : per * CG, lanes] += o


def tap_grad(plan, ready, d_own, small):
    s, _, _, tmask, _, xt = ready
    devices = small.shape[0]
    shape = (devices, TAPS // devices * CG + EXTRA, HALF)
    chunked = lambda sh: pl.BlockSpec(
        (1,) + sh, lambda h, c, n: (jnp.minimum(c, n[0] - 1),) + (0,) * len(sh)
    )
    x_spec = pl.BlockSpec((1, 2, 256, XM), lambda h, c, n: (jnp.minimum(c, n[0] - 1), h, 0, 0))
    return call(
        tap_grad_kernel,
        "tap_gradient",
        (4, chunk_count(plan)),
        plan,
        [
            x_spec,
            chunked((4, XM, WIN)),
            chunked((NQ, XM, 128)),
            fixed((WIN, HALF)),
            fixed(small.shape),
        ],
        fixed(shape),
        jax.ShapeDtypeStruct(shape, bf16),
        [
            pltpu.VMEM((2, 32 + CM + 32, 256), bf16),
            pltpu.VMEM((2, PJ, 64, 128), f32),
            pltpu.VMEM((2, PJ, 64, 128), f32),
        ],
        1_000_000_000,
        (xt, s, tmask, d_own, small),
    )
REACH = 1536
SPAN = ROWS + 2 * REACH
QT_AHEAD, QT_BACK, KT = 512, 256, 1664
NEAR = REACH - ROWS
NEG = -1e30


def segment_count(ends, positions):
    return jnp.sum((ends[None, :] <= positions[:, None]).astype(i32), axis=1).astype(i32)

def attention_plan(starts, ends, first, odd):
    w = first - REACH + jnp.arange(SPAN, dtype=i32)
    kseg = segment_count(ends, w)
    kseg = jnp.where(w < 0, -1, kseg)
    qseg = kseg[REACH : REACH + ROWS]
    n = jnp.arange(starts.shape[0], dtype=i32)

    def tiles_of(rows):
        edge = qseg.reshape(ROWS // rows, rows)
        head = jnp.sum(jnp.where(n[None] == edge[:, :1], starts[None], 0), axis=1) - (first - REACH)
        tail = jnp.sum(jnp.where(n[None] == edge[:, -1:], ends[None], 0), axis=1) - (first - REACH)
        lo = jnp.clip(head // 128, 0, SPAN // 128)
        hi = jnp.clip((tail + 127) // 128, 1, SPAN // 128)
        tiles = jnp.maximum((hi - lo + KT // 128 - 1) // (KT // 128), 1)
        lo = jnp.minimum(lo, SPAN // 128 - tiles * (KT // 128))
        return jnp.stack([lo, tiles, jnp.full_like(lo, odd)]).astype(i32)

    return (
        tiles_of(QT_AHEAD),
        tiles_of(QT_BACK),
        jnp.broadcast_to(qseg[None], (8, ROWS)),
        jnp.broadcast_to(kseg[:, None], (SPAN, 128)),
    )


def split_heads(a):
    low = iota(a.shape, 1) < 64
    zero = jnp.zeros((), a.dtype)
    return jnp.where(low, a, zero), jnp.where(low, zero, a)

def spots(range_ref):
    odd = range_ref[2, 0] == 1
    right, end = REACH + ROWS, SPAN - NEAR
    at = [
        jnp.where(odd, NEAR, right),
        jnp.where(odd, right, NEAR),
        jnp.where(odd, end, 0),
        jnp.where(odd, 0, end),
    ]
    return [pl.multiple_of(x, NEAR) for x in at]


def fill_span(range_ref, span_ref, own, others):
    span_ref[REACH : REACH + ROWS, :] = own[...]
    for at, piece in zip(spots(range_ref), others):
        span_ref[pl.ds(at, piece.shape[0]), :] = piece[...]


def flip_span(src_ref, dst_ref, lane):
    for at in range(0, SPAN, 512):
        dst_ref[:, at : at + 512] = src_ref[at : at + 512, lane : lane + 128].T


def same_segment(kseg_ref, qseg_ref, at):
    ks = kseg_ref[at, :]
    ks = jnp.concatenate([ks] * (qseg_ref.shape[1] // 128), axis=1)
    return ks == qseg_ref[0:1, :]


def forward_kernel(range_ref, qseg_ref, kseg_ref, q_ref, k0, k1, k2, k3, k4, o_ref, half_ref, lse_ref, span_ref, vt_ref):
    qi = pl.program_id(0)

    @pl.when(qi == 0)
    def _():
        fill_span(range_ref, span_ref, k0, (k1, k2, k3, k4))
        flip_span(span_ref, vt_ref, 128)

    qs = split_heads(q_ref[...])

    first, count = range_ref[0, qi], range_ref[1, qi]

    def tile(t, carry):
        at = pl.ds(pl.multiple_of((first + t * (KT // 128)) * 128, 128), KT)
        same = same_segment(kseg_ref, qseg_ref, at)
        k = span_ref[at, 0:128]
        out = []
        for e in range(2):
            m, l, acc = carry[e]
            s = lax.dot_general(k, qs[e], (((1,), (1,)), ((), ())), preferred_element_type=f32)
            s = jnp.where(same, s, NEG)
            new = jnp.maximum(m, jnp.max(s, axis=0, keepdims=True))
            p = jnp.exp(s - new)
            alpha = jnp.exp(m - new)
            l = l * alpha + jnp.sum(p, axis=0, keepdims=True)
            vt = vt_ref[64 * e : 64 * e + 64, at]
            acc = acc * alpha + jnp.dot(vt, p.astype(bf16), preferred_element_type=f32)
            out.append((new, l, acc))
        return tuple(out)

    start = (jnp.full((1, QT_AHEAD), NEG, f32), jnp.zeros((1, QT_AHEAD), f32), jnp.zeros((64, QT_AHEAD), f32))
    ends = lax.fori_loop(0, count, tile, (start, start))
    o = jnp.concatenate([acc / l for _, l, acc in ends], axis=0).T
    o_ref[...] = o
    half_ref[...] = o.astype(bf16)
    for e in range(2):
        lse_ref[e : e + 1, :] = ends[e][0] + jnp.log(ends[e][1])


def piece_specs(h, pieces):
    at = [h - (PAIRS - p.shape[1] // 256) if p.shape[1] > 256 else 0 for p in pieces]
    return [pl.BlockSpec((p.shape[0], 256), lambda i, c=c: (0, c)) for p, c in zip(pieces, at)]


def attend(plan, h, q, pieces):
    ranges, _, qseg, kseg = plan
    return pl.pallas_call(
        forward_kernel,
        grid=(ROWS // QT_AHEAD,),
        out_shape=(
            jax.ShapeDtypeStruct((ROWS, 128), f32),
            jax.ShapeDtypeStruct((ROWS, 128), bf16),
            jax.ShapeDtypeStruct((8, ROWS), f32),
        ),
        in_specs=[
            pl.BlockSpec(memory_space=pltpu.SMEM),
            pl.BlockSpec((8, QT_AHEAD), lambda i: (0, i)),
            pl.BlockSpec((SPAN, 128), lambda i: (0, 0)),
            pl.BlockSpec((QT_AHEAD, 128), lambda i: (i, h)),
        ]
        + piece_specs(h, pieces),
        out_specs=(
            pl.BlockSpec((QT_AHEAD, 128), lambda i: (i, 0)),
            pl.BlockSpec((QT_AHEAD, 128), lambda i: (i, 0)),
            pl.BlockSpec((8, QT_AHEAD), lambda i: (0, i)),
        ),
        scratch_shapes=[pltpu.VMEM((SPAN, 256), bf16), pltpu.VMEM((128, SPAN), bf16)],
        compiler_params=pltpu.CompilerParams(vmem_limit_bytes=VLIM),
        cost_estimate=pl.CostEstimate(flops=8_000_000_000, bytes_accessed=8_000_000, transcendentals=0),
        name="attention_forward",
    )(ranges, qseg, kseg, q, *pieces)


def backward_kernel(range_ref, qseg_ref, kseg_ref, q_ref, k0, k1, k2, k3, k4, do_ref, o_ref, lse_ref,
                    dq_ref, own_ref, f1, f2, f3, f4, span_ref, kt_ref, dkv_ref):
    qi = pl.program_id(0)
    last = ROWS // QT_BACK - 1

    @pl.when(qi == 0)
    def _():
        dkv_ref[...] = jnp.zeros_like(dkv_ref)
        fill_span(range_ref, span_ref, k0, (k1, k2, k3, k4))
        flip_span(span_ref, kt_ref, 0)

    qs = split_heads(q_ref[...])
    dos = split_heads(do_ref[...])
    qcat = jnp.concatenate(qs, axis=0)
    docat = jnp.concatenate(dos, axis=0)
    dm = (do_ref[...].astype(f32) * o_ref[...]).T
    delta = [jnp.sum(dm[64 * e : 64 * e + 64], axis=0, keepdims=True) for e in range(2)]

    first, count = range_ref[0, qi], range_ref[1, qi]

    def tile(t, carry):
        at = pl.ds(pl.multiple_of((first + t * (KT // 128)) * 128, 128), KT)
        same = same_segment(kseg_ref, qseg_ref, at)
        k = span_ref[at, 0:128]
        v = span_ref[at, 128:256]
        ps, dss, out = [], [], []
        for e in range(2):
            dims = (((1,), (1,)), ((), ()))
            s = lax.dot_general(k, qs[e], dims, preferred_element_type=f32)
            p = jnp.exp(jnp.where(same, s - lse_ref[e : e + 1, :], NEG))
            dp = lax.dot_general(v, dos[e], dims, preferred_element_type=f32)
            ds = (p * (dp - delta[e])).astype(bf16)
            kt = kt_ref[64 * e : 64 * e + 64, at]
            out.append(carry[e] + jnp.dot(kt, ds, preferred_element_type=f32))
            ps.append(p.astype(bf16))
            dss.append(ds)
        dkv_ref[at, 0:128] += jnp.dot(jnp.concatenate(dss, axis=1), qcat, preferred_element_type=f32)
        dkv_ref[at, 128:256] += jnp.dot(jnp.concatenate(ps, axis=1), docat, preferred_element_type=f32)
        return tuple(out)

    zero = jnp.zeros((64, QT_BACK), f32)
    dqt = lax.fori_loop(0, count, tile, (zero, zero))
    dq = jnp.concatenate(dqt, axis=0).T
    dq_ref[...] = dq.astype(bf16) * jnp.asarray(0.125, bf16)

    @pl.when(qi == last)
    def _():
        for at, far in zip(spots(range_ref), (f1, f2, f3, f4)):
            far[...] = dkv_ref[pl.ds(at, far.shape[0]), :].astype(bf16)
        own_ref[...] = dkv_ref[REACH : REACH + ROWS, :]


def attend_back(plan, h, q, pieces, d_att, mixed, lse):
    _, ranges, qseg, kseg = plan
    rowspec = pl.BlockSpec((QT_BACK, 128), lambda i: (i, 0))
    colspec = pl.BlockSpec((QT_BACK, 128), lambda i: (i, h))
    return pl.pallas_call(
        backward_kernel,
        grid=(ROWS // QT_BACK,),
        out_shape=(
            jax.ShapeDtypeStruct((ROWS, 128), bf16),
            jax.ShapeDtypeStruct((ROWS, 256), f32),
        )
        + tuple(jax.ShapeDtypeStruct((n, 256), bf16) for n in (ROWS, ROWS, NEAR, NEAR)),
        in_specs=[
            pl.BlockSpec(memory_space=pltpu.SMEM),
            pl.BlockSpec((8, QT_BACK), lambda i: (0, i)),
            pl.BlockSpec((SPAN, 128), lambda i: (0, 0)),
            colspec,
        ]
        + piece_specs(h, pieces)
        + [colspec, rowspec, pl.BlockSpec((8, QT_BACK), lambda i: (0, i))],
        out_specs=(
            rowspec,
            pl.BlockSpec((ROWS, 256), lambda i: (0, 0)),
        )
        + tuple(pl.BlockSpec((n, 256), lambda i: (0, 0)) for n in (ROWS, ROWS, NEAR, NEAR)),
        scratch_shapes=[
            pltpu.VMEM((SPAN, 256), bf16),
            pltpu.VMEM((128, SPAN), bf16),
            pltpu.VMEM((SPAN, 256), f32),
        ],
        compiler_params=pltpu.CompilerParams(vmem_limit_bytes=VLIM),
        cost_estimate=pl.CostEstimate(flops=8_000_000_000, bytes_accessed=12_000_000, transcendentals=0),
        name="attention_backward",
    )(ranges, qseg, kseg, q, *pieces, d_att, mixed, lse)


def exchange(part):
    return lax.ppermute(part, "heads", [(0, 1), (1, 0)])


def pair_sum(part):
    half = part.astype(bf16)
    return half.astype(f32) + exchange(half).astype(f32)


def side_by_side(own, other, index):
    return jnp.where(
        index == 0,
        jnp.concatenate([own, other], axis=1),
        jnp.concatenate([other, own], axis=1),
    )


def passed(block, distance):
    count = lax.axis_size("seq")
    route = [(i - distance, i) for i in range(count) if 0 <= i - distance < count]
    return lax.ppermute(block, "seq", route)


def across_cores(block):
    return lax.ppermute(block, "seq", [(i, i ^ 1) for i in range(lax.axis_size("seq"))])


def across_chips(block):
    count = lax.axis_size("seq")
    route = [(i, i + 1 if i % 2 else i - 1) for i in range(count)]
    return lax.ppermute(block, "seq", [(i, j) for i, j in route if 0 <= j < count])


def chip_along(block, step):
    count = lax.axis_size("seq")
    route = [(i, i - 2 * step if i % 2 else i + 2 * step) for i in range(count)]
    return lax.ppermute(block, "seq", [(i, j) for i, j in route if 0 <= j < count])


def layer_norm(values, gain, shift):
    centered = values - jnp.mean(values, axis=-1, keepdims=True)
    scale = lax.rsqrt(jnp.mean(centered * centered, axis=-1, keepdims=True) + EPSILON)
    return centered * scale * gain + shift


def gelu_exact(values):
    return jax.nn.gelu(values, approximate=False)


def nesterov(weight, grad, moment, average, rate):
    moment_new = 0.5 * moment + grad
    weight_new = weight - rate * (grad + 0.5 * moment_new)
    average_new = 0.5 * average + 0.5 * weight_new
    return (grad, weight_new, moment_new, average_new, weight_new.astype(bf16))


def dot(a, b, ca, cb):
    return lax.dot_general(a, b, (((ca,), (cb,)), ((), ())), preferred_element_type=f32)


def gathered(shard):
    return lax.all_gather(shard, "seq", axis=0, tiled=True)


def scattered(whole_sum):
    return lax.psum_scatter(whole_sum, "seq", scatter_dimension=0, tiled=True)


def body(
    frames,
    cotangent,
    lengths,
    kernel,
    kernel_moment,
    kernel_average,
    project,
    project_moment,
    project_average,
    combine,
    combine_moment,
    combine_average,
    expand,
    expand_moment,
    expand_average,
    shrink,
    shrink_moment,
    shrink_average,
    unitbias,
    unitbias_moment,
    unitbias_average,
    chanbias,
    chanbias_moment,
    chanbias_average,
    outbias,
    outbias_moment,
    outbias_average,
    normparams,
    normparams_moment,
    normparams_average,
):
    devices = lax.axis_size("seq")
    rows, width = frames.shape
    total = devices * rows
    first = lax.axis_index("seq") * rows
    index = lax.axis_index("heads")
    odd = lax.axis_index("seq") % 2
    local = project.shape[0]
    hidden_units = expand.shape[1]

    w_kernel = gathered(jnp.transpose(kernel, (2, 1, 0)).astype(bf16))
    small = jnp.concatenate(
        [unitbias, chanbias.reshape(-1), outbias.reshape(-1), normparams.reshape(-1)]
    ).astype(bf16)
    w_small = gathered(small[None])
    w_first = gathered(
        jnp.concatenate(
            [project[:, 0]]
            + [project[:, c, 128 * h : 128 * h + 128] for h in range(PAIRS) for c in (1, 2)]
            + [combine.T],
            axis=1,
        ).astype(bf16)
    )
    w_second = gathered(jnp.concatenate([expand, shrink.T], axis=1).astype(bf16))
    w_combine = w_first[:, 3 * HALF :]
    cuts = [unitbias.size, chanbias.size, outbias.size, normparams.size]
    parts, at = [], 0
    for size in cuts:
        parts.append(w_small[:, at : at + size].astype(f32))
        at += size
    b_unit = parts[0].reshape(-1)
    b_chan = jnp.transpose(parts[1].reshape(devices, 3, -1), (1, 0, 2)).reshape(3, -1)
    b_out = jnp.transpose(parts[2].reshape(devices, 2, -1), (1, 0, 2)).reshape(2, -1)
    norms = jnp.transpose(parts[3].reshape(devices, 3, 2, -1), (1, 2, 0, 3)).reshape(3, 2, -1)

    count = lengths.shape[0]
    order = jnp.arange(count, dtype=i32)
    ends = jnp.sum(jnp.where(order[None, :] <= order[:, None], lengths[None, :], 0), axis=1).astype(i32)
    starts = ends - lengths
    plan = block_plan(starts, ends, first)
    reach = attention_plan(starts, ends, first, odd)

    x_half = lax.dynamic_slice_in_dim(frames, index * HALF, HALF, 1).astype(bf16)
    window = jnp.concatenate(
        [passed(x_half[rows - HALO :], 1), x_half, passed(x_half[:HALO], -1)], axis=0
    )
    window, reach = lax.optimization_barrier((window, reach))
    ready = prepare(plan, window)
    conv_out, spread_taps = conv(plan, ready, w_kernel)
    pre = conv_out + b_chan[0]
    step = rows // CHUNKS
    cuts_of = [slice(c * step, (c + 1) * step) for c in range(CHUNKS)]
    spread_parts = [gelu_exact(pre[cut]).astype(bf16) for cut in cuts_of]
    spread_came = [exchange(part) for part in spread_parts]
    h1_parts, norm0_backs, h1_halves = [], [], []
    for c, cut in enumerate(cuts_of):
        came = spread_came[c]
        if c:
            came, _ = lax.optimization_barrier((came, h1_halves[-1]))
        spread = side_by_side(spread_parts[c], came, index)
        h1, back = jax.vjp(layer_norm, frames[cut] + spread.astype(f32), norms[0, 0], norms[0, 1])
        h1_parts.append(h1)
        norm0_backs.append(back)
        h1_halves.append(h1.astype(bf16))
    h1_half = jnp.concatenate(h1_halves, axis=0)
    proj = dot(h1_half, w_first[:, : 3 * HALF], 1, 0)
    scale = HEAD ** (-0.5)
    queries = ((proj[:, :HALF] + b_chan[1]) * scale).astype(bf16)
    kv_bias = b_chan[2].reshape(PAIRS, 1, 128)
    kv_bias = jnp.concatenate([jnp.zeros_like(kv_bias), kv_bias], axis=1).reshape(-1)
    both = (proj[:, HALF:] + kv_bias).astype(bf16)
    near = NEAR
    w_combine_sent, queries = lax.optimization_barrier((w_combine, queries))
    w_combine_far = exchange(w_combine_sent)

    def fetched(lo, hi):
        block = both[:, lo:hi]
        head, tail = block[:near], block[rows - near :]
        beside = across_chips(block)
        shared = jnp.where(odd == 1, beside[:near], beside[rows - near :])
        return (
            across_cores(block),
            beside,
            chip_along(jnp.where(odd == 1, head, tail), 1),
            shared,
        )

    early = fetched(0, 256)
    early = early[:3] + (across_cores(early[3]),)
    both, early = lax.optimization_barrier((both, early))
    late = fetched(256, 256 * PAIRS)
    pieces = [(both,) + early]
    mixed, attended, attended_far, lse = [], [], [], []
    for h in range(PAIRS):
        q_part = queries
        if h == 1:
            q_part, w_combine_far = lax.optimization_barrier((queries, w_combine_far))
        if h >= 2:
            q_part, attended_far[h - 2] = lax.optimization_barrier((queries, attended_far[h - 2]))
        mixed_part, half, lse_part = attend(reach, h, q_part, pieces[h])
        mixed.append(mixed_part)
        lse.append(lse_part)
        attended.append(half)
        attended_far.append(exchange(half))
        if h == 0:
            shared, _ = lax.optimization_barrier((late[3], half))
            pieces += [(both,) + late[:3] + (across_cores(shared),)] * (PAIRS - 1)
    attended = jnp.concatenate(attended, axis=1)
    attended_all = side_by_side(attended, jnp.concatenate(attended_far, axis=1), index)
    w_combine_all = side_by_side(w_combine, w_combine_far, index)
    w_expand = w_second[:, :hidden_units]
    w_shrink = w_second[:, hidden_units:]
    first_half, second_half = [], []
    for cut, h1 in zip(cuts_of, h1_parts):
        branch = dot(attended_all[cut], w_combine_all, 1, 1)
        h2, norm1_back = jax.vjp(layer_norm, h1 + branch + b_out[0], norms[1, 0], norms[1, 1])
        h2_half = h2.astype(bf16)
        inner = dot(h2_half, w_expand, 1, 0) + b_unit
        hidden, gelu_inner_back = jax.vjp(gelu_exact, inner)
        hidden_half = hidden.astype(bf16)
        sent = dot(hidden_half, w_shrink, 1, 1).astype(bf16)
        first_half.append((h2, norm1_back, h2_half, gelu_inner_back, hidden_half, sent, exchange(sent)))
    sent_back = None
    for cut, (h2, norm1_back, h2_half, gelu_inner_back, hidden_half, sent, came) in zip(
        cuts_of, first_half
    ):
        if sent_back is not None:
            came, _ = lax.optimization_barrier((came, sent_back))
        outer = sent.astype(f32) + came.astype(f32)
        out_part, norm2_back = jax.vjp(layer_norm, h2 + outer + b_out[1], norms[2, 0], norms[2, 1])
        dx3, gain2_grad, shift2_grad = norm2_back(cotangent[cut])
        d_out = dx3.astype(bf16)
        d_hidden = dot(d_out, w_shrink, 1, 0)
        d_inner = gelu_inner_back(d_hidden)[0]
        d_inner_half = d_inner.astype(bf16)
        sent_back = dot(d_inner_half, w_expand, 1, 1).astype(bf16)
        sums = [gain2_grad, shift2_grad, jnp.sum(dx3, axis=0), jnp.sum(d_inner, axis=0)]
        second_half.append(
            [out_part, (sent_back, exchange(sent_back)), norm1_back, h2_half, d_inner_half, d_out, hidden_half, dx3, sums]
        )
    layer_out = jnp.concatenate([part[0] for part in second_half], axis=0)
    gain2_grad, shift2_grad, outer_bias_grad, unit_grad = map(sum, zip(*[p[-1] for p in second_half]))
    second_part = jnp.concatenate(
        [
            sum(dot(p[a], p[b], 0, 0) for p in second_half).astype(bf16)
            for a, b in ((3, 4), (5, 6))
        ],
        axis=1,
    )
    dx2_parts, gain1_parts, shift1_parts = zip(
        *[p[2](p[7] + (p[1][0].astype(f32) + p[1][1].astype(f32))) for p in second_half]
    )
    gain1_grad, shift1_grad = sum(gain1_parts), sum(shift1_parts)
    dx2 = jnp.concatenate(dx2_parts, axis=0)
    branch_bias_grad = jnp.sum(dx2, axis=0)
    d_branch = dx2.astype(bf16)
    d_att = dot(d_branch, w_combine, 1, 0).astype(bf16)
    d_att, second_part = lax.optimization_barrier((d_att, second_part))
    second_sum = scattered(second_part).astype(f32)
    dq_parts, kv_parts = [], []
    arrived = {}
    for h in range(PAIRS):
        d_part = d_att
        if h >= 2:
            two = arrived[h - 2][:2]
            d_part, two = lax.optimization_barrier((d_att, two))
            arrived[h - 2] = two + arrived[h - 2][2:]
        dq_part, own, core, chip, far, beyond = attend_back(
            reach, h, queries, pieces[h], d_part, mixed[h], lse[h]
        )
        arrived[h] = (
            across_cores(core),
            across_chips(chip),
            chip_along(far, -1),
            chip_along(beyond, 1),
            own,
        )
        dq_parts.append(dq_part)
    for h in range(PAIRS):
        core, chip, far, beyond, own = [a.astype(f32) for a in arrived[h]]
        ends_of = jnp.concatenate(
            [jnp.where(odd == 1, far, beyond), jnp.where(odd == 1, beyond, far)], axis=0
        )
        kv_parts.append((own + core + chip + ends_of).astype(bf16))
    dq_half = jnp.concatenate(dq_parts, axis=1)
    d_both_half = jnp.concatenate(kv_parts, axis=1)
    stacked = jnp.concatenate([dq_half, d_both_half], axis=1)
    query_bias_grad = jnp.sum(dq_half.astype(f32), axis=0)
    value_bias_grad = jnp.sum(
        d_both_half.astype(f32), axis=0
    ).reshape(PAIRS, 2, 128)[:, 1].reshape(-1)
    dh1_parts = [dot(stacked[cut], w_first[:, : 3 * HALF], 1, 1).astype(bf16) for cut in cuts_of]
    dh1_parts[-1], second_sum = lax.optimization_barrier((dh1_parts[-1], second_sum))
    dh1_came = [exchange(part) for part in dh1_parts]
    first_part = (
        jnp.concatenate(
            [dot(h1_half, stacked, 0, 0).astype(bf16), dot(d_branch, attended, 0, 0).astype(bf16)],
            axis=1,
        )
    )
    first_part, second_sum = lax.optimization_barrier((first_part, second_sum))
    first_sum = scattered(first_part).astype(f32)
    dx1_parts, norm0_sums, conv_sums, d_conv_parts = [], [], [], []
    for c, cut in enumerate(cuts_of):
        came = dh1_came[c]
        if c:
            came, _ = lax.optimization_barrier((came, d_conv_parts[-1]))
        dh1 = dx2_parts[c] + (dh1_parts[c].astype(f32) + came.astype(f32))
        dx1, gain0_grad, shift0_grad = norm0_backs[c](dh1)
        d_spread = lax.dynamic_slice_in_dim(dx1, index * HALF, HALF, 1)
        d_conv = jax.vjp(gelu_exact, pre[cut])[1](d_spread)[0]
        dx1_parts.append(dx1)
        norm0_sums.append((gain0_grad, shift0_grad))
        conv_sums.append(jnp.sum(d_conv, axis=0))
        d_conv_parts.append(d_conv.astype(bf16))
    gain0_grad, shift0_grad = map(sum, zip(*norm0_sums))
    conv_bias_grad = sum(conv_sums)
    d_conv_half = jnp.concatenate(d_conv_parts, axis=0)
    dx1 = jnp.concatenate(dx1_parts, axis=0)
    spread_out = lambda grad, lead: jnp.transpose(
        grad.reshape(lead, devices, -1), (1, 0, 2)
    ).reshape(devices, -1)
    small_part = jnp.concatenate(
            [
                unit_grad.reshape(devices, -1),
                spread_out(jnp.stack([conv_bias_grad, query_bias_grad, value_bias_grad]), 3),
                spread_out(jnp.stack([branch_bias_grad, outer_bias_grad]), 2),
                spread_out(
                    jnp.stack(
                        [gain0_grad, shift0_grad, gain1_grad, shift1_grad, gain2_grad, shift2_grad]
                    ),
                    6,
                ),
            ],
            axis=1,
        )
    small_part = jnp.pad(small_part, ((0, 0), (0, EXTRA * HALF - small_part.shape[1])))
    small_part = small_part.astype(bf16).reshape(devices, EXTRA, HALF)
    d_own = jnp.pad(d_conv_half, ((HALO, HALO), (0, 0)))
    tap_raw = tap_grad(plan, ready, d_own, small_part)
    tap_part, first_sum = lax.optimization_barrier((tap_raw, first_sum))
    tap_sum = scattered(tap_part)[0].astype(f32)
    kernel_sum = tap_sum[:-EXTRA].reshape(TAPS // devices, CG, HALF)
    small_sum = tap_sum[-EXTRA:].reshape(-1)
    d_rim = jnp.concatenate([d_conv_half[:HALO], d_conv_half[rows - HALO :]], axis=0)
    d_rim, _ = lax.optimization_barrier((d_rim, tap_raw))
    d_window = jnp.concatenate(
        [passed(d_rim[HALO:], 1), d_conv_half, passed(d_rim[:HALO], -1)], axis=0
    )
    d_input = conv_back(plan, ready, d_window, spread_taps).astype(bf16)
    frames_grad = dx1 + side_by_side(d_input, exchange(d_input), index).astype(f32)

    pieces, at = [], 0
    for size in cuts:
        pieces.append(small_sum[at : at + size])
        at += size
    unit_sum = pieces[0]
    chan_sum = pieces[1].reshape(chanbias.shape)
    out_sum = pieces[2].reshape(outbias.shape)
    norm_sum = pieces[3].reshape(normparams.shape)
    kv_sum = first_sum[:, HALF : 3 * HALF].reshape(local, PAIRS, 2, 128)
    project_sum = jnp.stack(
        [first_sum[:, :HALF]] + [kv_sum[:, :, c].reshape(local, HALF) for c in range(2)], axis=1
    )

    root = total**0.5
    small_rate = 0.1 / root
    out = [layer_out, frames_grad]
    for weight, grad, moment, average, rate in (
        (kernel, jnp.transpose(kernel_sum, (2, 1, 0)), kernel_moment, kernel_average, (CG * TAPS) ** (-0.5) / root),
        (project, project_sum, project_moment, project_average, width ** (-0.5) / root),
        (combine, first_sum[:, 3 * HALF :].T, combine_moment, combine_average, (width // 16) ** (-0.5) / root),
        (expand, second_sum[:, :hidden_units], expand_moment, expand_average, width ** (-0.5) / root),
        (shrink, second_sum[:, hidden_units:].T, shrink_moment, shrink_average, (2 * hidden_units) ** (-0.5) / root),
        (unitbias, unit_sum, unitbias_moment, unitbias_average, 0.5 / root),
        (chanbias, chan_sum, chanbias_moment, chanbias_average, small_rate),
        (outbias, out_sum, outbias_moment, outbias_average, small_rate),
        (normparams, norm_sum, normparams_moment, normparams_average, small_rate),
    ):
        out.extend(nesterov(weight, grad, moment, average, rate))
    return tuple(out)


def solution(mesh):
    kernel_spec = P("heads", None, "seq")
    project_spec = P("seq", None, "heads")
    tall = P("heads", "seq")
    wide = P("seq", "heads")
    unit = P(("heads", "seq"))
    chan = P(None, ("heads", "seq"))
    outb = P(None, "seq")
    norm = P(None, None, "seq")
    weights = (kernel_spec, project_spec, tall, wide, tall, unit, chan, outb, norm)
    rows = P("seq", None)
    return jax.shard_map(
        body,
        mesh=mesh,
        in_specs=(rows, rows, P()) + tuple(s for s in weights for _ in range(3)),
        out_specs=(rows, rows) + tuple(s for s in weights for _ in range(5)),
        check_vma=False,
    )
```

```python
import functools

import jax
import jax.numpy as jnp
from jax import lax
from jax.experimental import pallas as pl
from jax.experimental.pallas import tpu as pltpu
from jax.sharding import PartitionSpec as P

HEAD = 64
PAIRS = 3
CHUNKS = 2
EPSILON = 1e-05

bf16, f32, i32 = jnp.bfloat16, jnp.float32, jnp.int32
CG, TAPS, GROUPS, HALO = 48, 128, 8, 64
ROWS, WIN, HALF = 1024, 1152, 384
CM, XM = 272, 304
NQ = 33
PJ = 134
EXTRA = 16
VLIM = 58 << 20


def iota(shape, dim):
    return lax.broadcasted_iota(i32, shape, dim)


def block_plan(starts, ends, first):
    w0 = first - HALO
    b = jnp.clip(starts - w0, 0, WIN)
    e = jnp.clip(ends - w0, 0, WIN)
    nblk = (e - b + 3) // 4
    n = starts.shape[0]
    before = jnp.arange(n)[None, :] < jnp.arange(n)[:, None]
    bs = jnp.sum(jnp.where(before, nblk[None, :], 0), axis=1).astype(i32)
    bs = bs + (jnp.clip(-w0, 0, WIN) + 3) // 4
    w = jnp.arange(WIN, dtype=i32)
    inside = (b[None, :] <= w[:, None]) & (w[:, None] < e[None, :])
    p = jnp.sum(jnp.where(inside, 4 * bs - b + w[:, None] + 1, 0), axis=1).astype(i32) - 1
    most = min(WIN, WIN // 4 + n)
    maxc = -((16 - most) // CM)
    lcap = CM * (maxc - 1) + XM
    m = jnp.arange(lcap, dtype=i32)
    hit = (bs[None, :] <= m[:, None]) & (m[:, None] < (bs + nblk)[None, :])
    bseg = jnp.sum(jnp.where(hit, jnp.arange(1, n + 1, dtype=i32)[None, :], 0), axis=1).astype(i32) - 1
    chunks = jnp.maximum((p[HALO + ROWS - 1] // 4 - 16) // CM + 1, 1)
    return (
        jnp.reshape(chunks, (1,)).astype(i32),
        jnp.broadcast_to(p[None, :], (8, WIN)),
        jnp.broadcast_to(p[:, None], (WIN, 128)),
        jnp.broadcast_to(bseg[:, None], (lcap, 128)),
    )


def select_pair(h, rows, base):
    lane = iota((rows, 256), 1)
    src = CG * (2 * h + (lane >> 7)) + (lane & 63) - base
    ok = ((lane & 63) < CG) & (iota((rows, 256), 0) == src)
    return jnp.where(ok, 1.0, 0.0).astype(bf16)


def build_blocks(s_ref, dup):
    y = [jnp.dot(s_ref[0, t], dup, preferred_element_type=f32).astype(bf16) for t in range(4)]
    low = iota((XM, 128), 1) < 64
    out = []
    for g in range(2):
        tiles = [v[:, 128 * g : 128 * g + 128] for v in y]
        out.append(
            jnp.concatenate(
                [jnp.where(low, tiles[0], tiles[1]), jnp.where(low, tiles[2], tiles[3])], axis=1
            )
        )
    return out


def build_taps(k_ref, sel, p_ref, base_tile):
    p_ref[...] = jnp.zeros_like(p_ref)
    step = 16
    for j0 in range(0, TAPS, step):
        part = k_ref[pl.ds(j0, step), :, pl.ds(pl.multiple_of(base_tile * 128, 128), 256)]
        d = jnp.dot(part.reshape(step * CG, 256), sel, preferred_element_type=f32)
        d = d.astype(bf16).reshape(step, CG, 256)
        for g in range(2):
            p_ref[g, pl.ds(j0 + 2, step), 0:CG, 0:64] = d[:, :, 128 * g : 128 * g + 64]
            p_ref[g, pl.ds(j0 + 3, step), 0:CG, 64:128] = d[:, :, 128 * g + 64 : 128 * g + 128]


def pair_lanes(h):
    base_tile = h >> 1
    return base_tile, pl.ds(pl.multiple_of(base_tile * 128, 128), 256)


def prepare_kernel(n_ref, *refs):
    @pl.when(pl.program_id(0) < n_ref[0])
    def _():
        prepare_chunk(pl.program_id(0), *refs)


def prepare_chunk(c, prow_ref, pcol_ref, bseg_ref, x_ref, s_ref, r_ref, mask_ref, tmask_ref, xb_ref, xt_ref):
    prow = prow_ref[0:1, :]
    for t in range(4):
        pos = 4 * (iota((XM, WIN), 0) + CM * c) + t
        s_ref[0, t] = jnp.where(pos == prow, 1.0, 0.0).astype(bf16)
    pcol = pcol_ref[HALO : HALO + ROWS, :]
    lane = iota((ROWS, 4 * CM), 1)
    phase = sum([(lane >= CM * t).astype(i32) for t in range(1, 4)])
    spot = 4 * (16 + CM * c) + 4 * lane - (4 * CM - 1) * phase
    wide = jnp.concatenate([pcol] * 9, axis=1)[:, : 4 * CM]
    r_ref[0] = jnp.where(wide == spot, 1.0, 0.0).astype(bf16)
    seg = bseg_ref[pl.ds(pl.multiple_of(CM * c, 16), XM), :]
    none = jnp.full((32, 128), -7, i32)
    own = jnp.concatenate([none, seg[16 : 16 + CM], none], axis=0)
    for q in range(NQ):
        same = seg[q : q + CM] == seg[16 : 16 + CM]
        mask_ref[0, q] = jnp.where(same, 1.0, 0.0).astype(bf16)
        same = seg == own[32 - q : 32 - q + XM]
        tmask_ref[0, q] = jnp.where(same, 1.0, 0.0).astype(bf16)
    for h in range(4):
        base = 128 * (h // 2)
        sel = select_pair(h, 256, base)
        dup = jnp.dot(x_ref[:, base : base + 256], sel, preferred_element_type=f32).astype(bf16)
        for g, block in enumerate(build_blocks(s_ref, dup)):
            xb_ref[0, 2 * h + g] = block
            xt_ref[0, 2 * h + g] = block.T


def fixed(shape):
    return pl.BlockSpec(shape, lambda *_: (0,) * len(shape))


def chunk_count(plan):
    return (plan[3].shape[0] - XM) // CM + 1


def call(kernel, name, grid, plan, in_specs, out_specs, out_shape, scratch, flops, args):
    return pl.pallas_call(
        kernel,
        grid_spec=pltpu.PrefetchScalarGridSpec(
            num_scalar_prefetch=1,
            grid=grid,
            in_specs=in_specs,
            out_specs=out_specs,
            scratch_shapes=scratch,
        ),
        out_shape=out_shape,
        compiler_params=pltpu.CompilerParams(vmem_limit_bytes=VLIM),
        cost_estimate=pl.CostEstimate(flops=flops, bytes_accessed=15_000_000, transcendentals=0),
        name=name,
    )(plan[0], *args)


def prepare(plan, window):
    chunks, prow, pcol, bseg = plan
    shapes = ((4, XM, WIN), (ROWS, 4 * CM), (NQ, CM, 128), (NQ, XM, 128), (8, XM, 256), (8, 256, XM))
    maxc = chunk_count(plan)
    return call(
        prepare_kernel,
        "conv_prepare",
        (maxc,),
        plan,
        [fixed(a.shape) for a in (prow, pcol, bseg, window)],
        tuple(
            pl.BlockSpec((1,) + s, lambda c, n, k=len(s): (jnp.minimum(c, n[0] - 1),) + (0,) * k)
            for s in shapes
        ),
        tuple(jax.ShapeDtypeStruct((maxc,) + s, bf16) for s in shapes),
        [],
        10_000_000_000,
        (prow, pcol, bseg, window),
    )


def conv_forward_kernel(n_ref, *refs):
    c, h = pl.program_id(0), pl.program_id(1)

    @pl.when(c < n_ref[0])
    def _():
        conv_chunk(False, c, h, *refs)


def conv_back_kernel(n_ref, d_ref, s_ref, *refs):
    c, h = pl.program_id(0), pl.program_id(1)

    @pl.when(c < n_ref[0])
    def _():
        conv_chunk(True, c, h, (d_ref, s_ref), *refs)


def conv_chunk(back, c, h, x_ref, mask_ref, r_ref, k_ref, out_ref, *rest):
    base_tile, lanes = pair_lanes(h)
    if back:
        s_ref, (xb_ref, o_ref) = x_ref[1], rest
        p_ref = k_ref
        sel = select_pair(h, 256, 128 * base_tile)
        dup = jnp.dot(x_ref[0][:, lanes], sel, preferred_element_type=f32).astype(bf16)
        for g, block in enumerate(build_blocks(s_ref, dup)):
            xb_ref[0, g] = block
    else:
        xb_ref = x_ref
        p_ref, o_ref = rest
        build_taps(k_ref, select_pair(h, 256, 128 * base_tile), p_ref, base_tile)

    @pl.when(h == 0)
    def _():
        o_ref[...] = jnp.zeros_like(o_ref)

    total = [jnp.zeros((CM, 256), f32) for _ in range(4)]
    for g in range(2):
        acc = jnp.zeros((CM, 256), f32)
        for q in range(NQ):
            m = mask_ref[0, q]
            xs = xb_ref[0, g, q : q + CM, :] * jnp.concatenate([m, m], axis=1)
            if back:
                a, b = 130 - 4 * q, 128 - 4 * q
            else:
                a, b = 4 * q + 2, 4 * q
            w = jnp.concatenate(
                [p_ref[g, a : a + 4].reshape(256, 128), p_ref[g, b : b + 4].reshape(256, 128)],
                axis=1,
            )
            dims = (((1,), (1 if back else 0,)), ((), ()))
            acc = acc + lax.dot_general(xs, w, dims, preferred_element_type=f32)
        acc = acc.astype(bf16)
        row = iota((256, 256), 0)
        target = CG * (2 * h + g) - 128 * base_tile + (row & 63)
        hit = ((row & 63) < CG) & (iota((256, 256), 1) == target)
        for t in range(4):
            fold = jnp.where(hit & ((row >> 6) == t), 1.0, 0.0).astype(bf16)
            total[t] = total[t] + jnp.dot(acc, fold, preferred_element_type=f32)
    for t in range(4):
        o_ref[CM * t : CM * t + CM, lanes] += total[t].astype(bf16)

    @pl.when(h == 3)
    def _():
        y = jnp.dot(r_ref[0], o_ref[...], preferred_element_type=f32)

        @pl.when(c == 0)
        def _():
            out_ref[...] = y

        @pl.when(c > 0)
        def _():
            out_ref[...] += y


def by_chunk(shape):
    return pl.BlockSpec(
        (1,) + shape, lambda c, h, n: (jnp.minimum(c, n[0] - 1),) + (0,) * len(shape)
    )


def by_pair(shape):
    return pl.BlockSpec(
        (2,) + shape, lambda c, h, n: (jnp.where(c < n[0], h, 3),) + (0,) * len(shape)
    )


def conv(plan, ready, taps):
    _, r, mask, _, xb, _ = ready
    x_spec = pl.BlockSpec(
        (1, 2, XM, 256),
        lambda c, h, n: (jnp.minimum(c, n[0] - 1), jnp.where(c < n[0], h, 3), 0, 0),
    )
    return call(
        conv_forward_kernel,
        "conv_forward",
        (chunk_count(plan), 4),
        plan,
        [x_spec, by_chunk((NQ, CM, 128)), by_chunk((ROWS, 4 * CM)), fixed((TAPS, CG, HALF))],
        (fixed((ROWS, HALF)), by_pair((PJ, 64, 128))),
        (
            jax.ShapeDtypeStruct((ROWS, HALF), f32),
            jax.ShapeDtypeStruct((8, PJ, 64, 128), bf16),
        ),
        [pltpu.VMEM((4 * CM, HALF), bf16)],
        25_000_000_000,
        (xb, mask, r, taps),
    )


def conv_back(plan, ready, window, spread_taps):
    s, r, mask, _, _, _ = ready
    return call(
        conv_back_kernel,
        "conv_back",
        (chunk_count(plan), 4),
        plan,
        [
            fixed((WIN, HALF)),
            by_chunk((4, XM, WIN)),
            by_chunk((NQ, CM, 128)),
            by_chunk((ROWS, 4 * CM)),
            by_pair((PJ, 64, 128)),
        ],
        fixed((ROWS, HALF)),
        jax.ShapeDtypeStruct((ROWS, HALF), f32),
        [pltpu.VMEM((1, 2, XM, 256), bf16), pltpu.VMEM((4 * CM, HALF), bf16)],
        25_000_000_000,
        (window, s, mask, r, spread_taps),
    )


def tap_grad_kernel(n_ref, xt_ref, s_ref, mask_ref, d_ref, small_ref, out_ref, dp_ref, acc_ref, sum_ref):
    h, c = pl.program_id(0), pl.program_id(1)
    base_tile, lanes = pair_lanes(h)

    @pl.when((h == 0) & (c == 0))
    def _():
        out_ref[...] = jnp.zeros_like(out_ref)
        out_ref[:, out_ref.shape[1] - EXTRA :, :] = small_ref[...]
        dp_ref[...] = jnp.zeros_like(dp_ref)

    @pl.when(c < n_ref[0])
    def _():
        sel = select_pair(h, 256, 128 * base_tile)
        ddup = jnp.dot(d_ref[:, lanes], sel, preferred_element_type=f32).astype(bf16)
        for g, block in enumerate(build_blocks(s_ref, ddup)):
            dp_ref[g, 32 : 32 + CM, :] = block[16 : 16 + CM]
        for g in range(2):
            carry = jnp.zeros((128, 128), f32)
            for q in range(NQ):
                m = mask_ref[0, q]
                ds = dp_ref[g, 32 - q : 32 - q + XM, :] * jnp.concatenate([m, m], axis=1)
                part = jnp.dot(xt_ref[0, g], ds, preferred_element_type=f32)
                left, right = part[:, 0:128], part[:, 128:256]
                acc_ref[g, 4 * q : 4 * q + 2] = (right[0:128] + carry).reshape(2, 64, 128)
                acc_ref[g, 4 * q + 2 : 4 * q + 4] = (left[0:128] + right[128:256]).reshape(2, 64, 128)
                carry = left[128:256]
            acc_ref[g, 4 * NQ : 4 * NQ + 2] = carry.reshape(2, 64, 128)

        @pl.when(c > 0)
        def _():
            acc_ref[...] += sum_ref[...]

        @pl.when(c < n_ref[0] - 1)
        def _():
            sum_ref[...] = acc_ref[...]

    @pl.when(c == pl.num_programs(1) - 1)
    def _():
        per = TAPS // out_ref.shape[0]
        low = iota((1, 1, 128), 2) < 64
        row = iota((128, 256), 0)
        src = CG * (2 * h + (row >> 6)) + (row & 63) - 128 * base_tile
        back = jnp.where(((row & 63) < CG) & (iota((128, 256), 1) == src), 1.0, 0.0).astype(bf16)
        step = 16
        for j0 in range(0, TAPS, step):
            now = [acc_ref[g, j0 + 2 : j0 + 2 + step, 0:CG, :] for g in range(2)]
            nxt = [acc_ref[g, j0 + 3 : j0 + 3 + step, 0:CG, :] for g in range(2)]
            here = jnp.where(low, now[0], nxt[1]).reshape(step * CG, 128)
            far = jnp.where(low, now[1], nxt[0]).reshape(step * CG, 128)
            both = (here + pltpu.roll(far, 64, 1)).astype(bf16)
            o = jnp.dot(both, back, preferred_element_type=f32).astype(bf16)
            o = o.reshape(step // per, per * CG, 256)
            out_ref[j0 // per : (j0 + step) // per, 0 : per * CG, lanes] += o


def tap_grad(plan, ready, d_own, small):
    s, _, _, tmask, _, xt = ready
    devices = small.shape[0]
    shape = (devices, TAPS // devices * CG + EXTRA, HALF)
    chunked = lambda sh: pl.BlockSpec(
        (1,) + sh, lambda h, c, n: (jnp.minimum(c, n[0] - 1),) + (0,) * len(sh)
    )
    x_spec = pl.BlockSpec((1, 2, 256, XM), lambda h, c, n: (jnp.minimum(c, n[0] - 1), h, 0, 0))
    return call(
        tap_grad_kernel,
        "tap_gradient",
        (4, chunk_count(plan)),
        plan,
        [
            x_spec,
            chunked((4, XM, WIN)),
            chunked((NQ, XM, 128)),
            fixed((WIN, HALF)),
            fixed(small.shape),
        ],
        fixed(shape),
        jax.ShapeDtypeStruct(shape, bf16),
        [
            pltpu.VMEM((2, 32 + CM + 32, 256), bf16),
            pltpu.VMEM((2, PJ, 64, 128), f32),
            pltpu.VMEM((2, PJ, 64, 128), f32),
        ],
        1_000_000_000,
        (xt, s, tmask, d_own, small),
    )
REACH = 1536
SPAN = ROWS + 2 * REACH
QT_AHEAD, QT_BACK, KT = 512, 256, 1664
NEAR = REACH - ROWS
NEG = -1e30


def segment_count(ends, positions):
    return jnp.sum((ends[None, :] <= positions[:, None]).astype(i32), axis=1).astype(i32)

def attention_plan(starts, ends, first, odd):
    w = first - REACH + jnp.arange(SPAN, dtype=i32)
    kseg = segment_count(ends, w)
    kseg = jnp.where(w < 0, -1, kseg)
    qseg = kseg[REACH : REACH + ROWS]
    n = jnp.arange(starts.shape[0], dtype=i32)

    def tiles_of(rows):
        edge = qseg.reshape(ROWS // rows, rows)
        head = jnp.sum(jnp.where(n[None] == edge[:, :1], starts[None], 0), axis=1) - (first - REACH)
        tail = jnp.sum(jnp.where(n[None] == edge[:, -1:], ends[None], 0), axis=1) - (first - REACH)
        lo = jnp.clip(head // 128, 0, SPAN // 128)
        hi = jnp.clip((tail + 127) // 128, 1, SPAN // 128)
        tiles = jnp.maximum((hi - lo + KT // 128 - 1) // (KT // 128), 1)
        lo = jnp.minimum(lo, SPAN // 128 - tiles * (KT // 128))
        return jnp.stack([lo, tiles, jnp.full_like(lo, odd)]).astype(i32)

    return (
        tiles_of(QT_AHEAD),
        tiles_of(QT_BACK),
        jnp.broadcast_to(qseg[None], (8, ROWS)),
        jnp.broadcast_to(kseg[:, None], (SPAN, 128)),
    )


def split_heads(a):
    low = iota(a.shape, 1) < 64
    zero = jnp.zeros((), a.dtype)
    return jnp.where(low, a, zero), jnp.where(low, zero, a)

def spots(range_ref):
    odd = range_ref[2, 0] == 1
    right, end = REACH + ROWS, SPAN - NEAR
    at = [
        jnp.where(odd, NEAR, right),
        jnp.where(odd, right, NEAR),
        jnp.where(odd, end, 0),
        jnp.where(odd, 0, end),
    ]
    return [pl.multiple_of(x, NEAR) for x in at]


def fill_span(range_ref, span_ref, own, others):
    span_ref[REACH : REACH + ROWS, :] = own[...]
    for at, piece in zip(spots(range_ref), others):
        span_ref[pl.ds(at, piece.shape[0]), :] = piece[...]


def flip_span(src_ref, dst_ref, lane):
    for at in range(0, SPAN, 512):
        dst_ref[:, at : at + 512] = src_ref[at : at + 512, lane : lane + 128].T


def same_segment(kseg_ref, qseg_ref, at):
    ks = kseg_ref[at, :]
    ks = jnp.concatenate([ks] * (qseg_ref.shape[1] // 128), axis=1)
    return ks == qseg_ref[0:1, :]


def forward_kernel(range_ref, qseg_ref, kseg_ref, q_ref, k0, k1, k2, k3, k4, o_ref, half_ref, lse_ref, span_ref, vt_ref):
    qi = pl.program_id(0)

    @pl.when(qi == 0)
    def _():
        fill_span(range_ref, span_ref, k0, (k1, k2, k3, k4))
        flip_span(span_ref, vt_ref, 128)

    qs = split_heads(q_ref[...])

    first, count = range_ref[0, qi], range_ref[1, qi]

    def tile(t, carry):
        at = pl.ds(pl.multiple_of((first + t * (KT // 128)) * 128, 128), KT)
        same = same_segment(kseg_ref, qseg_ref, at)
        k = span_ref[at, 0:128]
        out = []
        for e in range(2):
            m, l, acc = carry[e]
            s = lax.dot_general(k, qs[e], (((1,), (1,)), ((), ())), preferred_element_type=f32)
            s = jnp.where(same, s, NEG)
            new = jnp.maximum(m, jnp.max(s, axis=0, keepdims=True))
            p = jnp.exp(s - new)
            alpha = jnp.exp(m - new)
            l = l * alpha + jnp.sum(p, axis=0, keepdims=True)
            vt = vt_ref[64 * e : 64 * e + 64, at]
            acc = acc * alpha + jnp.dot(vt, p.astype(bf16), preferred_element_type=f32)
            out.append((new, l, acc))
        return tuple(out)

    start = (jnp.full((1, QT_AHEAD), NEG, f32), jnp.zeros((1, QT_AHEAD), f32), jnp.zeros((64, QT_AHEAD), f32))
    ends = lax.fori_loop(0, count, tile, (start, start))
    o = jnp.concatenate([acc / l for _, l, acc in ends], axis=0).T
    o_ref[...] = o
    half_ref[...] = o.astype(bf16)
    for e in range(2):
        lse_ref[e : e + 1, :] = ends[e][0] + jnp.log(ends[e][1])


def piece_specs(h, pieces):
    at = [h - (PAIRS - p.shape[1] // 256) if p.shape[1] > 256 else 0 for p in pieces]
    return [pl.BlockSpec((p.shape[0], 256), lambda i, c=c: (0, c)) for p, c in zip(pieces, at)]


def attend(plan, h, q, pieces):
    ranges, _, qseg, kseg = plan
    return pl.pallas_call(
        forward_kernel,
        grid=(ROWS // QT_AHEAD,),
        out_shape=(
            jax.ShapeDtypeStruct((ROWS, 128), f32),
            jax.ShapeDtypeStruct((ROWS, 128), bf16),
            jax.ShapeDtypeStruct((8, ROWS), f32),
        ),
        in_specs=[
            pl.BlockSpec(memory_space=pltpu.SMEM),
            pl.BlockSpec((8, QT_AHEAD), lambda i: (0, i)),
            pl.BlockSpec((SPAN, 128), lambda i: (0, 0)),
            pl.BlockSpec((QT_AHEAD, 128), lambda i: (i, h)),
        ]
        + piece_specs(h, pieces),
        out_specs=(
            pl.BlockSpec((QT_AHEAD, 128), lambda i: (i, 0)),
            pl.BlockSpec((QT_AHEAD, 128), lambda i: (i, 0)),
            pl.BlockSpec((8, QT_AHEAD), lambda i: (0, i)),
        ),
        scratch_shapes=[pltpu.VMEM((SPAN, 256), bf16), pltpu.VMEM((128, SPAN), bf16)],
        compiler_params=pltpu.CompilerParams(vmem_limit_bytes=VLIM),
        cost_estimate=pl.CostEstimate(flops=8_000_000_000, bytes_accessed=8_000_000, transcendentals=0),
        name="attention_forward",
    )(ranges, qseg, kseg, q, *pieces)


def backward_kernel(range_ref, qseg_ref, kseg_ref, q_ref, k0, k1, k2, k3, k4, do_ref, o_ref, lse_ref,
                    dq_ref, own_ref, f1, f2, f3, f4, span_ref, kt_ref, dkv_ref):
    qi = pl.program_id(0)
    last = ROWS // QT_BACK - 1

    @pl.when(qi == 0)
    def _():
        dkv_ref[...] = jnp.zeros_like(dkv_ref)
        fill_span(range_ref, span_ref, k0, (k1, k2, k3, k4))
        flip_span(span_ref, kt_ref, 0)

    qs = split_heads(q_ref[...])
    dos = split_heads(do_ref[...])
    qcat = jnp.concatenate(qs, axis=0)
    docat = jnp.concatenate(dos, axis=0)
    dm = (do_ref[...].astype(f32) * o_ref[...]).T
    delta = [jnp.sum(dm[64 * e : 64 * e + 64], axis=0, keepdims=True) for e in range(2)]

    first, count = range_ref[0, qi], range_ref[1, qi]

    def tile(t, carry):
        at = pl.ds(pl.multiple_of((first + t * (KT // 128)) * 128, 128), KT)
        same = same_segment(kseg_ref, qseg_ref, at)
        k = span_ref[at, 0:128]
        v = span_ref[at, 128:256]
        ps, dss, out = [], [], []
        for e in range(2):
            dims = (((1,), (1,)), ((), ()))
            s = lax.dot_general(k, qs[e], dims, preferred_element_type=f32)
            p = jnp.exp(jnp.where(same, s - lse_ref[e : e + 1, :], NEG))
            dp = lax.dot_general(v, dos[e], dims, preferred_element_type=f32)
            ds = (p * (dp - delta[e])).astype(bf16)
            kt = kt_ref[64 * e : 64 * e + 64, at]
            out.append(carry[e] + jnp.dot(kt, ds, preferred_element_type=f32))
            ps.append(p.astype(bf16))
            dss.append(ds)
        dkv_ref[at, 0:128] += jnp.dot(jnp.concatenate(dss, axis=1), qcat, preferred_element_type=f32)
        dkv_ref[at, 128:256] += jnp.dot(jnp.concatenate(ps, axis=1), docat, preferred_element_type=f32)
        return tuple(out)

    zero = jnp.zeros((64, QT_BACK), f32)
    dqt = lax.fori_loop(0, count, tile, (zero, zero))
    dq = jnp.concatenate(dqt, axis=0).T
    dq_ref[...] = dq.astype(bf16) * jnp.asarray(0.125, bf16)

    @pl.when(qi == last)
    def _():
        for at, far in zip(spots(range_ref), (f1, f2, f3, f4)):
            far[...] = dkv_ref[pl.ds(at, far.shape[0]), :].astype(bf16)
        own_ref[...] = dkv_ref[REACH : REACH + ROWS, :]


def attend_back(plan, h, q, pieces, d_att, mixed, lse):
    _, ranges, qseg, kseg = plan
    rowspec = pl.BlockSpec((QT_BACK, 128), lambda i: (i, 0))
    colspec = pl.BlockSpec((QT_BACK, 128), lambda i: (i, h))
    return pl.pallas_call(
        backward_kernel,
        grid=(ROWS // QT_BACK,),
        out_shape=(
            jax.ShapeDtypeStruct((ROWS, 128), bf16),
            jax.ShapeDtypeStruct((ROWS, 256), f32),
        )
        + tuple(jax.ShapeDtypeStruct((n, 256), bf16) for n in (ROWS, ROWS, NEAR, NEAR)),
        in_specs=[
            pl.BlockSpec(memory_space=pltpu.SMEM),
            pl.BlockSpec((8, QT_BACK), lambda i: (0, i)),
            pl.BlockSpec((SPAN, 128), lambda i: (0, 0)),
            colspec,
        ]
        + piece_specs(h, pieces)
        + [colspec, rowspec, pl.BlockSpec((8, QT_BACK), lambda i: (0, i))],
        out_specs=(
            rowspec,
            pl.BlockSpec((ROWS, 256), lambda i: (0, 0)),
        )
        + tuple(pl.BlockSpec((n, 256), lambda i: (0, 0)) for n in (ROWS, ROWS, NEAR, NEAR)),
        scratch_shapes=[
            pltpu.VMEM((SPAN, 256), bf16),
            pltpu.VMEM((128, SPAN), bf16),
            pltpu.VMEM((SPAN, 256), f32),
        ],
        compiler_params=pltpu.CompilerParams(vmem_limit_bytes=VLIM),
        cost_estimate=pl.CostEstimate(flops=8_000_000_000, bytes_accessed=12_000_000, transcendentals=0),
        name="attention_backward",
    )(ranges, qseg, kseg, q, *pieces, d_att, mixed, lse)


def exchange(part):
    return lax.ppermute(part, "heads", [(0, 1), (1, 0)])


def pair_sum(part):
    half = part.astype(bf16)
    return half.astype(f32) + exchange(half).astype(f32)


def side_by_side(own, other, index):
    return jnp.where(
        index == 0,
        jnp.concatenate([own, other], axis=1),
        jnp.concatenate([other, own], axis=1),
    )


def passed(block, distance):
    count = lax.axis_size("seq")
    route = [(i - distance, i) for i in range(count) if 0 <= i - distance < count]
    return lax.ppermute(block, "seq", route)


def across_cores(block):
    return lax.ppermute(block, "seq", [(i, i ^ 1) for i in range(lax.axis_size("seq"))])


def across_chips(block):
    count = lax.axis_size("seq")
    route = [(i, i + 1 if i % 2 else i - 1) for i in range(count)]
    return lax.ppermute(block, "seq", [(i, j) for i, j in route if 0 <= j < count])


def chip_along(block, step):
    count = lax.axis_size("seq")
    route = [(i, i - 2 * step if i % 2 else i + 2 * step) for i in range(count)]
    return lax.ppermute(block, "seq", [(i, j) for i, j in route if 0 <= j < count])


def layer_norm(values, gain, shift):
    centered = values - jnp.mean(values, axis=-1, keepdims=True)
    scale = lax.rsqrt(jnp.mean(centered * centered, axis=-1, keepdims=True) + EPSILON)
    return centered * scale * gain + shift


def gelu_exact(values):
    return jax.nn.gelu(values, approximate=False)


def nesterov(weight, grad, moment, average, rate):
    moment_new = 0.5 * moment + grad
    weight_new = weight - rate * (grad + 0.5 * moment_new)
    average_new = 0.5 * average + 0.5 * weight_new
    return (grad, weight_new, moment_new, average_new, weight_new.astype(bf16))


def dot(a, b, ca, cb):
    return lax.dot_general(a, b, (((ca,), (cb,)), ((), ())), preferred_element_type=f32)


def gathered(shard):
    return lax.all_gather(shard, "seq", axis=0, tiled=True)


def scattered(whole_sum):
    return lax.psum_scatter(whole_sum, "seq", scatter_dimension=0, tiled=True)


def body(
    frames,
    cotangent,
    lengths,
    kernel,
    kernel_moment,
    kernel_average,
    project,
    project_moment,
    project_average,
    combine,
    combine_moment,
    combine_average,
    expand,
    expand_moment,
    expand_average,
    shrink,
    shrink_moment,
    shrink_average,
    unitbias,
    unitbias_moment,
    unitbias_average,
    chanbias,
    chanbias_moment,
    chanbias_average,
    outbias,
    outbias_moment,
    outbias_average,
    normparams,
    normparams_moment,
    normparams_average,
):
    devices = lax.axis_size("seq")
    rows, width = frames.shape
    total = devices * rows
    first = lax.axis_index("seq") * rows
    index = lax.axis_index("heads")
    odd = lax.axis_index("seq") % 2
    local = project.shape[0]
    hidden_units = expand.shape[1]

    w_kernel = gathered(jnp.transpose(kernel, (2, 1, 0)).astype(bf16))
    small = jnp.concatenate(
        [unitbias, chanbias.reshape(-1), outbias.reshape(-1), normparams.reshape(-1)]
    ).astype(bf16)
    w_small = gathered(small[None])
    w_first = gathered(
        jnp.concatenate(
            [project[:, 0]]
            + [project[:, c, 128 * h : 128 * h + 128] for h in range(PAIRS) for c in (1, 2)]
            + [combine.T],
            axis=1,
        ).astype(bf16)
    )
    w_second = gathered(jnp.concatenate([expand, shrink.T], axis=1).astype(bf16))
    w_combine = w_first[:, 3 * HALF :]
    cuts = [unitbias.size, chanbias.size, outbias.size, normparams.size]
    parts, at = [], 0
    for size in cuts:
        parts.append(w_small[:, at : at + size].astype(f32))
        at += size
    b_unit = parts[0].reshape(-1)
    b_chan = jnp.transpose(parts[1].reshape(devices, 3, -1), (1, 0, 2)).reshape(3, -1)
    b_out = jnp.transpose(parts[2].reshape(devices, 2, -1), (1, 0, 2)).reshape(2, -1)
    norms = jnp.transpose(parts[3].reshape(devices, 3, 2, -1), (1, 2, 0, 3)).reshape(3, 2, -1)

    count = lengths.shape[0]
    order = jnp.arange(count, dtype=i32)
    ends = jnp.sum(jnp.where(order[None, :] <= order[:, None], lengths[None, :], 0), axis=1).astype(i32)
    starts = ends - lengths
    plan = block_plan(starts, ends, first)
    reach = attention_plan(starts, ends, first, odd)

    x_half = lax.dynamic_slice_in_dim(frames, index * HALF, HALF, 1).astype(bf16)
    window = jnp.concatenate(
        [passed(x_half[rows - HALO :], 1), x_half, passed(x_half[:HALO], -1)], axis=0
    )
    window, reach = lax.optimization_barrier((window, reach))
    ready = prepare(plan, window)
    conv_out, spread_taps = conv(plan, ready, w_kernel)
    pre = conv_out + b_chan[0]
    spread_part = gelu_exact(pre).astype(bf16)
    spread = side_by_side(spread_part, exchange(spread_part), index)
    h1, norm0_back = jax.vjp(layer_norm, frames + spread.astype(f32), norms[0, 0], norms[0, 1])
    h1_half = h1.astype(bf16)
    proj = dot(h1_half, w_first[:, : 3 * HALF], 1, 0)
    scale = HEAD ** (-0.5)
    queries = ((proj[:, :HALF] + b_chan[1]) * scale).astype(bf16)
    kv_bias = b_chan[2].reshape(PAIRS, 1, 128)
    kv_bias = jnp.concatenate([jnp.zeros_like(kv_bias), kv_bias], axis=1).reshape(-1)
    both = (proj[:, HALF:] + kv_bias).astype(bf16)
    near = NEAR
    w_combine_sent, queries = lax.optimization_barrier((w_combine, queries))
    w_combine_far = exchange(w_combine_sent)

    def fetched(lo, hi):
        block = both[:, lo:hi]
        head, tail = block[:near], block[rows - near :]
        beside = across_chips(block)
        shared = jnp.where(odd == 1, beside[:near], beside[rows - near :])
        return (
            across_cores(block),
            beside,
            chip_along(jnp.where(odd == 1, head, tail), 1),
            shared,
        )

    early = fetched(0, 256)
    early = early[:3] + (across_cores(early[3]),)
    both, early = lax.optimization_barrier((both, early))
    late = fetched(256, 256 * PAIRS)
    pieces = [(both,) + early]
    mixed, attended, attended_far, lse = [], [], [], []
    for h in range(PAIRS):
        q_part = queries
        if h == 1:
            q_part, w_combine_far = lax.optimization_barrier((queries, w_combine_far))
        if h >= 2:
            q_part, attended_far[h - 2] = lax.optimization_barrier((queries, attended_far[h - 2]))
        mixed_part, half, lse_part = attend(reach, h, q_part, pieces[h])
        mixed.append(mixed_part)
        lse.append(lse_part)
        attended.append(half)
        attended_far.append(exchange(half))
        if h == 0:
            shared, _ = lax.optimization_barrier((late[3], half))
            pieces += [(both,) + late[:3] + (across_cores(shared),)] * (PAIRS - 1)
    attended = jnp.concatenate(attended, axis=1)
    attended_all = side_by_side(attended, jnp.concatenate(attended_far, axis=1), index)
    w_combine_all = side_by_side(w_combine, w_combine_far, index)
    w_expand = w_second[:, :hidden_units]
    w_shrink = w_second[:, hidden_units:]
    step = rows // CHUNKS
    cuts_of = [slice(c * step, (c + 1) * step) for c in range(CHUNKS)]
    first_half, second_half = [], []
    for cut in cuts_of:
        branch = dot(attended_all[cut], w_combine_all, 1, 1)
        h2, norm1_back = jax.vjp(layer_norm, h1[cut] + branch + b_out[0], norms[1, 0], norms[1, 1])
        h2_half = h2.astype(bf16)
        inner = dot(h2_half, w_expand, 1, 0) + b_unit
        hidden, gelu_inner_back = jax.vjp(gelu_exact, inner)
        hidden_half = hidden.astype(bf16)
        sent = dot(hidden_half, w_shrink, 1, 1).astype(bf16)
        first_half.append((h2, norm1_back, h2_half, gelu_inner_back, hidden_half, sent, exchange(sent)))
    sent_back = None
    for cut, (h2, norm1_back, h2_half, gelu_inner_back, hidden_half, sent, came) in zip(
        cuts_of, first_half
    ):
        if sent_back is not None:
            came, _ = lax.optimization_barrier((came, sent_back))
        outer = sent.astype(f32) + came.astype(f32)
        out_part, norm2_back = jax.vjp(layer_norm, h2 + outer + b_out[1], norms[2, 0], norms[2, 1])
        dx3, gain2_grad, shift2_grad = norm2_back(cotangent[cut])
        d_out = dx3.astype(bf16)
        d_hidden = dot(d_out, w_shrink, 1, 0)
        d_inner = gelu_inner_back(d_hidden)[0]
        d_inner_half = d_inner.astype(bf16)
        sent_back = dot(d_inner_half, w_expand, 1, 1).astype(bf16)
        sums = [gain2_grad, shift2_grad, jnp.sum(dx3, axis=0), jnp.sum(d_inner, axis=0)]
        second_half.append(
            [out_part, (sent_back, exchange(sent_back)), norm1_back, h2_half, d_inner_half, d_out, hidden_half, dx3, sums]
        )
    layer_out = jnp.concatenate([part[0] for part in second_half], axis=0)
    gain2_grad, shift2_grad, outer_bias_grad, unit_grad = map(sum, zip(*[p[-1] for p in second_half]))
    second_part = jnp.concatenate(
        [
            sum(dot(p[a], p[b], 0, 0) for p in second_half).astype(bf16)
            for a, b in ((3, 4), (5, 6))
        ],
        axis=1,
    )
    dx2_parts, gain1_parts, shift1_parts = zip(
        *[p[2](p[7] + (p[1][0].astype(f32) + p[1][1].astype(f32))) for p in second_half]
    )
    gain1_grad, shift1_grad = sum(gain1_parts), sum(shift1_parts)
    dx2 = jnp.concatenate(dx2_parts, axis=0)
    branch_bias_grad = jnp.sum(dx2, axis=0)
    d_branch = dx2.astype(bf16)
    d_att = dot(d_branch, w_combine, 1, 0).astype(bf16)
    d_att, second_part = lax.optimization_barrier((d_att, second_part))
    second_sum = scattered(second_part).astype(f32)
    dq_parts, kv_parts = [], []
    arrived = {}
    for h in range(PAIRS):
        d_part = d_att
        if h >= 2:
            two = arrived[h - 2][:2]
            d_part, two = lax.optimization_barrier((d_att, two))
            arrived[h - 2] = two + arrived[h - 2][2:]
        dq_part, own, core, chip, far, beyond = attend_back(
            reach, h, queries, pieces[h], d_part, mixed[h], lse[h]
        )
        arrived[h] = (
            across_cores(core),
            across_chips(chip),
            chip_along(far, -1),
            chip_along(beyond, 1),
            own,
        )
        dq_parts.append(dq_part)
    for h in range(PAIRS):
        core, chip, far, beyond, own = [a.astype(f32) for a in arrived[h]]
        ends_of = jnp.concatenate(
            [jnp.where(odd == 1, far, beyond), jnp.where(odd == 1, beyond, far)], axis=0
        )
        kv_parts.append((own + core + chip + ends_of).astype(bf16))
    dq_half = jnp.concatenate(dq_parts, axis=1)
    d_both_half = jnp.concatenate(kv_parts, axis=1)
    stacked = jnp.concatenate([dq_half, d_both_half], axis=1)
    query_bias_grad = jnp.sum(dq_half.astype(f32), axis=0)
    value_bias_grad = jnp.sum(
        d_both_half.astype(f32), axis=0
    ).reshape(PAIRS, 2, 128)[:, 1].reshape(-1)
    dh1_half = dot(stacked, w_first[:, : 3 * HALF], 1, 1).astype(bf16)
    dh1_half, second_sum = lax.optimization_barrier((dh1_half, second_sum))
    dh1 = dx2 + (dh1_half.astype(f32) + exchange(dh1_half).astype(f32))
    first_part = (
        jnp.concatenate(
            [dot(h1_half, stacked, 0, 0).astype(bf16), dot(d_branch, attended, 0, 0).astype(bf16)],
            axis=1,
        )
    )
    first_part, second_sum = lax.optimization_barrier((first_part, second_sum))
    first_sum = scattered(first_part).astype(f32)
    dx1, gain0_grad, shift0_grad = norm0_back(dh1)
    d_spread = lax.dynamic_slice_in_dim(dx1, index * HALF, HALF, 1)
    d_conv = jax.vjp(gelu_exact, pre)[1](d_spread)[0]
    conv_bias_grad = jnp.sum(d_conv, axis=0)
    d_conv_half = d_conv.astype(bf16)
    spread_out = lambda grad, lead: jnp.transpose(
        grad.reshape(lead, devices, -1), (1, 0, 2)
    ).reshape(devices, -1)
    small_part = jnp.concatenate(
            [
                unit_grad.reshape(devices, -1),
                spread_out(jnp.stack([conv_bias_grad, query_bias_grad, value_bias_grad]), 3),
                spread_out(jnp.stack([branch_bias_grad, outer_bias_grad]), 2),
                spread_out(
                    jnp.stack(
                        [gain0_grad, shift0_grad, gain1_grad, shift1_grad, gain2_grad, shift2_grad]
                    ),
                    6,
                ),
            ],
            axis=1,
        )
    small_part = jnp.pad(small_part, ((0, 0), (0, EXTRA * HALF - small_part.shape[1])))
    small_part = small_part.astype(bf16).reshape(devices, EXTRA, HALF)
    d_own = jnp.pad(d_conv_half, ((HALO, HALO), (0, 0)))
    tap_raw = tap_grad(plan, ready, d_own, small_part)
    tap_part, first_sum = lax.optimization_barrier((tap_raw, first_sum))
    tap_sum = scattered(tap_part)[0].astype(f32)
    kernel_sum = tap_sum[:-EXTRA].reshape(TAPS // devices, CG, HALF)
    small_sum = tap_sum[-EXTRA:].reshape(-1)
    d_rim = jnp.concatenate([d_conv_half[:HALO], d_conv_half[rows - HALO :]], axis=0)
    d_rim, _ = lax.optimization_barrier((d_rim, tap_raw))
    d_window = jnp.concatenate(
        [passed(d_rim[HALO:], 1), d_conv_half, passed(d_rim[:HALO], -1)], axis=0
    )
    d_input = conv_back(plan, ready, d_window, spread_taps).astype(bf16)
    frames_grad = dx1 + side_by_side(d_input, exchange(d_input), index).astype(f32)

    pieces, at = [], 0
    for size in cuts:
        pieces.append(small_sum[at : at + size])
        at += size
    unit_sum = pieces[0]
    chan_sum = pieces[1].reshape(chanbias.shape)
    out_sum = pieces[2].reshape(outbias.shape)
    norm_sum = pieces[3].reshape(normparams.shape)
    kv_sum = first_sum[:, HALF : 3 * HALF].reshape(local, PAIRS, 2, 128)
    project_sum = jnp.stack(
        [first_sum[:, :HALF]] + [kv_sum[:, :, c].reshape(local, HALF) for c in range(2)], axis=1
    )

    root = total**0.5
    small_rate = 0.1 / root
    out = [layer_out, frames_grad]
    for weight, grad, moment, average, rate in (
        (kernel, jnp.transpose(kernel_sum, (2, 1, 0)), kernel_moment, kernel_average, (CG * TAPS) ** (-0.5) / root),
        (project, project_sum, project_moment, project_average, width ** (-0.5) / root),
        (combine, first_sum[:, 3 * HALF :].T, combine_moment, combine_average, (width // 16) ** (-0.5) / root),
        (expand, second_sum[:, :hidden_units], expand_moment, expand_average, width ** (-0.5) / root),
        (shrink, second_sum[:, hidden_units:].T, shrink_moment, shrink_average, (2 * hidden_units) ** (-0.5) / root),
        (unitbias, unit_sum, unitbias_moment, unitbias_average, 0.5 / root),
        (chanbias, chan_sum, chanbias_moment, chanbias_average, small_rate),
        (outbias, out_sum, outbias_moment, outbias_average, small_rate),
        (normparams, norm_sum, normparams_moment, normparams_average, small_rate),
    ):
        out.extend(nesterov(weight, grad, moment, average, rate))
    return tuple(out)


def solution(mesh):
    kernel_spec = P("heads", None, "seq")
    project_spec = P("seq", None, "heads")
    tall = P("heads", "seq")
    wide = P("seq", "heads")
    unit = P(("heads", "seq"))
    chan = P(None, ("heads", "seq"))
    outb = P(None, "seq")
    norm = P(None, None, "seq")
    weights = (kernel_spec, project_spec, tall, wide, tall, unit, chan, outb, norm)
    rows = P("seq", None)
    return jax.shard_map(
        body,
        mesh=mesh,
        in_specs=(rows, rows, P()) + tuple(s for s in weights for _ in range(3)),
        out_specs=(rows, rows) + tuple(s for s in weights for _ in range(5)),
        check_vma=False,
    )
```

```python
import functools

import jax
import jax.numpy as jnp
from jax import lax
from jax.experimental import pallas as pl
from jax.experimental.pallas import tpu as pltpu
from jax.sharding import PartitionSpec as P

HEAD = 64
PAIRS = 3

EPSILON = 1e-05

bf16, f32, i32 = jnp.bfloat16, jnp.float32, jnp.int32
CG, TAPS, GROUPS, HALO = 48, 128, 8, 64
ROWS, WIN, HALF = 1024, 1152, 384
CM, XM = 272, 304
NQ = 33
PJ = 134
EXTRA = 16
VLIM = 58 << 20


def iota(shape, dim):
    return lax.broadcasted_iota(i32, shape, dim)


def block_plan(starts, ends, first):
    w0 = first - HALO
    b = jnp.clip(starts - w0, 0, WIN)
    e = jnp.clip(ends - w0, 0, WIN)
    nblk = (e - b + 3) // 4
    n = starts.shape[0]
    before = jnp.arange(n)[None, :] < jnp.arange(n)[:, None]
    bs = jnp.sum(jnp.where(before, nblk[None, :], 0), axis=1).astype(i32)
    bs = bs + (jnp.clip(-w0, 0, WIN) + 3) // 4
    w = jnp.arange(WIN, dtype=i32)
    inside = (b[None, :] <= w[:, None]) & (w[:, None] < e[None, :])
    p = jnp.sum(jnp.where(inside, 4 * bs - b + w[:, None] + 1, 0), axis=1).astype(i32) - 1
    most = min(WIN, WIN // 4 + n)
    maxc = -((16 - most) // CM)
    lcap = CM * (maxc - 1) + XM
    m = jnp.arange(lcap, dtype=i32)
    hit = (bs[None, :] <= m[:, None]) & (m[:, None] < (bs + nblk)[None, :])
    bseg = jnp.sum(jnp.where(hit, jnp.arange(1, n + 1, dtype=i32)[None, :], 0), axis=1).astype(i32) - 1
    chunks = jnp.maximum((p[HALO + ROWS - 1] // 4 - 16) // CM + 1, 1)
    return (
        jnp.reshape(chunks, (1,)).astype(i32),
        jnp.broadcast_to(p[None, :], (8, WIN)),
        jnp.broadcast_to(p[:, None], (WIN, 128)),
        jnp.broadcast_to(bseg[:, None], (lcap, 128)),
    )


def select_pair(h, rows, base):
    lane = iota((rows, 256), 1)
    src = CG * (2 * h + (lane >> 7)) + (lane & 63) - base
    ok = ((lane & 63) < CG) & (iota((rows, 256), 0) == src)
    return jnp.where(ok, 1.0, 0.0).astype(bf16)


def build_blocks(s_ref, dup):
    y = [jnp.dot(s_ref[0, t], dup, preferred_element_type=f32).astype(bf16) for t in range(4)]
    low = iota((XM, 128), 1) < 64
    out = []
    for g in range(2):
        tiles = [v[:, 128 * g : 128 * g + 128] for v in y]
        out.append(
            jnp.concatenate(
                [jnp.where(low, tiles[0], tiles[1]), jnp.where(low, tiles[2], tiles[3])], axis=1
            )
        )
    return out


def build_taps(k_ref, sel, p_ref, base_tile):
    p_ref[...] = jnp.zeros_like(p_ref)
    step = 16
    for j0 in range(0, TAPS, step):
        part = k_ref[pl.ds(j0, step), :, pl.ds(pl.multiple_of(base_tile * 128, 128), 256)]
        d = jnp.dot(part.reshape(step * CG, 256), sel, preferred_element_type=f32)
        d = d.astype(bf16).reshape(step, CG, 256)
        for g in range(2):
            p_ref[g, pl.ds(j0 + 2, step), 0:CG, 0:64] = d[:, :, 128 * g : 128 * g + 64]
            p_ref[g, pl.ds(j0 + 3, step), 0:CG, 64:128] = d[:, :, 128 * g + 64 : 128 * g + 128]


def pair_lanes(h):
    base_tile = h >> 1
    return base_tile, pl.ds(pl.multiple_of(base_tile * 128, 128), 256)


def prepare_kernel(n_ref, *refs):
    @pl.when(pl.program_id(0) < n_ref[0])
    def _():
        prepare_chunk(pl.program_id(0), *refs)


def prepare_chunk(c, prow_ref, pcol_ref, bseg_ref, x_ref, s_ref, r_ref, mask_ref, tmask_ref, xb_ref, xt_ref):
    prow = prow_ref[0:1, :]
    for t in range(4):
        pos = 4 * (iota((XM, WIN), 0) + CM * c) + t
        s_ref[0, t] = jnp.where(pos == prow, 1.0, 0.0).astype(bf16)
    pcol = pcol_ref[HALO : HALO + ROWS, :]
    lane = iota((ROWS, 4 * CM), 1)
    phase = sum([(lane >= CM * t).astype(i32) for t in range(1, 4)])
    spot = 4 * (16 + CM * c) + 4 * lane - (4 * CM - 1) * phase
    wide = jnp.concatenate([pcol] * 9, axis=1)[:, : 4 * CM]
    r_ref[0] = jnp.where(wide == spot, 1.0, 0.0).astype(bf16)
    seg = bseg_ref[pl.ds(pl.multiple_of(CM * c, 16), XM), :]
    none = jnp.full((32, 128), -7, i32)
    own = jnp.concatenate([none, seg[16 : 16 + CM], none], axis=0)
    for q in range(NQ):
        same = seg[q : q + CM] == seg[16 : 16 + CM]
        mask_ref[0, q] = jnp.where(same, 1.0, 0.0).astype(bf16)
        same = seg == own[32 - q : 32 - q + XM]
        tmask_ref[0, q] = jnp.where(same, 1.0, 0.0).astype(bf16)
    for h in range(4):
        base = 128 * (h // 2)
        sel = select_pair(h, 256, base)
        dup = jnp.dot(x_ref[:, base : base + 256], sel, preferred_element_type=f32).astype(bf16)
        for g, block in enumerate(build_blocks(s_ref, dup)):
            xb_ref[0, 2 * h + g] = block
            xt_ref[0, 2 * h + g] = block.T


def fixed(shape):
    return pl.BlockSpec(shape, lambda *_: (0,) * len(shape))


def chunk_count(plan):
    return (plan[3].shape[0] - XM) // CM + 1


def call(kernel, name, grid, plan, in_specs, out_specs, out_shape, scratch, flops, args):
    return pl.pallas_call(
        kernel,
        grid_spec=pltpu.PrefetchScalarGridSpec(
            num_scalar_prefetch=1,
            grid=grid,
            in_specs=in_specs,
            out_specs=out_specs,
            scratch_shapes=scratch,
        ),
        out_shape=out_shape,
        compiler_params=pltpu.CompilerParams(vmem_limit_bytes=VLIM),
        cost_estimate=pl.CostEstimate(flops=flops, bytes_accessed=15_000_000, transcendentals=0),
        name=name,
    )(plan[0], *args)


def prepare(plan, window):
    chunks, prow, pcol, bseg = plan
    shapes = ((4, XM, WIN), (ROWS, 4 * CM), (NQ, CM, 128), (NQ, XM, 128), (8, XM, 256), (8, 256, XM))
    maxc = chunk_count(plan)
    return call(
        prepare_kernel,
        "conv_prepare",
        (maxc,),
        plan,
        [fixed(a.shape) for a in (prow, pcol, bseg, window)],
        tuple(
            pl.BlockSpec((1,) + s, lambda c, n, k=len(s): (jnp.minimum(c, n[0] - 1),) + (0,) * k)
            for s in shapes
        ),
        tuple(jax.ShapeDtypeStruct((maxc,) + s, bf16) for s in shapes),
        [],
        10_000_000_000,
        (prow, pcol, bseg, window),
    )


def conv_forward_kernel(n_ref, *refs):
    c, h = pl.program_id(0), pl.program_id(1)

    @pl.when(c < n_ref[0])
    def _():
        conv_chunk(False, c, h, *refs)


def conv_back_kernel(n_ref, d_ref, s_ref, *refs):
    c, h = pl.program_id(0), pl.program_id(1)

    @pl.when(c < n_ref[0])
    def _():
        conv_chunk(True, c, h, (d_ref, s_ref), *refs)


def conv_chunk(back, c, h, x_ref, mask_ref, r_ref, k_ref, out_ref, *rest):
    base_tile, lanes = pair_lanes(h)
    if back:
        s_ref, (xb_ref, o_ref) = x_ref[1], rest
        p_ref = k_ref
        sel = select_pair(h, 256, 128 * base_tile)
        dup = jnp.dot(x_ref[0][:, lanes], sel, preferred_element_type=f32).astype(bf16)
        for g, block in enumerate(build_blocks(s_ref, dup)):
            xb_ref[0, g] = block
    else:
        xb_ref = x_ref
        p_ref, o_ref = rest
        build_taps(k_ref, select_pair(h, 256, 128 * base_tile), p_ref, base_tile)

    @pl.when(h == 0)
    def _():
        o_ref[...] = jnp.zeros_like(o_ref)

    total = [jnp.zeros((CM, 256), f32) for _ in range(4)]
    for g in range(2):
        acc = jnp.zeros((CM, 256), f32)
        for q in range(NQ):
            m = mask_ref[0, q]
            xs = xb_ref[0, g, q : q + CM, :] * jnp.concatenate([m, m], axis=1)
            if back:
                a, b = 130 - 4 * q, 128 - 4 * q
            else:
                a, b = 4 * q + 2, 4 * q
            w = jnp.concatenate(
                [p_ref[g, a : a + 4].reshape(256, 128), p_ref[g, b : b + 4].reshape(256, 128)],
                axis=1,
            )
            dims = (((1,), (1 if back else 0,)), ((), ()))
            acc = acc + lax.dot_general(xs, w, dims, preferred_element_type=f32)
        acc = acc.astype(bf16)
        row = iota((256, 256), 0)
        target = CG * (2 * h + g) - 128 * base_tile + (row & 63)
        hit = ((row & 63) < CG) & (iota((256, 256), 1) == target)
        for t in range(4):
            fold = jnp.where(hit & ((row >> 6) == t), 1.0, 0.0).astype(bf16)
            total[t] = total[t] + jnp.dot(acc, fold, preferred_element_type=f32)
    for t in range(4):
        o_ref[CM * t : CM * t + CM, lanes] += total[t].astype(bf16)

    @pl.when(h == 3)
    def _():
        y = jnp.dot(r_ref[0], o_ref[...], preferred_element_type=f32)

        @pl.when(c == 0)
        def _():
            out_ref[...] = y

        @pl.when(c > 0)
        def _():
            out_ref[...] += y


def by_chunk(shape):
    return pl.BlockSpec(
        (1,) + shape, lambda c, h, n: (jnp.minimum(c, n[0] - 1),) + (0,) * len(shape)
    )


def by_pair(shape):
    return pl.BlockSpec(
        (2,) + shape, lambda c, h, n: (jnp.where(c < n[0], h, 3),) + (0,) * len(shape)
    )


def conv(plan, ready, taps):
    _, r, mask, _, xb, _ = ready
    x_spec = pl.BlockSpec(
        (1, 2, XM, 256),
        lambda c, h, n: (jnp.minimum(c, n[0] - 1), jnp.where(c < n[0], h, 3), 0, 0),
    )
    return call(
        conv_forward_kernel,
        "conv_forward",
        (chunk_count(plan), 4),
        plan,
        [x_spec, by_chunk((NQ, CM, 128)), by_chunk((ROWS, 4 * CM)), fixed((TAPS, CG, HALF))],
        (fixed((ROWS, HALF)), by_pair((PJ, 64, 128))),
        (
            jax.ShapeDtypeStruct((ROWS, HALF), f32),
            jax.ShapeDtypeStruct((8, PJ, 64, 128), bf16),
        ),
        [pltpu.VMEM((4 * CM, HALF), bf16)],
        25_000_000_000,
        (xb, mask, r, taps),
    )


def conv_back(plan, ready, window, spread_taps):
    s, r, mask, _, _, _ = ready
    return call(
        conv_back_kernel,
        "conv_back",
        (chunk_count(plan), 4),
        plan,
        [
            fixed((WIN, HALF)),
            by_chunk((4, XM, WIN)),
            by_chunk((NQ, CM, 128)),
            by_chunk((ROWS, 4 * CM)),
            by_pair((PJ, 64, 128)),
        ],
        fixed((ROWS, HALF)),
        jax.ShapeDtypeStruct((ROWS, HALF), f32),
        [pltpu.VMEM((1, 2, XM, 256), bf16), pltpu.VMEM((4 * CM, HALF), bf16)],
        25_000_000_000,
        (window, s, mask, r, spread_taps),
    )


def tap_grad_kernel(n_ref, xt_ref, s_ref, mask_ref, d_ref, small_ref, out_ref, dp_ref, acc_ref, sum_ref):
    h, c = pl.program_id(0), pl.program_id(1)
    base_tile, lanes = pair_lanes(h)

    @pl.when((h == 0) & (c == 0))
    def _():
        out_ref[...] = jnp.zeros_like(out_ref)
        out_ref[:, out_ref.shape[1] - EXTRA :, :] = small_ref[...]
        dp_ref[...] = jnp.zeros_like(dp_ref)

    @pl.when(c < n_ref[0])
    def _():
        sel = select_pair(h, 256, 128 * base_tile)
        ddup = jnp.dot(d_ref[:, lanes], sel, preferred_element_type=f32).astype(bf16)
        for g, block in enumerate(build_blocks(s_ref, ddup)):
            dp_ref[g, 32 : 32 + CM, :] = block[16 : 16 + CM]
        for g in range(2):
            carry = jnp.zeros((128, 128), f32)
            for q in range(NQ):
                m = mask_ref[0, q]
                ds = dp_ref[g, 32 - q : 32 - q + XM, :] * jnp.concatenate([m, m], axis=1)
                part = jnp.dot(xt_ref[0, g], ds, preferred_element_type=f32)
                left, right = part[:, 0:128], part[:, 128:256]
                acc_ref[g, 4 * q : 4 * q + 2] = (right[0:128] + carry).reshape(2, 64, 128)
                acc_ref[g, 4 * q + 2 : 4 * q + 4] = (left[0:128] + right[128:256]).reshape(2, 64, 128)
                carry = left[128:256]
            acc_ref[g, 4 * NQ : 4 * NQ + 2] = carry.reshape(2, 64, 128)

        @pl.when(c > 0)
        def _():
            acc_ref[...] += sum_ref[...]

        @pl.when(c < n_ref[0] - 1)
        def _():
            sum_ref[...] = acc_ref[...]

    @pl.when(c == pl.num_programs(1) - 1)
    def _():
        per = TAPS // out_ref.shape[0]
        low = iota((1, 1, 128), 2) < 64
        row = iota((128, 256), 0)
        src = CG * (2 * h + (row >> 6)) + (row & 63) - 128 * base_tile
        back = jnp.where(((row & 63) < CG) & (iota((128, 256), 1) == src), 1.0, 0.0).astype(bf16)
        step = 16
        for j0 in range(0, TAPS, step):
            now = [acc_ref[g, j0 + 2 : j0 + 2 + step, 0:CG, :] for g in range(2)]
            nxt = [acc_ref[g, j0 + 3 : j0 + 3 + step, 0:CG, :] for g in range(2)]
            here = jnp.where(low, now[0], nxt[1]).reshape(step * CG, 128)
            far = jnp.where(low, now[1], nxt[0]).reshape(step * CG, 128)
            both = (here + pltpu.roll(far, 64, 1)).astype(bf16)
            o = jnp.dot(both, back, preferred_element_type=f32).astype(bf16)
            o = o.reshape(step // per, per * CG, 256)
            out_ref[j0 // per : (j0 + step) // per, 0 : per * CG, lanes] += o


def tap_grad(plan, ready, d_own, small):
    s, _, _, tmask, _, xt = ready
    devices = small.shape[0]
    shape = (devices, TAPS // devices * CG + EXTRA, HALF)
    chunked = lambda sh: pl.BlockSpec(
        (1,) + sh, lambda h, c, n: (jnp.minimum(c, n[0] - 1),) + (0,) * len(sh)
    )
    x_spec = pl.BlockSpec((1, 2, 256, XM), lambda h, c, n: (jnp.minimum(c, n[0] - 1), h, 0, 0))
    return call(
        tap_grad_kernel,
        "tap_gradient",
        (4, chunk_count(plan)),
        plan,
        [
            x_spec,
            chunked((4, XM, WIN)),
            chunked((NQ, XM, 128)),
            fixed((WIN, HALF)),
            fixed(small.shape),
        ],
        fixed(shape),
        jax.ShapeDtypeStruct(shape, bf16),
        [
            pltpu.VMEM((2, 32 + CM + 32, 256), bf16),
            pltpu.VMEM((2, PJ, 64, 128), f32),
            pltpu.VMEM((2, PJ, 64, 128), f32),
        ],
        1_000_000_000,
        (xt, s, tmask, d_own, small),
    )
REACH = 1536
SPAN = ROWS + 2 * REACH
QT_AHEAD, QT_BACK, KT = 512, 256, 1664
NEAR = REACH - ROWS
NEG = -1e30


def segment_count(ends, positions):
    return jnp.sum((ends[None, :] <= positions[:, None]).astype(i32), axis=1).astype(i32)

def attention_plan(starts, ends, first, odd):
    w = first - REACH + jnp.arange(SPAN, dtype=i32)
    kseg = segment_count(ends, w)
    kseg = jnp.where(w < 0, -1, kseg)
    qseg = kseg[REACH : REACH + ROWS]
    n = jnp.arange(starts.shape[0], dtype=i32)

    def tiles_of(rows):
        edge = qseg.reshape(ROWS // rows, rows)
        head = jnp.sum(jnp.where(n[None] == edge[:, :1], starts[None], 0), axis=1) - (first - REACH)
        tail = jnp.sum(jnp.where(n[None] == edge[:, -1:], ends[None], 0), axis=1) - (first - REACH)
        lo = jnp.clip(head // 128, 0, SPAN // 128)
        hi = jnp.clip((tail + 127) // 128, 1, SPAN // 128)
        tiles = jnp.maximum((hi - lo + KT // 128 - 1) // (KT // 128), 1)
        lo = jnp.minimum(lo, SPAN // 128 - tiles * (KT // 128))
        return jnp.stack([lo, tiles, jnp.full_like(lo, odd)]).astype(i32)

    return (
        tiles_of(QT_AHEAD),
        tiles_of(QT_BACK),
        jnp.broadcast_to(qseg[None], (8, ROWS)),
        jnp.broadcast_to(kseg[:, None], (SPAN, 128)),
    )


def split_heads(a):
    low = iota(a.shape, 1) < 64
    zero = jnp.zeros((), a.dtype)
    return jnp.where(low, a, zero), jnp.where(low, zero, a)

def spots(range_ref):
    odd = range_ref[2, 0] == 1
    right, end = REACH + ROWS, SPAN - NEAR
    at = [
        jnp.where(odd, NEAR, right),
        jnp.where(odd, right, NEAR),
        jnp.where(odd, end, 0),
        jnp.where(odd, 0, end),
    ]
    return [pl.multiple_of(x, NEAR) for x in at]


def fill_span(range_ref, span_ref, own, others):
    span_ref[REACH : REACH + ROWS, :] = own[...]
    for at, piece in zip(spots(range_ref), others):
        span_ref[pl.ds(at, piece.shape[0]), :] = piece[...]


def flip_span(src_ref, dst_ref, lane):
    for at in range(0, SPAN, 512):
        dst_ref[:, at : at + 512] = src_ref[at : at + 512, lane : lane + 128].T


def same_segment(kseg_ref, qseg_ref, at):
    ks = kseg_ref[at, :]
    ks = jnp.concatenate([ks] * (qseg_ref.shape[1] // 128), axis=1)
    return ks == qseg_ref[0:1, :]


def forward_kernel(range_ref, qseg_ref, kseg_ref, q_ref, k0, k1, k2, k3, k4, o_ref, half_ref, lse_ref, span_ref, vt_ref):
    qi = pl.program_id(0)

    @pl.when(qi == 0)
    def _():
        fill_span(range_ref, span_ref, k0, (k1, k2, k3, k4))
        flip_span(span_ref, vt_ref, 128)

    qs = split_heads(q_ref[...])

    first, count = range_ref[0, qi], range_ref[1, qi]

    def tile(t, carry):
        at = pl.ds(pl.multiple_of((first + t * (KT // 128)) * 128, 128), KT)
        same = same_segment(kseg_ref, qseg_ref, at)
        k = span_ref[at, 0:128]
        out = []
        for e in range(2):
            m, l, acc = carry[e]
            s = lax.dot_general(k, qs[e], (((1,), (1,)), ((), ())), preferred_element_type=f32)
            s = jnp.where(same, s, NEG)
            new = jnp.maximum(m, jnp.max(s, axis=0, keepdims=True))
            p = jnp.exp(s - new)
            alpha = jnp.exp(m - new)
            l = l * alpha + jnp.sum(p, axis=0, keepdims=True)
            vt = vt_ref[64 * e : 64 * e + 64, at]
            acc = acc * alpha + jnp.dot(vt, p.astype(bf16), preferred_element_type=f32)
            out.append((new, l, acc))
        return tuple(out)

    start = (jnp.full((1, QT_AHEAD), NEG, f32), jnp.zeros((1, QT_AHEAD), f32), jnp.zeros((64, QT_AHEAD), f32))
    ends = lax.fori_loop(0, count, tile, (start, start))
    o = jnp.concatenate([acc / l for _, l, acc in ends], axis=0).T
    o_ref[...] = o
    half_ref[...] = o.astype(bf16)
    for e in range(2):
        lse_ref[e : e + 1, :] = ends[e][0] + jnp.log(ends[e][1])


def piece_specs(h, pieces):
    at = [h - (PAIRS - p.shape[1] // 256) if p.shape[1] > 256 else 0 for p in pieces]
    return [pl.BlockSpec((p.shape[0], 256), lambda i, c=c: (0, c)) for p, c in zip(pieces, at)]


def attend(plan, h, q, pieces):
    ranges, _, qseg, kseg = plan
    return pl.pallas_call(
        forward_kernel,
        grid=(ROWS // QT_AHEAD,),
        out_shape=(
            jax.ShapeDtypeStruct((ROWS, 128), f32),
            jax.ShapeDtypeStruct((ROWS, 128), bf16),
            jax.ShapeDtypeStruct((8, ROWS), f32),
        ),
        in_specs=[
            pl.BlockSpec(memory_space=pltpu.SMEM),
            pl.BlockSpec((8, QT_AHEAD), lambda i: (0, i)),
            pl.BlockSpec((SPAN, 128), lambda i: (0, 0)),
            pl.BlockSpec((QT_AHEAD, 128), lambda i: (i, h)),
        ]
        + piece_specs(h, pieces),
        out_specs=(
            pl.BlockSpec((QT_AHEAD, 128), lambda i: (i, 0)),
            pl.BlockSpec((QT_AHEAD, 128), lambda i: (i, 0)),
            pl.BlockSpec((8, QT_AHEAD), lambda i: (0, i)),
        ),
        scratch_shapes=[pltpu.VMEM((SPAN, 256), bf16), pltpu.VMEM((128, SPAN), bf16)],
        compiler_params=pltpu.CompilerParams(vmem_limit_bytes=VLIM),
        cost_estimate=pl.CostEstimate(flops=8_000_000_000, bytes_accessed=8_000_000, transcendentals=0),
        name="attention_forward",
    )(ranges, qseg, kseg, q, *pieces)


def backward_kernel(range_ref, qseg_ref, kseg_ref, q_ref, k0, k1, k2, k3, k4, do_ref, o_ref, lse_ref,
                    dq_ref, own_ref, f1, f2, f3, f4, span_ref, kt_ref, dkv_ref):
    qi = pl.program_id(0)
    last = ROWS // QT_BACK - 1

    @pl.when(qi == 0)
    def _():
        dkv_ref[...] = jnp.zeros_like(dkv_ref)
        fill_span(range_ref, span_ref, k0, (k1, k2, k3, k4))
        flip_span(span_ref, kt_ref, 0)

    qs = split_heads(q_ref[...])
    dos = split_heads(do_ref[...])
    qcat = jnp.concatenate(qs, axis=0)
    docat = jnp.concatenate(dos, axis=0)
    dm = (do_ref[...].astype(f32) * o_ref[...]).T
    delta = [jnp.sum(dm[64 * e : 64 * e + 64], axis=0, keepdims=True) for e in range(2)]

    first, count = range_ref[0, qi], range_ref[1, qi]

    def tile(t, carry):
        at = pl.ds(pl.multiple_of((first + t * (KT // 128)) * 128, 128), KT)
        same = same_segment(kseg_ref, qseg_ref, at)
        k = span_ref[at, 0:128]
        v = span_ref[at, 128:256]
        ps, dss, out = [], [], []
        for e in range(2):
            dims = (((1,), (1,)), ((), ()))
            s = lax.dot_general(k, qs[e], dims, preferred_element_type=f32)
            p = jnp.exp(jnp.where(same, s - lse_ref[e : e + 1, :], NEG))
            dp = lax.dot_general(v, dos[e], dims, preferred_element_type=f32)
            ds = (p * (dp - delta[e])).astype(bf16)
            kt = kt_ref[64 * e : 64 * e + 64, at]
            out.append(carry[e] + jnp.dot(kt, ds, preferred_element_type=f32))
            ps.append(p.astype(bf16))
            dss.append(ds)
        dkv_ref[at, 0:128] += jnp.dot(jnp.concatenate(dss, axis=1), qcat, preferred_element_type=f32)
        dkv_ref[at, 128:256] += jnp.dot(jnp.concatenate(ps, axis=1), docat, preferred_element_type=f32)
        return tuple(out)

    zero = jnp.zeros((64, QT_BACK), f32)
    dqt = lax.fori_loop(0, count, tile, (zero, zero))
    dq = jnp.concatenate(dqt, axis=0).T
    dq_ref[...] = dq.astype(bf16) * jnp.asarray(0.125, bf16)

    @pl.when(qi == last)
    def _():
        for at, far in zip(spots(range_ref), (f1, f2, f3, f4)):
            far[...] = dkv_ref[pl.ds(at, far.shape[0]), :].astype(bf16)
        own_ref[...] = dkv_ref[REACH : REACH + ROWS, :]


def attend_back(plan, h, q, pieces, d_att, mixed, lse):
    _, ranges, qseg, kseg = plan
    rowspec = pl.BlockSpec((QT_BACK, 128), lambda i: (i, 0))
    colspec = pl.BlockSpec((QT_BACK, 128), lambda i: (i, h))
    return pl.pallas_call(
        backward_kernel,
        grid=(ROWS // QT_BACK,),
        out_shape=(
            jax.ShapeDtypeStruct((ROWS, 128), bf16),
            jax.ShapeDtypeStruct((ROWS, 256), f32),
        )
        + tuple(jax.ShapeDtypeStruct((n, 256), bf16) for n in (ROWS, ROWS, NEAR, NEAR)),
        in_specs=[
            pl.BlockSpec(memory_space=pltpu.SMEM),
            pl.BlockSpec((8, QT_BACK), lambda i: (0, i)),
            pl.BlockSpec((SPAN, 128), lambda i: (0, 0)),
            colspec,
        ]
        + piece_specs(h, pieces)
        + [colspec, rowspec, pl.BlockSpec((8, QT_BACK), lambda i: (0, i))],
        out_specs=(
            rowspec,
            pl.BlockSpec((ROWS, 256), lambda i: (0, 0)),
        )
        + tuple(pl.BlockSpec((n, 256), lambda i: (0, 0)) for n in (ROWS, ROWS, NEAR, NEAR)),
        scratch_shapes=[
            pltpu.VMEM((SPAN, 256), bf16),
            pltpu.VMEM((128, SPAN), bf16),
            pltpu.VMEM((SPAN, 256), f32),
        ],
        compiler_params=pltpu.CompilerParams(vmem_limit_bytes=VLIM),
        cost_estimate=pl.CostEstimate(flops=8_000_000_000, bytes_accessed=12_000_000, transcendentals=0),
        name="attention_backward",
    )(ranges, qseg, kseg, q, *pieces, d_att, mixed, lse)


def exchange(part):
    return lax.ppermute(part, "heads", [(0, 1), (1, 0)])


def pair_sum(part):
    half = part.astype(bf16)
    return half.astype(f32) + exchange(half).astype(f32)


def side_by_side(own, other, index):
    return jnp.where(
        index == 0,
        jnp.concatenate([own, other], axis=1),
        jnp.concatenate([other, own], axis=1),
    )


def passed(block, distance):
    count = lax.axis_size("seq")
    route = [(i - distance, i) for i in range(count) if 0 <= i - distance < count]
    return lax.ppermute(block, "seq", route)


def across_cores(block):
    return lax.ppermute(block, "seq", [(i, i ^ 1) for i in range(lax.axis_size("seq"))])


def across_chips(block):
    count = lax.axis_size("seq")
    route = [(i, i + 1 if i % 2 else i - 1) for i in range(count)]
    return lax.ppermute(block, "seq", [(i, j) for i, j in route if 0 <= j < count])


def chip_along(block, step):
    count = lax.axis_size("seq")
    route = [(i, i - 2 * step if i % 2 else i + 2 * step) for i in range(count)]
    return lax.ppermute(block, "seq", [(i, j) for i, j in route if 0 <= j < count])


def layer_norm(values, gain, shift):
    centered = values - jnp.mean(values, axis=-1, keepdims=True)
    scale = lax.rsqrt(jnp.mean(centered * centered, axis=-1, keepdims=True) + EPSILON)
    return centered * scale * gain + shift


def gelu_exact(values):
    return jax.nn.gelu(values, approximate=False)


def nesterov(weight, grad, moment, average, rate):
    moment_new = 0.5 * moment + grad
    weight_new = weight - rate * (grad + 0.5 * moment_new)
    average_new = 0.5 * average + 0.5 * weight_new
    return (grad, weight_new, moment_new, average_new, weight_new.astype(bf16))


def dot(a, b, ca, cb):
    return lax.dot_general(a, b, (((ca,), (cb,)), ((), ())), preferred_element_type=f32)


def gathered(shard):
    return lax.all_gather(shard, "seq", axis=0, tiled=True)


def scattered(whole_sum):
    return lax.psum_scatter(whole_sum, "seq", scatter_dimension=0, tiled=True)


def body(
    frames,
    cotangent,
    lengths,
    kernel,
    kernel_moment,
    kernel_average,
    project,
    project_moment,
    project_average,
    combine,
    combine_moment,
    combine_average,
    expand,
    expand_moment,
    expand_average,
    shrink,
    shrink_moment,
    shrink_average,
    unitbias,
    unitbias_moment,
    unitbias_average,
    chanbias,
    chanbias_moment,
    chanbias_average,
    outbias,
    outbias_moment,
    outbias_average,
    normparams,
    normparams_moment,
    normparams_average,
):
    devices = lax.axis_size("seq")
    rows, width = frames.shape
    total = devices * rows
    first = lax.axis_index("seq") * rows
    index = lax.axis_index("heads")
    odd = lax.axis_index("seq") % 2
    local = project.shape[0]
    hidden_units = expand.shape[1]

    w_kernel = gathered(jnp.transpose(kernel, (2, 1, 0)).astype(bf16))
    small = jnp.concatenate(
        [unitbias, chanbias.reshape(-1), outbias.reshape(-1), normparams.reshape(-1)]
    ).astype(bf16)
    w_small = gathered(small[None])
    w_first = gathered(
        jnp.concatenate(
            [project[:, 0]]
            + [project[:, c, 128 * h : 128 * h + 128] for h in range(PAIRS) for c in (1, 2)]
            + [combine.T],
            axis=1,
        ).astype(bf16)
    )
    w_second = gathered(jnp.concatenate([expand, shrink.T], axis=1).astype(bf16))
    w_combine = w_first[:, 3 * HALF :]
    cuts = [unitbias.size, chanbias.size, outbias.size, normparams.size]
    parts, at = [], 0
    for size in cuts:
        parts.append(w_small[:, at : at + size].astype(f32))
        at += size
    b_unit = parts[0].reshape(-1)
    b_chan = jnp.transpose(parts[1].reshape(devices, 3, -1), (1, 0, 2)).reshape(3, -1)
    b_out = jnp.transpose(parts[2].reshape(devices, 2, -1), (1, 0, 2)).reshape(2, -1)
    norms = jnp.transpose(parts[3].reshape(devices, 3, 2, -1), (1, 2, 0, 3)).reshape(3, 2, -1)

    count = lengths.shape[0]
    order = jnp.arange(count, dtype=i32)
    ends = jnp.sum(jnp.where(order[None, :] <= order[:, None], lengths[None, :], 0), axis=1).astype(i32)
    starts = ends - lengths
    plan = block_plan(starts, ends, first)
    reach = attention_plan(starts, ends, first, odd)

    x_half = lax.dynamic_slice_in_dim(frames, index * HALF, HALF, 1).astype(bf16)
    window = jnp.concatenate(
        [passed(x_half[rows - HALO :], 1), x_half, passed(x_half[:HALO], -1)], axis=0
    )
    window, reach = lax.optimization_barrier((window, reach))
    ready = prepare(plan, window)
    conv_out, spread_taps = conv(plan, ready, w_kernel)
    pre = conv_out + b_chan[0]
    spread_part = gelu_exact(pre).astype(bf16)
    spread = side_by_side(spread_part, exchange(spread_part), index)
    h1, norm0_back = jax.vjp(layer_norm, frames + spread.astype(f32), norms[0, 0], norms[0, 1])
    h1_half = h1.astype(bf16)
    proj = dot(h1_half, w_first[:, : 3 * HALF], 1, 0)
    scale = HEAD ** (-0.5)
    queries = ((proj[:, :HALF] + b_chan[1]) * scale).astype(bf16)
    kv_bias = b_chan[2].reshape(PAIRS, 1, 128)
    kv_bias = jnp.concatenate([jnp.zeros_like(kv_bias), kv_bias], axis=1).reshape(-1)
    both = (proj[:, HALF:] + kv_bias).astype(bf16)
    near = NEAR
    w_combine_sent, queries = lax.optimization_barrier((w_combine, queries))
    w_combine_far = exchange(w_combine_sent)

    def fetched(lo, hi):
        block = both[:, lo:hi]
        head, tail = block[:near], block[rows - near :]
        beside = across_chips(block)
        shared = jnp.where(odd == 1, beside[:near], beside[rows - near :])
        return (
            across_cores(block),
            beside,
            chip_along(jnp.where(odd == 1, head, tail), 1),
            shared,
        )

    early = fetched(0, 256)
    early = early[:3] + (across_cores(early[3]),)
    both, early = lax.optimization_barrier((both, early))
    late = fetched(256, 256 * PAIRS)
    pieces = [(both,) + early]
    mixed, attended, attended_far, lse = [], [], [], []
    for h in range(PAIRS):
        q_part = queries
        if h == 1:
            q_part, w_combine_far = lax.optimization_barrier((queries, w_combine_far))
        if h >= 2:
            q_part, attended_far[h - 2] = lax.optimization_barrier((queries, attended_far[h - 2]))
        mixed_part, half, lse_part = attend(reach, h, q_part, pieces[h])
        mixed.append(mixed_part)
        lse.append(lse_part)
        attended.append(half)
        attended_far.append(exchange(half))
        if h == 0:
            shared, _ = lax.optimization_barrier((late[3], half))
            pieces += [(both,) + late[:3] + (across_cores(shared),)] * (PAIRS - 1)
    attended = jnp.concatenate(attended, axis=1)
    attended_all = side_by_side(attended, jnp.concatenate(attended_far, axis=1), index)
    w_combine_all = side_by_side(w_combine, w_combine_far, index)
    w_expand = w_second[:, :hidden_units]
    w_shrink = w_second[:, hidden_units:]
    cuts_of = [slice(0, rows * 3 // 8), slice(rows * 3 // 8, rows)]
    first_half, second_half = [], []
    for cut in cuts_of:
        branch = dot(attended_all[cut], w_combine_all, 1, 1)
        h2, norm1_back = jax.vjp(layer_norm, h1[cut] + branch + b_out[0], norms[1, 0], norms[1, 1])
        h2_half = h2.astype(bf16)
        inner = dot(h2_half, w_expand, 1, 0) + b_unit
        hidden, gelu_inner_back = jax.vjp(gelu_exact, inner)
        hidden_half = hidden.astype(bf16)
        sent = dot(hidden_half, w_shrink, 1, 1).astype(bf16)
        first_half.append((h2, norm1_back, h2_half, gelu_inner_back, hidden_half, sent, exchange(sent)))
    sent_back = None
    for cut, (h2, norm1_back, h2_half, gelu_inner_back, hidden_half, sent, came) in zip(
        cuts_of, first_half
    ):
        if sent_back is not None:
            came, _ = lax.optimization_barrier((came, sent_back))
        outer = sent.astype(f32) + came.astype(f32)
        out_part, norm2_back = jax.vjp(layer_norm, h2 + outer + b_out[1], norms[2, 0], norms[2, 1])
        dx3, gain2_grad, shift2_grad = norm2_back(cotangent[cut])
        d_out = dx3.astype(bf16)
        d_hidden = dot(d_out, w_shrink, 1, 0)
        d_inner = gelu_inner_back(d_hidden)[0]
        d_inner_half = d_inner.astype(bf16)
        sent_back = dot(d_inner_half, w_expand, 1, 1).astype(bf16)
        sums = [gain2_grad, shift2_grad, jnp.sum(dx3, axis=0), jnp.sum(d_inner, axis=0)]
        second_half.append(
            [out_part, (sent_back, exchange(sent_back)), norm1_back, h2_half, d_inner_half, d_out, hidden_half, dx3, sums]
        )
    layer_out = jnp.concatenate([part[0] for part in second_half], axis=0)
    gain2_grad, shift2_grad, outer_bias_grad, unit_grad = map(sum, zip(*[p[-1] for p in second_half]))
    second_part = jnp.concatenate(
        [
            sum(dot(p[a], p[b], 0, 0) for p in second_half).astype(bf16)
            for a, b in ((3, 4), (5, 6))
        ],
        axis=1,
    )
    dx2_parts, gain1_parts, shift1_parts = zip(
        *[p[2](p[7] + (p[1][0].astype(f32) + p[1][1].astype(f32))) for p in second_half]
    )
    gain1_grad, shift1_grad = sum(gain1_parts), sum(shift1_parts)
    dx2 = jnp.concatenate(dx2_parts, axis=0)
    branch_bias_grad = jnp.sum(dx2, axis=0)
    d_branch = dx2.astype(bf16)
    d_att = dot(d_branch, w_combine, 1, 0).astype(bf16)
    d_att, second_part = lax.optimization_barrier((d_att, second_part))
    second_sum = scattered(second_part).astype(f32)
    combine_part = dot(d_branch, attended, 0, 0).astype(bf16)
    dq_parts, kv_parts = [], []
    arrived = {}
    for h in range(PAIRS):
        d_part = d_att
        if h >= 2:
            two = arrived[h - 2][:2]
            d_part, two, combine_part = lax.optimization_barrier((d_att, two, combine_part))
            arrived[h - 2] = two + arrived[h - 2][2:]
        dq_part, own, core, chip, far, beyond = attend_back(
            reach, h, queries, pieces[h], d_part, mixed[h], lse[h]
        )
        arrived[h] = (
            across_cores(core),
            across_chips(chip),
            chip_along(far, -1),
            chip_along(beyond, 1),
            own,
        )
        dq_parts.append(dq_part)
    for h in range(PAIRS):
        core, chip, far, beyond, own = [a.astype(f32) for a in arrived[h]]
        ends_of = jnp.concatenate(
            [jnp.where(odd == 1, far, beyond), jnp.where(odd == 1, beyond, far)], axis=0
        )
        kv_parts.append((own + core + chip + ends_of).astype(bf16))
    dq_half = jnp.concatenate(dq_parts, axis=1)
    d_both_half = jnp.concatenate(kv_parts, axis=1)
    stacked = jnp.concatenate([dq_half, d_both_half], axis=1)
    query_bias_grad = jnp.sum(dq_half.astype(f32), axis=0)
    value_bias_grad = jnp.sum(
        d_both_half.astype(f32), axis=0
    ).reshape(PAIRS, 2, 128)[:, 1].reshape(-1)
    dh1_half = dot(stacked, w_first[:, : 3 * HALF], 1, 1).astype(bf16)
    dh1_half, second_sum = lax.optimization_barrier((dh1_half, second_sum))
    dh1 = dx2 + (dh1_half.astype(f32) + exchange(dh1_half).astype(f32))
    first_part = (
        jnp.concatenate(
            [dot(h1_half, stacked, 0, 0).astype(bf16), combine_part],
            axis=1,
        )
    )
    first_part, second_sum = lax.optimization_barrier((first_part, second_sum))
    first_sum = scattered(first_part).astype(f32)
    dx1, gain0_grad, shift0_grad = norm0_back(dh1)
    d_spread = lax.dynamic_slice_in_dim(dx1, index * HALF, HALF, 1)
    d_conv = jax.vjp(gelu_exact, pre)[1](d_spread)[0]
    conv_bias_grad = jnp.sum(d_conv, axis=0)
    d_conv_half = d_conv.astype(bf16)
    spread_out = lambda grad, lead: jnp.transpose(
        grad.reshape(lead, devices, -1), (1, 0, 2)
    ).reshape(devices, -1)
    small_part = jnp.concatenate(
            [
                unit_grad.reshape(devices, -1),
                spread_out(jnp.stack([conv_bias_grad, query_bias_grad, value_bias_grad]), 3),
                spread_out(jnp.stack([branch_bias_grad, outer_bias_grad]), 2),
                spread_out(
                    jnp.stack(
                        [gain0_grad, shift0_grad, gain1_grad, shift1_grad, gain2_grad, shift2_grad]
                    ),
                    6,
                ),
            ],
            axis=1,
        )
    small_part = jnp.pad(small_part, ((0, 0), (0, EXTRA * HALF - small_part.shape[1])))
    small_part = small_part.astype(bf16).reshape(devices, EXTRA, HALF)
    d_own = jnp.pad(d_conv_half, ((HALO, HALO), (0, 0)))
    tap_raw = tap_grad(plan, ready, d_own, small_part)
    tap_part, first_sum = lax.optimization_barrier((tap_raw, first_sum))
    tap_sum = scattered(tap_part)[0].astype(f32)
    kernel_sum = tap_sum[:-EXTRA].reshape(TAPS // devices, CG, HALF)
    small_sum = tap_sum[-EXTRA:].reshape(-1)
    d_rim = jnp.concatenate([d_conv_half[:HALO], d_conv_half[rows - HALO :]], axis=0)
    d_rim, _ = lax.optimization_barrier((d_rim, tap_raw))
    d_window = jnp.concatenate(
        [passed(d_rim[HALO:], 1), d_conv_half, passed(d_rim[:HALO], -1)], axis=0
    )
    d_input = conv_back(plan, ready, d_window, spread_taps).astype(bf16)
    frames_grad = dx1 + side_by_side(d_input, exchange(d_input), index).astype(f32)

    pieces, at = [], 0
    for size in cuts:
        pieces.append(small_sum[at : at + size])
        at += size
    unit_sum = pieces[0]
    chan_sum = pieces[1].reshape(chanbias.shape)
    out_sum = pieces[2].reshape(outbias.shape)
    norm_sum = pieces[3].reshape(normparams.shape)
    kv_sum = first_sum[:, HALF : 3 * HALF].reshape(local, PAIRS, 2, 128)
    project_sum = jnp.stack(
        [first_sum[:, :HALF]] + [kv_sum[:, :, c].reshape(local, HALF) for c in range(2)], axis=1
    )

    root = total**0.5
    small_rate = 0.1 / root
    out = [layer_out, frames_grad]
    for weight, grad, moment, average, rate in (
        (kernel, jnp.transpose(kernel_sum, (2, 1, 0)), kernel_moment, kernel_average, (CG * TAPS) ** (-0.5) / root),
        (project, project_sum, project_moment, project_average, width ** (-0.5) / root),
        (combine, first_sum[:, 3 * HALF :].T, combine_moment, combine_average, (width // 16) ** (-0.5) / root),
        (expand, second_sum[:, :hidden_units], expand_moment, expand_average, width ** (-0.5) / root),
        (shrink, second_sum[:, hidden_units:].T, shrink_moment, shrink_average, (2 * hidden_units) ** (-0.5) / root),
        (unitbias, unit_sum, unitbias_moment, unitbias_average, 0.5 / root),
        (chanbias, chan_sum, chanbias_moment, chanbias_average, small_rate),
        (outbias, out_sum, outbias_moment, outbias_average, small_rate),
        (normparams, norm_sum, normparams_moment, normparams_average, small_rate),
    ):
        out.extend(nesterov(weight, grad, moment, average, rate))
    return tuple(out)


def solution(mesh):
    kernel_spec = P("heads", None, "seq")
    project_spec = P("seq", None, "heads")
    tall = P("heads", "seq")
    wide = P("seq", "heads")
    unit = P(("heads", "seq"))
    chan = P(None, ("heads", "seq"))
    outb = P(None, "seq")
    norm = P(None, None, "seq")
    weights = (kernel_spec, project_spec, tall, wide, tall, unit, chan, outb, norm)
    rows = P("seq", None)
    return jax.shard_map(
        body,
        mesh=mesh,
        in_specs=(rows, rows, P()) + tuple(s for s in weights for _ in range(3)),
        out_specs=(rows, rows) + tuple(s for s in weights for _ in range(5)),
        check_vma=False,
    )
```
